128 devices in a mesh: row: 32 (over y, z, core), col: 4 (over x).
Axes of the slice: x: 4, y: 4, z: 4, core: 2. Of those that a mesh axis runs over, the one named last changes fastest.
Arguments:
- amplitudes: bfloat16 [4, 1280, 1280], P(None, ('row', 'col')), may hold values from -0.75 to 0.75
- integrals: bfloat16 [96, 1280, 1280], P('row', 'col'), may hold values from -0.15625 to 0.15625
- occupied_integrals: bfloat16 [96, 160, 1280], P('row'), may hold values from -1 to 1
- pair_orbitals: int32 [4, 2], replicated, may hold values from 0 to 159
- amplitude_tiles: int32 [4, 20, 20], replicated, may hold values 0 or 1
- integral_tiles: int32 [20, 20], replicated, may hold values 0 or 1
Outputs:
- residual: float32 [4, 1280, 1280], P(None, 'col', 'row')
The draws below stay inside these ranges and needn't reach their ends.
All inputs are finite; a program needn't handle non-finite values.
Results may differ from the reference program's by a relative error of at most 0.005.
Values may be sent and summed in bfloat16 or wider, within the bound.
A program may use at most 128 MiB of HBM per device.

```python
import jax
import jax.numpy as jnp
from jax import lax

O = 160
TILE = 64
VT = 20
P_SIZE = 4
V = 1280
NAUX = 96


def place_ends(array, key, least, largest):
    shape = array.shape
    place = [jax.random.randint(jax.random.fold_in(key, axis), (), 0, shape[axis]) for axis in range(len(shape))]
    array = array.at[tuple(place)].set(least)
    longest = shape.index(max(shape))
    place[longest] = (place[longest] + 1) % shape[longest]
    return array.at[tuple(place)].set(largest)


def block_levels(stream_key, shape, shards, low, top_value):
    gain, own = 1.0, jax.random.fold_in(stream_key, 6)
    for axis_at, parts in shards:
        heights = jnp.exp(jax.random.uniform(jax.random.fold_in(own, axis_at), (parts,), jnp.float32, low / len(shards), top_value / len(shards)))
        gain = gain * jnp.repeat(heights, shape[axis_at] // parts).reshape([-1 if axis == axis_at else 1 for axis in range(len(shape))])
    return gain


def gaussian(own_key, dims, width, most, pieces=(), kind=jnp.bfloat16):
    values = width * jax.random.normal(own_key, dims, jnp.float32)
    if pieces:
        values = values * block_levels(own_key, dims, pieces, -0.22, 0.18)
    return jnp.clip(values, -most, most).astype(kind)


def setup_inputs(seed: int = 0) -> dict:
    seeds = jax.random.split(jax.random.key(seed), 7)
    return {
        "amplitudes": gaussian(seeds[0], (P_SIZE, V, V), 0.125, 0.75, ((1, 128),)),
        "integrals": gaussian(seeds[1], (NAUX, V, V), V ** -0.5, 0.15625, ((0, 32), (1, 4))),
        "occupied_integrals": gaussian(seeds[2], (NAUX, O, V), 0.17, 1.0, ((0, 32),)),
        "pair_orbitals": place_ends(jax.random.randint(seeds[3], (P_SIZE, 2), 0, O), jax.random.fold_in(seeds[3], 1), 0, O - 1).astype(jnp.int32),
        "amplitude_tiles": place_ends((jax.random.randint(seeds[4], (P_SIZE, VT, VT), 0, 2) < 1).astype(jnp.int32), jax.random.fold_in(seeds[4], 1), 0, 1),
        "integral_tiles": place_ends((jax.random.randint(seeds[5], (VT, VT), 0, 4) < 3).astype(jnp.int32), jax.random.fold_in(seeds[5], 1), 0, 1),
    }


def expand_tiles(tiles, tile_size):
    return jnp.repeat(jnp.repeat(tiles, tile_size, axis=-2), tile_size, axis=-1)


def reference(amplitudes, integrals, occupied_integrals, pair_orbitals, amplitude_tiles, integral_tiles):
    masked_amp = amplitudes * expand_tiles(amplitude_tiles, TILE).astype(jnp.bfloat16)
    masked_int = integrals * expand_tiles(integral_tiles, TILE).astype(jnp.bfloat16)[None]
    amp_wide = masked_amp.astype(jnp.float32)

    def one_aux(total, factor):
        factor_wide = factor.astype(jnp.float32)
        inter = jnp.einsum('ac,pcd->pad', factor_wide, amp_wide).astype(jnp.bfloat16)
        term = jnp.einsum('pad,bd->pab', inter.astype(jnp.float32), factor_wide)
        return total + term, None

    ladder, _ = lax.scan(one_aux, jnp.zeros((P_SIZE, V, V), jnp.float32), masked_int)
    orbital_ids = jnp.arange(O, dtype=jnp.int32)
    pick_first = (pair_orbitals[:, 0][:, None] == orbital_ids[None, :]).astype(jnp.float32)
    pick_second = (pair_orbitals[:, 1][:, None] == orbital_ids[None, :]).astype(jnp.float32)
    occ_wide = occupied_integrals.astype(jnp.float32)
    first_rows = jnp.einsum('po,qov->qpv', pick_first, occ_wide)
    second_rows = jnp.einsum('po,qov->qpv', pick_second, occ_wide)
    carried = jnp.einsum('qpc,pcd->qpd', second_rows, amp_wide)
    cycle = jnp.einsum('qpa,qpb->pab', first_rows, carried)
    return ladder + cycle
```

```python
import jax
import jax.numpy as jnp
from jax import lax
from jax.experimental import pallas as pl
from jax.experimental.pallas import tpu as pltpu
from jax.sharding import PartitionSpec as P

MESH = pl.DeviceIdType.MESH
TILE = 64
V = 1280
BLK = 320
PIECE = 80
HALF = 640
NT = 256
NS = 2
SUB = BLK // NS
F32 = jnp.float32
BF16 = jnp.bfloat16


def kernel(
    b_own, t_own, l_own, out,
    bbuf, tst, tbuf, lbuf, ut, li2, xbuf, acc,
    s1, r1, s2, r2, fin, gbuf, hbuf,
    t1_ss, t1_rs, tg_ss, tg_rs, l_ss, l_rs, own_ls,
    bo_ss, bf_ss, b_rs, sh_ss, sh_rs, p1_ss, p1_rs, p2_ss, p2_rs, g_ss, g_rs,
):
    x = lax.axis_index("col")
    row = lax.axis_index("row")
    k = lax.rem(row, 2)
    yz = row // 2
    y = yz // 4
    z = lax.rem(yz, 4)
    s = 1 - 2 * lax.rem(x, 2)
    xp = lax.rem(x + s + 4, 4)
    xm = lax.rem(x - s + 4, 4)
    xo = lax.rem(x + 2, 4)
    sg = 1 - 2 * k
    me8 = k * 4 + x
    pair = 2 * lax.rem(x, 2) + k
    sib = (yz * 2 + 1 - k, x)
    owner2 = lax.rem((x + 1) // 2 + 1, 2)
    is_owner = k == owner2
    main_j = x // 2

    def dev(yy, zz, kk, xx):
        return ((yy * 4 + zz) * 2 + kk, xx)

    def ring(v):
        return lax.rem(v + 8, 4)

    def peer8(d):
        idx = lax.rem(me8 + d, 8)
        return idx, idx // 4, lax.rem(idx, 4)

    def rcopy(src, dst, ss, rs, to):
        return pltpu.make_async_remote_copy(
            src_ref=src, dst_ref=dst, send_sem=ss, recv_sem=rs, device_id=to, device_id_type=MESH
        )

    pending = []

    def send(src, dst, ss, rs, to):
        c = rcopy(src, dst, ss, rs, to)
        c.start()
        pending.append(c)
        return c

    barrier = pltpu.get_barrier_semaphore()
    for d in range(1, 8):
        _, kk, xx = peer8(d)
        pl.semaphore_signal(barrier, inc=1, device_id=dev(y, z, kk, xx), device_id_type=MESH)
    for step in (1, -1):
        pl.semaphore_signal(barrier, inc=1, device_id=dev(ring(y + step), z, k, x), device_id_type=MESH)
        pl.semaphore_signal(barrier, inc=1, device_id=dev(y, ring(z + step), k, x), device_id_type=MESH)
    pl.semaphore_wait(barrier, 11)

    for d in range(1, 8):
        idx, kk, xx = peer8(d)
        send(t_own.at[2 * lax.rem(xx, 2) + kk], tst.at[me8], t1_ss.at[d], t1_rs.at[d], dev(y, z, kk, xx))
    send(l_own.at[2 * lax.rem(x, 2) + 1 - k], lbuf.at[1], l_ss, l_rs, sib)

    dest2 = jnp.where(is_owner, xm, xp)
    which2 = jnp.where(is_owner, 0, 2)

    def rows(i):
        return pl.ds(i * SUB, SUB)

    for i in range(NS):
        send(b_own.at[1 - main_j, rows(i)], bbuf.at[k, x, rows(i)], bo_ss.at[1, i], b_rs.at[0, 2, i],
             (row, xm))
        send(b_own.at[main_j, rows(i)], bbuf.at[k, x, rows(i)], bo_ss.at[0, i], b_rs.at[0, 0, i],
             (row, xp))
    for i in range(NS):
        send(b_own.at[2, rows(i)], bbuf.at[2, x, rows(i)], bo_ss.at[2, i], b_rs.at[1, which2, i],
             (row, dest2))

    def share(kind, pos, i, src=None):
        slot, blk = (k, None) if kind == 0 else (2, None)
        blk = (x, pos_main(pos) if kind == 0 else pos_second(pos))[pos > 0]
        dst = bbuf.at[slot, blk, rows(i)]
        return rcopy(dst if src is None else src, dst, sh_ss.at[kind, pos, i], sh_rs.at[kind, pos, i], sib)

    def pos_main(pos):
        return (x, xm, xp, xo)[pos]

    def pos_second(pos):
        return (x, xp, xm, xo)[pos]

    which_of = (None, 2, 0, 1)

    for i in range(NS):
        c = share(0, 0, i, b_own.at[main_j, rows(i)])
        c.start()
        pending.append(c)

    @pl.when(is_owner)
    def _():
        for i in range(NS):
            share(1, 0, i, b_own.at[2, rows(i)]).start()

    own_main = pltpu.make_async_copy(b_own.at[main_j], bbuf.at[k, x], own_ls.at[0])
    own_main.start()
    own_second = pltpu.make_async_copy(b_own.at[2], bbuf.at[2, x], own_ls.at[1])

    @pl.when(is_owner)
    def _():
        own_second.start()

    tst[me8] = t_own[pair]
    lbuf[0] = l_own[pair]
    for d in range(1, 8):
        src8 = lax.rem(me8 + 8 - d, 8)
        rcopy(t_own.at[0], tst.at[src8], t1_ss.at[d], t1_rs.at[d], sib).wait_recv()
    ri = lax.broadcasted_iota(jnp.int32, (PIECE, 128), 0)
    ci = lax.broadcasted_iota(jnp.int32, (PIECE, 128), 1)
    within = jnp.bitwise_and(ci, 15)
    pick = jnp.where((within < 10) & (ri == jnp.right_shift(ci, 4) * 10 + within), 1.0, 0.0).astype(BF16)
    for n in range(V // NT):
        cols = pl.ds(n * NT, NT)
        piece = jnp.dot(pick, tst[:, :, cols].reshape(128, NT), preferred_element_type=F32)
        tbuf[y, z, :, cols] = piece.astype(BF16)

    col_a, col_b = pl.ds(0, HALF), pl.ds(HALF, HALF)

    def t_slice(half, phase, i):
        if half == 0:
            return tbuf.at[i, z, :, col_a] if phase == 0 else tbuf.at[:, i, :, col_a]
        return tbuf.at[y, i, :, col_b] if phase == 0 else tbuf.at[i, :, :, col_b]

    def along(half, phase, off):
        if (half == 0) == (phase == 0):
            return ring(y + off), dev(ring(y + off), z, k, x)
        return ring(z + off), dev(y, ring(z + off), k, x)

    def t_start(half, phase):
        mine = t_slice(half, phase, along(half, phase, 0)[0])
        for n, off in ((0, sg), (1, -sg)):
            send(mine, mine, tg_ss.at[half, phase, n], tg_rs.at[half, phase, n], along(half, phase, off)[1])

    def t_forward(half, phase):
        got = t_slice(half, phase, along(half, phase, -sg)[0])
        rcopy(got, got, tg_ss.at[half, phase, 0], tg_rs.at[half, phase, 0], sib).wait_recv()
        send(got, got, tg_ss.at[half, phase, 2], tg_rs.at[half, phase, 2], along(half, phase, sg)[1])

    def t_finish(half, phase):
        for n, off in ((1, sg), (2, 2)):
            got = t_slice(half, phase, along(half, phase, off)[0])
            rcopy(got, got, tg_ss.at[half, phase, n], tg_rs.at[half, phase, n], sib).wait_recv()

    for phase in range(2):
        for half in range(2):
            if phase == 1:
                t_finish(half, 0)
            t_start(half, phase)
        for half in range(2):
            t_forward(half, phase)

    def land(kind, pos):
        slot = k if kind == 0 else 2
        blk = pos_main(pos) if kind == 0 else pos_second(pos)
        for i in range(NS):
            ref = bbuf.at[slot, blk, rows(i)]
            rcopy(ref, ref, bo_ss.at[0, i], b_rs.at[kind, which_of[pos], i], sib).wait_recv()
            if pos == 1:
                to = xp if kind == 0 else xm
                rcopy(ref, ref, bf_ss.at[kind, i], b_rs.at[kind, 1, i], (row, to)).start()
            share(kind, pos, i).start()

    def from_sib(kind, pos):
        slot = 1 - k if kind == 0 else 2
        blk = pos_main(pos) if kind == 0 else pos_second(pos)
        for i in range(NS):
            ref = bbuf.at[slot, blk, rows(i)]
            rcopy(ref, ref, sh_ss.at[kind, pos, i], sh_rs.at[kind, pos, i], sib).wait_recv()

    def get_second(pos):
        @pl.when(is_owner)
        def _():
            if pos == 0:
                own_second.wait()
            else:
                land(1, pos)

        @pl.when(jnp.logical_not(is_owner))
        def _():
            from_sib(1, pos)

    def first_product(slot, blk):
        @pl.loop(0, V // NT)
        def _(n):
            cols = pl.ds(pl.multiple_of(n * NT, NT), NT)
            rhs = tbuf[:, :, :, cols].reshape(V, NT)
            val = jnp.dot(bbuf[slot, blk], rhs, preferred_element_type=F32)
            xbuf[slot, pl.ds(pl.multiple_of(blk * BLK, 64), BLK), cols] = val.astype(BF16)

    land(0, 1)
    own_main.wait()
    t_finish(0, 1)
    t_finish(1, 1)
    land(0, 2)
    first_product(k, x)

    rcopy(l_own.at[0], lbuf.at[1], l_ss, l_rs, sib).wait_recv()
    pick_l = jnp.where(k == x // 2, 0, 1)
    for n in range(V // NT):
        cols = pl.ds(n * NT, NT)
        u = jnp.dot(lbuf[pick_l, 0:16], tbuf[:, :, :, cols].reshape(V, NT), preferred_element_type=F32)
        hi = u.astype(BF16).astype(F32)
        both = jnp.concatenate([hi, u - hi], axis=0)
        ut[cols, :] = both.T.astype(BF16)
    li2[0:16] = lbuf[pick_l, 16:32]
    li2[16:32] = lbuf[pick_l, 16:32]

    from_sib(0, 0)
    first_product(1 - k, x)
    get_second(0)
    first_product(2, x)
    get_second(1)
    first_product(k, xm)
    first_product(k, xp)
    from_sib(0, 1)
    first_product(1 - k, xm)
    from_sib(0, 2)
    first_product(1 - k, xp)
    land(0, 3)
    first_product(k, xo)
    get_second(2)
    from_sib(0, 3)
    first_product(1 - k, xo)

    nt = (((1,), (1,)), ((), ()))

    @pl.loop(0, 4)
    def _(m):
        @pl.loop(0, V // NT)
        def _(n):
            cols = pl.ds(pl.multiple_of(n * NT, NT), NT)
            val = jnp.dot(ut[pl.ds(pl.multiple_of(m * BLK, 64), BLK), :], li2[:, cols],
                          preferred_element_type=F32)
            for sl in range(2):
                val += lax.dot_general(bbuf[sl, m], xbuf[sl, cols, :], nt, preferred_element_type=F32)
            acc[m, :, :, cols] = val.reshape(4, PIECE, NT)

    first_product(2, xp)
    first_product(2, xm)
    get_second(3)
    first_product(2, xo)

    def last_product(lo, hi):
        @pl.loop(lo, hi)
        def _(n):
            cols = pl.ds(pl.multiple_of(n * NT, NT), NT)

            @pl.loop(0, 4)
            def _(m):
                val = lax.dot_general(bbuf[2, m], xbuf[2, cols, :], nt, preferred_element_type=F32)
                acc[m, :, :, cols] += val.reshape(4, PIECE, NT)

    def ralong(half, phase, off):
        return along(1 - half, phase, off)

    def part(half, t, i):
        cols = (col_a, col_b)[half]
        return acc[t, i, :, cols] if half == 0 else acc[i, t, :, cols]

    def put(half, t, i, val):
        cols = (col_a, col_b)[half]
        if half == 0:
            acc[t, i, :, cols] = val
        else:
            acc[i, t, :, cols] = val

    def p1_start(half):
        far = ralong(half, 0, 2)[0]
        back, back_dev = ralong(half, 0, -sg)
        fwd_dev = ralong(half, 0, sg)[1]
        for t in range(4):
            s1[half, 0, t] = part(half, t, far).astype(BF16)
        send(s1.at[half, 0], r1.at[half, 0], p1_ss.at[half, 0], p1_rs.at[half, 0], fwd_dev)
        for t in range(4):
            s1[half, 1, t] = part(half, t, back).astype(BF16)
        send(s1.at[half, 1], r1.at[half, 1], p1_ss.at[half, 1], p1_rs.at[half, 1], back_dev)

    def p1_wait(half, n):
        rcopy(s1.at[half, n], r1.at[half, n], p1_ss.at[half, n], p1_rs.at[half, n], sib).wait_recv()

    def p1_middle(half):
        nxt, nxt_dev = ralong(half, 0, sg)
        p1_wait(half, 0)
        for t in range(4):
            s1[half, 2, t] = (part(half, t, nxt) + r1[half, 0, t].astype(F32)).astype(BF16)
        send(s1.at[half, 2], r1.at[half, 2], p1_ss.at[half, 2], p1_rs.at[half, 2], nxt_dev)

    def p1_end(half):
        here = ralong(half, 0, 0)[0]
        p1_wait(half, 1)
        p1_wait(half, 2)

        def total(t):
            return part(half, t, here) + r1[half, 1, t].astype(F32) + r1[half, 2, t].astype(F32)

        far = ralong(half, 1, 2)[0]
        back, back_dev = ralong(half, 1, -sg)
        nxt, nxt_dev = ralong(half, 1, sg)
        s2[half, 0] = total(far).astype(BF16)
        send(s2.at[half, 0], r2.at[half, 0], p2_ss.at[half, 0], p2_rs.at[half, 0], nxt_dev)
        s2[half, 1] = total(back).astype(BF16)
        send(s2.at[half, 1], r2.at[half, 1], p2_ss.at[half, 1], p2_rs.at[half, 1], back_dev)
        put(half, nxt, here, total(nxt))
        mid = ralong(half, 1, 0)[0]
        put(half, mid, here, total(mid))

    def p2_wait(half, n):
        rcopy(s2.at[half, n], r2.at[half, n], p2_ss.at[half, n], p2_rs.at[half, n], sib).wait_recv()

    def p2_middle(half):
        nxt, nxt_dev = ralong(half, 1, sg)
        here = ralong(half, 0, 0)[0]
        p2_wait(half, 0)
        s2[half, 2] = (part(half, nxt, here) + r2[half, 0].astype(F32)).astype(BF16)
        send(s2.at[half, 2], r2.at[half, 2], p2_ss.at[half, 2], p2_rs.at[half, 2], nxt_dev)

    def p2_end(half):
        mid = ralong(half, 1, 0)[0]
        here = ralong(half, 0, 0)[0]
        p2_wait(half, 1)
        p2_wait(half, 2)
        fin[:, (col_a, col_b)[half]] = (
            part(half, mid, here) + r2[half, 1].astype(F32) + r2[half, 2].astype(F32)
        )

    last_product(0, 3)
    p1_start(0)
    last_product(3, 5)
    p1_start(1)
    for step in (p1_middle, p1_end, p2_middle, p2_end):
        for half in range(2):
            step(half)

    for kk in range(2):
        for xx in range(4):
            gbuf[kk * 4 + xx] = fin[kk * 40:(kk + 1) * 40, xx * BLK:(xx + 1) * BLK]
    for d in range(1, 8):
        idx, kk, xx = peer8(d)
        send(gbuf.at[idx], hbuf.at[me8], g_ss.at[d], g_rs.at[d], dev(y, z, kk, xx))
    hbuf[me8] = gbuf[me8]
    for d in range(1, 8):
        src8 = lax.rem(me8 + 8 - d, 8)
        rcopy(gbuf.at[0], hbuf.at[src8], g_ss.at[d], g_rs.at[d], sib).wait_recv()
    for p in range(4):
        src = (p % 2) * 4 + p // 2
        out[p] = hbuf[src] + hbuf[src + 2]

    for c in pending:
        c.wait_send()

    def wait_own(kind, pos_list):
        for pos in pos_list:
            for i in range(NS):
                share(kind, pos, i).wait_send()
        for i in range(NS):
            ref = bbuf.at[k if kind == 0 else 2, xm if kind == 0 else xp, rows(i)]
            rcopy(ref, ref, bf_ss.at[kind, i], b_rs.at[kind, 1, i], (row, xp if kind == 0 else xm)).wait_send()

    wait_own(0, (1, 2, 3))

    @pl.when(is_owner)
    def _():
        wait_own(1, (0, 1, 2, 3))


def exchange(b_own, t_own, l_own):
    vmem = pl.BlockSpec(memory_space=pltpu.VMEM)
    dma = pltpu.SemaphoreType.DMA
    return pl.pallas_call(
        kernel,
        out_shape=jax.ShapeDtypeStruct((4, 40, BLK), F32),
        in_specs=[vmem] * 3,
        out_specs=vmem,
        scratch_shapes=[
            pltpu.VMEM((3, 4, BLK, V), BF16),
            pltpu.VMEM((8, 16, V), BF16),
            pltpu.VMEM((4, 4, PIECE, V), BF16),
            pltpu.VMEM((2, 32, V), BF16),
            pltpu.VMEM((V, 32), BF16),
            pltpu.VMEM((32, V), BF16),
            pltpu.VMEM((3, V, V), BF16),
            pltpu.VMEM((4, 4, PIECE, V), F32),
            pltpu.VMEM((2, 3, 4, PIECE, HALF), BF16),
            pltpu.VMEM((2, 3, 4, PIECE, HALF), BF16),
            pltpu.VMEM((2, 3, PIECE, HALF), BF16),
            pltpu.VMEM((2, 3, PIECE, HALF), BF16),
            pltpu.VMEM((PIECE, V), F32),
            pltpu.VMEM((8, 40, BLK), F32),
            pltpu.VMEM((8, 40, BLK), F32),
            dma((8,)), dma((8,)),
            dma((2, 2, 3)), dma((2, 2, 3)),
            dma, dma,
            dma((2,)),
            dma((3, NS)), dma((2, NS)), dma((2, 3, NS)),
            dma((2, 4, NS)), dma((2, 4, NS)),
            dma((2, 3)), dma((2, 3)), dma((2, 3)), dma((2, 3)),
            dma((8,)), dma((8,)),
        ],
        compiler_params=pltpu.CompilerParams(
            collective_id=0, has_side_effects=True, vmem_limit_bytes=62 * 1024 * 1024
        ),
    )(b_own, t_own, l_own)


def local(
    amplitudes, integrals, occupied_integrals, pair_orbitals, amplitude_tiles, integral_tiles
):
    x = lax.axis_index("col")
    row = lax.axis_index("row")
    tiles_here = BLK // TILE
    tile_rows = lax.dynamic_slice_in_dim(integral_tiles, x * tiles_here, tiles_here, 0)
    factor_mask = jnp.repeat(jnp.repeat(tile_rows, TILE, axis=0), TILE, axis=1)
    masked_int = integrals * factor_mask.astype(BF16)[None]

    amp_rows = amplitudes.shape[1]
    tile_of = ((row * 4 + x) * amp_rows + jnp.arange(amp_rows, dtype=jnp.int32)) // TILE
    picker = (tile_of[:, None] == jnp.arange(V // TILE, dtype=jnp.int32)[None, :]).astype(F32)
    amp_mask = jnp.einsum("nk,pkm->pnm", picker, amplitude_tiles.astype(F32))
    amp_mask = jnp.repeat(amp_mask, TILE, axis=2).astype(BF16)
    masked_amp = jnp.pad(amplitudes * amp_mask, ((0, 0), (0, 16 - amp_rows), (0, 0)))

    orbital_ids = jnp.arange(occupied_integrals.shape[1], dtype=jnp.int32)
    order = pair_orbitals[:, ::-1].reshape(-1)
    pick = (order[:, None] == orbital_ids[None, :]).astype(BF16)
    occ = jnp.einsum("ro,qov->rqv", pick, occupied_integrals, preferred_element_type=F32).astype(BF16)
    occ = jnp.pad(occ, ((0, 0), (0, 13), (0, 0))).reshape(4, 32, V)

    res = exchange(masked_int, masked_amp, occ)
    return jnp.swapaxes(res, 1, 2)


def solution(mesh):
    placed = (
        P(None, ("row", "col"), None),
        P("row", "col", None),
        P("row", None, None),
        P(),
        P(),
        P(),
    )
    return jax.shard_map(
        local, mesh=mesh, in_specs=placed, out_specs=P(None, "col", "row"), check_vma=False
    )
```

```python
import jax
import jax.numpy as jnp
from jax import lax
from jax.experimental import pallas as pl
from jax.experimental.pallas import tpu as pltpu
from jax.sharding import PartitionSpec as P

MESH = pl.DeviceIdType.MESH
TILE = 64
V = 1280
VT = 20
BLK = 320
PIECE = 80
HALF = 640
EARLY = 768
WIDE = 384
PARTS = ((0, 0, WIDE), (1, WIDE, WIDE), (0, EARLY, 256), (1, EARLY + 256, 256))
NS = 2
SUB = BLK // NS
F32 = jnp.float32
BF16 = jnp.bfloat16


def kernel(
    b_in, t_in, occ_in, pairs, a_tiles, i_tiles, out,
    b_own, t_own, occ, l_own,
    bbuf, tst, tbuf, lbuf, ut, li2, xbuf, acc,
    s1, r1, s2, r2, fin, gbuf, hbuf,
    in_ls, t1_ss, t1_rs, tg_ss, tg_rs, th_ss, th_rs, l_ss, l_rs, own_ls,
    bo_ss, bf_ss, b_rs, sh_ss, sh_rs, p1_ss, p1_rs, p2_ss, p2_rs, g_ss, g_rs,
):
    x = lax.axis_index("col")
    row = lax.axis_index("row")
    k = lax.rem(row, 2)
    yz = row // 2
    y = yz // 4
    z = lax.rem(yz, 4)
    s = 1 - 2 * lax.rem(x, 2)
    xp = lax.rem(x + s + 4, 4)
    xm = lax.rem(x - s + 4, 4)
    xo = lax.rem(x + 2, 4)
    sg = 1 - 2 * k
    me8 = k * 4 + x
    pair = 2 * lax.rem(x, 2) + k
    sib = (yz * 2 + 1 - k, x)
    owner2 = lax.rem((x + 1) // 2 + 1, 2)
    is_owner = k == owner2
    main_j = x // 2

    def dev(yy, zz, kk, xx):
        return ((yy * 4 + zz) * 2 + kk, xx)

    def ring(v):
        return lax.rem(v + 8, 4)

    def peer8(d):
        idx = lax.rem(me8 + d, 8)
        return idx, idx // 4, lax.rem(idx, 4)

    def rcopy(src, dst, ss, rs, to):
        return pltpu.make_async_remote_copy(
            src_ref=src, dst_ref=dst, send_sem=ss, recv_sem=rs, device_id=to, device_id_type=MESH
        )

    pending = []

    def send(src, dst, ss, rs, to):
        c = rcopy(src, dst, ss, rs, to)
        c.start()
        pending.append(c)
        return c

    load_b = pltpu.make_async_copy(b_in, b_own, in_ls.at[0])
    load_b.start()
    load_occ = pltpu.make_async_copy(occ_in, occ, in_ls.at[1])
    load_occ.start()

    barrier = pltpu.get_barrier_semaphore()
    for d in range(1, 8):
        _, kk, xx = peer8(d)
        pl.semaphore_signal(barrier, inc=1, device_id=dev(y, z, kk, xx), device_id_type=MESH)
    for step in (1, -1):
        pl.semaphore_signal(barrier, inc=1, device_id=dev(ring(y + step), z, k, x), device_id_type=MESH)
        pl.semaphore_signal(barrier, inc=1, device_id=dev(y, ring(z + step), k, x), device_id_type=MESH)

    def iota(shape, dim):
        return lax.broadcasted_iota(jnp.int32, shape, dim)

    def ones(cond):
        return jnp.where(cond, 1.0, 0.0).astype(BF16)

    spread = ones(iota((VT, V), 0) == jnp.right_shift(iota((VT, V), 1), 6))
    first_row = (row * 4 + x) * 10
    pick_t = ones(jnp.right_shift(iota((16, VT), 0) + first_row, 6) == iota((16, VT), 1))
    for p in range(4):
        tiles = a_tiles[p].astype(F32).astype(BF16)
        small = jnp.dot(pick_t, tiles, preferred_element_type=F32).astype(BF16)
        mask = jnp.dot(small, spread, preferred_element_type=F32).astype(BF16)
        t_own[p] = jnp.zeros((16, V), BF16)
        t_own[p, 0:10] = t_in[p] * mask[0:10]
    pick_b = ones(iota((16, VT), 0) + 5 * x == iota((16, VT), 1))
    small = jnp.dot(pick_b, i_tiles[...].astype(F32).astype(BF16), preferred_element_type=F32).astype(BF16)
    mask = jnp.dot(small, spread, preferred_element_type=F32)
    load_b.wait()
    for t in range(BLK // TILE):
        wide = jnp.broadcast_to(mask[t:t + 1], (TILE, V)).astype(BF16)
        for j in range(3):
            b_own[j, t * TILE:(t + 1) * TILE] = b_own[j, t * TILE:(t + 1) * TILE] * wide
    pl.semaphore_wait(barrier, 11)

    for d in range(1, 8):
        idx, kk, xx = peer8(d)
        send(t_own.at[2 * lax.rem(xx, 2) + kk], tst.at[me8], t1_ss.at[d], t1_rs.at[d], dev(y, z, kk, xx))
    dest2 = jnp.where(is_owner, xm, xp)
    which2 = jnp.where(is_owner, 0, 2)

    def rows(i):
        return pl.ds(i * SUB, SUB)

    for i in range(NS):
        send(b_own.at[1 - main_j, rows(i)], bbuf.at[k, x, rows(i)], bo_ss.at[1, i], b_rs.at[0, 2, i],
             (row, xm))
    for i in range(NS):
        send(b_own.at[2, rows(i)], bbuf.at[2, x, rows(i)], bo_ss.at[2, i], b_rs.at[1, which2, i],
             (row, dest2))
    for i in range(NS):
        send(b_own.at[main_j, rows(i)], bbuf.at[k, x, rows(i)], bo_ss.at[0, i], b_rs.at[0, 0, i],
             (row, xp))

    def share(kind, pos, i, src=None):
        slot, blk = (k, None) if kind == 0 else (2, None)
        blk = (x, pos_main(pos) if kind == 0 else pos_second(pos))[pos > 0]
        dst = bbuf.at[slot, blk, rows(i)]
        return rcopy(dst if src is None else src, dst, sh_ss.at[kind, pos, i], sh_rs.at[kind, pos, i], sib)

    def pos_main(pos):
        return (x, xm, xp, xo)[pos]

    def pos_second(pos):
        return (x, xp, xm, xo)[pos]

    which_of = (None, 2, 0, 1)

    for i in range(NS):
        c = share(0, 0, i, b_own.at[main_j, rows(i)])
        c.start()
        pending.append(c)

    @pl.when(is_owner)
    def _():
        for i in range(NS):
            share(1, 0, i, b_own.at[2, rows(i)]).start()

    own_main = pltpu.make_async_copy(b_own.at[main_j], bbuf.at[k, x], own_ls.at[0])
    own_main.start()
    own_second = pltpu.make_async_copy(b_own.at[2], bbuf.at[2, x], own_ls.at[1])

    @pl.when(is_owner)
    def _():
        own_second.start()

    load_occ.wait()
    other = 2 * lax.rem(x, 2) + 1 - k
    orb_row, orb_col = iota((32, 480), 0), iota((32, 480), 1)

    def occ_rows(p):
        aux = jnp.bitwise_and(orb_row, 15)
        orb = jnp.where(orb_row < 16, pairs[p, 1], pairs[p, 0])
        hot = ones((orb_col == aux * 160 + orb) & (aux < 3))
        return jnp.dot(hot, occ[...].reshape(480, V), preferred_element_type=F32).astype(BF16)

    l_own[...] = occ_rows(other)
    lbuf[0] = occ_rows(pair)
    send(l_own, lbuf.at[1], l_ss, l_rs, sib)

    tst[me8] = t_own[pair]
    ri, ci = iota((PIECE, 128), 0), iota((PIECE, 128), 1)
    within = jnp.bitwise_and(ci, 15)
    pick = ones((within < 10) & (ri == jnp.right_shift(ci, 4) * 10 + within))
    for d in range(1, 8):
        src8 = lax.rem(me8 + 8 - d, 8)
        rcopy(t_own.at[0], tst.at[src8], t1_ss.at[d], t1_rs.at[d], sib).wait_recv()
    piece = jnp.dot(pick, tst[...].reshape(128, V), preferred_element_type=F32)
    tbuf[y, z] = piece.astype(BF16)

    col_h = (pl.ds(0, HALF), pl.ds(HALF, HALF))

    def along(half, phase, off):
        if (half == 0) == (phase == 0):
            return ring(y + off), dev(ring(y + off), z, k, x)
        return ring(z + off), dev(y, ring(z + off), k, x)

    def t_at(half, first, second):
        if half == 0:
            return tbuf.at[ring(y + first), ring(z + second), :, col_h[0]]
        return tbuf.at[ring(y + second), ring(z + first), :, col_h[1]]

    offs = (0, -sg, sg, 2)

    def t_one(half, n):
        ref = t_at(half, offs[n], 0)
        return ref, tg_ss.at[half, n], tg_rs.at[half, n]

    def t_two(half, m, n):
        ref = t_at(half, offs[m], offs[n])
        return ref, th_ss.at[half, m, n], th_rs.at[half, m, n]

    def t_spread(half, m):
        ref = t_at(half, offs[m], 0)
        send(ref, ref, th_ss.at[half, m, 0], th_rs.at[half, m, 1], along(half, 1, sg)[1])
        send(ref, ref, th_ss.at[half, m, 1], th_rs.at[half, m, 2], along(half, 1, -sg)[1])

    def t_arrive(ref, ss, rs):
        rcopy(ref, ref, ss, rs, sib).wait_recv()

    def t_first(m):
        for half in range(2):
            if m == 0:
                ref = t_at(half, 0, 0)
                send(ref, ref, tg_ss.at[half, 0], tg_rs.at[half, 1], along(half, 0, sg)[1])
                send(ref, ref, tg_ss.at[half, 1], tg_rs.at[half, 2], along(half, 0, -sg)[1])
            else:
                ref, ss, rs = t_one(half, m)
                t_arrive(ref, ss, rs)
                if m == 1:
                    send(ref, ref, tg_ss.at[half, 2], tg_rs.at[half, 3], along(half, 0, sg)[1])
            if m > 0:
                t_spread(half, m)
        if m == 0:
            for half in range(2):
                t_spread(half, 0)

    def t_second(m):
        for half in range(2):
            ref, ss, rs = t_two(half, m, 1)
            t_arrive(ref, ss, rs)
            send(ref, ref, th_ss.at[half, m, 2], th_rs.at[half, m, 3], along(half, 1, sg)[1])

    def t_finish(m):
        for half in range(2):
            for n in (2, 3):
                t_arrive(*t_two(half, m, n))

    for m in range(4):
        t_first(m)
    for m in range(4):
        t_second(m)

    def land(kind, pos):
        slot = k if kind == 0 else 2
        blk = pos_main(pos) if kind == 0 else pos_second(pos)
        for i in range(NS):
            ref = bbuf.at[slot, blk, rows(i)]
            rcopy(ref, ref, bo_ss.at[0, i], b_rs.at[kind, which_of[pos], i], sib).wait_recv()
            if pos == 1:
                to = xp if kind == 0 else xm
                rcopy(ref, ref, bf_ss.at[kind, i], b_rs.at[kind, 1, i], (row, to)).start()
            share(kind, pos, i).start()

    def from_sib(kind, pos):
        slot = 1 - k if kind == 0 else 2
        blk = pos_main(pos) if kind == 0 else pos_second(pos)
        for i in range(NS):
            ref = bbuf.at[slot, blk, rows(i)]
            rcopy(ref, ref, sh_ss.at[kind, pos, i], sh_rs.at[kind, pos, i], sib).wait_recv()

    def land_second(pos):
        @pl.when(is_owner)
        def _():
            land(1, pos)

    def from_owner(pos):
        @pl.when(jnp.logical_not(is_owner))
        def _():
            from_sib(1, pos)

    def blk_at(pos):
        off = jnp.where(pos == 1, -s, jnp.where(pos == 2, s, jnp.where(pos == 3, 2, 0)))
        return ring(x + off)

    def first_product(slot, pos):
        val = jnp.dot(bbuf[slot, blk_at(pos)], tbuf[...].reshape(V, V), preferred_element_type=F32)
        xbuf[slot, pl.ds(pl.multiple_of(pos * BLK, 64), BLK), :] = val.astype(BF16)

    def first_products(pos):
        @pl.loop(0, 3)
        def _(sl):
            first_product(sl, pos)

    nt = (((1,), (1,)), ((), ()))

    def second_product(pos, lo, width):
        blk = blk_at(pos)
        cols = pl.ds(lo, width)
        val = jnp.dot(ut[pl.ds(pl.multiple_of(blk * BLK, 64), BLK), :], li2[:, cols], preferred_element_type=F32)
        for sl in range(3):
            val += lax.dot_general(bbuf[sl, blk], xbuf[sl, cols, :], nt, preferred_element_type=F32)
        acc[blk, :, :, cols] = val.reshape(4, PIECE, width)

    land(0, 1)
    land_second(1)
    for m in range(4):
        t_finish(m)
    own_main.wait()

    @pl.when(is_owner)
    def _():
        own_second.wait()

    from_sib(0, 0)
    from_owner(0)
    first_products(0)

    rcopy(l_own, lbuf.at[1], l_ss, l_rs, sib).wait_recv()
    pick_l = jnp.where(k == x // 2, 0, 1)
    u = jnp.dot(lbuf[pick_l, 0:16], tbuf[...].reshape(V, V), preferred_element_type=F32)
    hi = u.astype(BF16).astype(F32)
    ut[...] = jnp.concatenate([hi, u - hi], axis=0).T.astype(BF16)
    li = lbuf[pick_l, 16:32]
    for n in range(4):
        blk = blk_at(n)
        for kk in range(4):
            @pl.when(blk == kk)
            def _():
                li2[0:16, n * BLK:(n + 1) * BLK] = li[:, kk * BLK:(kk + 1) * BLK]
                li2[16:32, n * BLK:(n + 1) * BLK] = li[:, kk * BLK:(kk + 1) * BLK]

    land(0, 2)
    land_second(2)
    from_sib(0, 1)
    from_owner(2)
    first_products(1)
    from_sib(0, 2)
    from_owner(1)
    first_products(2)

    @pl.loop(0, 3)
    def _(pos):
        second_product(pos, 0, EARLY)

    land(0, 3)
    land_second(3)
    first_product(k, 3)
    from_sib(0, 3)
    first_product(1 - k, 3)
    from_owner(3)
    first_product(2, 3)
    second_product(3, 0, EARLY)

    def late_product(lo, hi):
        @pl.loop(lo, hi)
        def _(pos):
            second_product(pos, EARLY, V - EARLY)

    def ralong(n, phase, off):
        return along(1 - PARTS[n][0], phase, off)

    def cols_of(n):
        return pl.ds(PARTS[n][1], PARTS[n][2])

    def part(n, t, i):
        if PARTS[n][0] == 0:
            return acc[t, i, :, cols_of(n)]
        return acc[i, t, :, cols_of(n)]

    def put(n, t, i, val):
        if PARTS[n][0] == 0:
            acc[t, i, :, cols_of(n)] = val
        else:
            acc[i, t, :, cols_of(n)] = val

    def p1_at(ref, n, m):
        return ref.at[n, m, :, :, pl.ds(0, PARTS[n][2])]

    def p2_at(ref, n, m):
        return ref.at[n, m, :, pl.ds(0, PARTS[n][2])]

    def p1_send(n, m, to):
        send(p1_at(s1, n, m), p1_at(r1, n, m), p1_ss.at[n, m], p1_rs.at[n, m], to)

    def p2_send(n, m, to):
        send(p2_at(s2, n, m), p2_at(r2, n, m), p2_ss.at[n, m], p2_rs.at[n, m], to)

    def p1_wait(n, m):
        rcopy(p1_at(s1, n, m), p1_at(r1, n, m), p1_ss.at[n, m], p1_rs.at[n, m], sib).wait_recv()

    def p2_wait(n, m):
        rcopy(p2_at(s2, n, m), p2_at(r2, n, m), p2_ss.at[n, m], p2_rs.at[n, m], sib).wait_recv()

    def got1(n, m, t):
        return r1[n, m, t, :, pl.ds(0, PARTS[n][2])].astype(F32)

    def got2(n, m):
        return r2[n, m, :, pl.ds(0, PARTS[n][2])].astype(F32)

    def p1_start(n):
        far = ralong(n, 0, 2)[0]
        back, back_dev = ralong(n, 0, -sg)
        for t in range(4):
            s1[n, 0, t, :, pl.ds(0, PARTS[n][2])] = part(n, t, far).astype(BF16)
        p1_send(n, 0, ralong(n, 0, sg)[1])
        for t in range(4):
            s1[n, 1, t, :, pl.ds(0, PARTS[n][2])] = part(n, t, back).astype(BF16)
        p1_send(n, 1, back_dev)

    def p1_middle(n):
        nxt, nxt_dev = ralong(n, 0, sg)
        p1_wait(n, 0)
        for t in range(4):
            s1[n, 2, t, :, pl.ds(0, PARTS[n][2])] = (part(n, t, nxt) + got1(n, 0, t)).astype(BF16)
        p1_send(n, 2, nxt_dev)

    def p1_end(n):
        here = ralong(n, 0, 0)[0]
        p1_wait(n, 1)
        p1_wait(n, 2)

        def total(t):
            return part(n, t, here) + got1(n, 1, t) + got1(n, 2, t)

        far = ralong(n, 1, 2)[0]
        back, back_dev = ralong(n, 1, -sg)
        nxt, nxt_dev = ralong(n, 1, sg)
        s2[n, 0, :, pl.ds(0, PARTS[n][2])] = total(far).astype(BF16)
        p2_send(n, 0, nxt_dev)
        s2[n, 1, :, pl.ds(0, PARTS[n][2])] = total(back).astype(BF16)
        p2_send(n, 1, back_dev)
        put(n, nxt, here, total(nxt))
        mid = ralong(n, 1, 0)[0]
        put(n, mid, here, total(mid))

    def p2_middle(n):
        nxt, nxt_dev = ralong(n, 1, sg)
        here = ralong(n, 0, 0)[0]
        p2_wait(n, 0)
        s2[n, 2, :, pl.ds(0, PARTS[n][2])] = (part(n, nxt, here) + got2(n, 0)).astype(BF16)
        p2_send(n, 2, nxt_dev)

    def p2_end(n):
        mid = ralong(n, 1, 0)[0]
        here = ralong(n, 0, 0)[0]
        p2_wait(n, 1)
        p2_wait(n, 2)
        fin[:, cols_of(n)] = part(n, mid, here) + got2(n, 1) + got2(n, 2)
        xx = blk_at(n)
        for kk in range(2):
            gbuf[n, kk] = fin[kk * 40:(kk + 1) * 40, n * BLK:(n + 1) * BLK]
        if n == 0:
            send(gbuf.at[0, 1 - k], hbuf.at[me8], g_ss.at[0, 0], g_rs.at[me8], sib)
            hbuf[me8] = gbuf[0, k]
        else:
            for kk in range(2):
                send(gbuf.at[n, kk], hbuf.at[me8], g_ss.at[n, kk], g_rs.at[me8], dev(y, z, kk, xx))

    p1_start(0)
    p1_start(1)
    late_product(0, 2)
    p1_middle(0)
    p1_middle(1)
    late_product(2, 4)
    p1_start(2)
    p1_start(3)
    p1_end(0)
    p1_end(1)
    p2_middle(0)
    p2_middle(1)
    p1_middle(2)
    p1_middle(3)
    p2_end(0)
    p2_end(1)
    p1_end(2)
    p1_end(3)
    p2_middle(2)
    p2_middle(3)
    p2_end(2)
    p2_end(3)

    for d in range(1, 8):
        src8 = lax.rem(me8 + d, 8)
        rcopy(gbuf.at[0, 0], hbuf.at[src8], g_ss.at[0, 0], g_rs.at[src8], sib).wait_recv()
    for p in range(4):
        src = (p % 2) * 4 + p // 2
        out[p] = hbuf[src] + hbuf[src + 2]

    for c in pending:
        c.wait_send()

    def wait_own(kind, pos_list):
        for pos in pos_list:
            for i in range(NS):
                share(kind, pos, i).wait_send()
        for i in range(NS):
            ref = bbuf.at[k if kind == 0 else 2, xm if kind == 0 else xp, rows(i)]
            rcopy(ref, ref, bf_ss.at[kind, i], b_rs.at[kind, 1, i], (row, xp if kind == 0 else xm)).wait_send()

    wait_own(0, (1, 2, 3))

    @pl.when(is_owner)
    def _():
        wait_own(1, (0, 1, 2, 3))


def exchange(*args):
    vmem = pl.BlockSpec(memory_space=pltpu.VMEM)
    anywhere = pl.BlockSpec(memory_space=pl.ANY)
    smem = pl.BlockSpec(memory_space=pltpu.SMEM)
    dma = pltpu.SemaphoreType.DMA
    return pl.pallas_call(
        kernel,
        out_shape=jax.ShapeDtypeStruct((4, 40, BLK), F32),
        in_specs=[anywhere, vmem, anywhere, smem, vmem, vmem],
        out_specs=vmem,
        scratch_shapes=[
            pltpu.VMEM((3, BLK, V), BF16),
            pltpu.VMEM((4, 16, V), BF16),
            pltpu.VMEM((3, 160, V), BF16),
            pltpu.VMEM((32, V), BF16),
            pltpu.VMEM((3, 4, BLK, V), BF16),
            pltpu.VMEM((8, 16, V), BF16),
            pltpu.VMEM((4, 4, PIECE, V), BF16),
            pltpu.VMEM((2, 32, V), BF16),
            pltpu.VMEM((V, 32), BF16),
            pltpu.VMEM((32, V), BF16),
            pltpu.VMEM((3, V, V), BF16),
            pltpu.VMEM((4, 4, PIECE, V), F32),
            pltpu.VMEM((4, 3, 4, PIECE, WIDE), BF16),
            pltpu.VMEM((4, 3, 4, PIECE, WIDE), BF16),
            pltpu.VMEM((4, 3, PIECE, WIDE), BF16),
            pltpu.VMEM((4, 3, PIECE, WIDE), BF16),
            pltpu.VMEM((PIECE, V), F32),
            pltpu.VMEM((4, 2, 40, BLK), F32),
            pltpu.VMEM((8, 40, BLK), F32),
            dma((2,)),
            dma((8,)), dma((8,)),
            dma((2, 4)), dma((2, 4)),
            dma((2, 4, 4)), dma((2, 4, 4)),
            dma, dma,
            dma((2,)),
            dma((3, NS)), dma((2, NS)), dma((2, 3, NS)),
            dma((2, 4, NS)), dma((2, 4, NS)),
            dma((4, 3)), dma((4, 3)), dma((4, 3)), dma((4, 3)),
            dma((4, 2)), dma((8,)),
        ],
        compiler_params=pltpu.CompilerParams(
            collective_id=0, has_side_effects=True, vmem_limit_bytes=62 * 1024 * 1024
        ),
    )(*args)


def local(
    amplitudes, integrals, occupied_integrals, pair_orbitals, amplitude_tiles, integral_tiles
):
    res = exchange(
        integrals, amplitudes, occupied_integrals, pair_orbitals, amplitude_tiles, integral_tiles
    )
    return jnp.swapaxes(res, 1, 2)


def solution(mesh):
    placed = (
        P(None, ("row", "col"), None),
        P("row", "col", None),
        P("row", None, None),
        P(),
        P(),
        P(),
    )
    return jax.shard_map(
        local, mesh=mesh, in_specs=placed, out_specs=P(None, "col", "row"), check_vma=False
    )
```

```python
import jax
import jax.numpy as jnp
from jax import lax
from jax.experimental import pallas as pl
from jax.experimental.pallas import tpu as pltpu
from jax.sharding import PartitionSpec as P

MESH = pl.DeviceIdType.MESH
TILE = 64
V = 1280
VT = 20
BLK = 320
PIECE = 80
HALF = 640
EARLY = 896
WIDE = 512
PARTS = ((0, 0, 384), (1, 384, WIDE), (0, EARLY, 256), (1, EARLY + 256, 128))
NS = 2
SUB = BLK // NS
F32 = jnp.float32
BF16 = jnp.bfloat16


def kernel(
    b_in, t_in, occ_in, pairs, a_tiles, i_tiles, out,
    b_own, t_own, occ, l_own,
    bbuf, tst, tbuf, lbuf, ut, li2, xbuf, acc,
    s1, r1, s2, r2, fin, gbuf, hbuf,
    in_ls, t1_ss, t1_rs, tg_ss, tg_rs, th_ss, th_rs, l_ss, l_rs, own_ls,
    bo_ss, bf_ss, b_rs, sh_ss, sh_rs, p1_ss, p1_rs, p2_ss, p2_rs, g_ss, g_rs,
):
    x = lax.axis_index("col")
    row = lax.axis_index("row")
    k = lax.rem(row, 2)
    yz = row // 2
    y = yz // 4
    z = lax.rem(yz, 4)
    s = 1 - 2 * lax.rem(x, 2)
    xp = lax.rem(x + s + 4, 4)
    xm = lax.rem(x - s + 4, 4)
    xo = lax.rem(x + 2, 4)
    sg = 1 - 2 * k
    me8 = k * 4 + x
    pair = 2 * lax.rem(x, 2) + k
    sib = (yz * 2 + 1 - k, x)
    owner2 = lax.rem((x + 1) // 2 + 1, 2)
    is_owner = k == owner2
    main_j = x // 2

    def dev(yy, zz, kk, xx):
        return ((yy * 4 + zz) * 2 + kk, xx)

    def ring(v):
        return lax.rem(v + 8, 4)

    def peer8(d):
        idx = lax.rem(me8 + d, 8)
        return idx, idx // 4, lax.rem(idx, 4)

    def rcopy(src, dst, ss, rs, to):
        return pltpu.make_async_remote_copy(
            src_ref=src, dst_ref=dst, send_sem=ss, recv_sem=rs, device_id=to, device_id_type=MESH
        )

    pending = []

    def send(src, dst, ss, rs, to):
        c = rcopy(src, dst, ss, rs, to)
        c.start()
        pending.append(c)
        return c

    load_b = pltpu.make_async_copy(b_in, b_own, in_ls.at[0])
    load_b.start()
    load_occ = pltpu.make_async_copy(occ_in, occ, in_ls.at[1])
    load_occ.start()

    barrier = pltpu.get_barrier_semaphore()
    for d in range(1, 8):
        _, kk, xx = peer8(d)
        pl.semaphore_signal(barrier, inc=1, device_id=dev(y, z, kk, xx), device_id_type=MESH)
    for step in (1, -1):
        pl.semaphore_signal(barrier, inc=1, device_id=dev(ring(y + step), z, k, x), device_id_type=MESH)
        pl.semaphore_signal(barrier, inc=1, device_id=dev(y, ring(z + step), k, x), device_id_type=MESH)

    def iota(shape, dim):
        return lax.broadcasted_iota(jnp.int32, shape, dim)

    def ones(cond):
        return jnp.where(cond, 1.0, 0.0).astype(BF16)

    spread = ones(iota((VT, V), 0) == jnp.right_shift(iota((VT, V), 1), 6))
    tile_row = jnp.right_shift(jnp.right_shift(iota((40, 80), 0), 2) + (row * 4 + x) * 10, 6)
    same_pair = jnp.bitwise_and(iota((40, 80), 0), 3) == jnp.bitwise_and(iota((40, 80), 1), 3)
    pick_t = ones(same_pair & (jnp.right_shift(iota((40, 80), 1), 2) == tile_row))
    small = jnp.dot(pick_t, a_tiles[...].astype(F32).astype(BF16), preferred_element_type=F32).astype(BF16)
    mask = jnp.dot(small, spread, preferred_element_type=F32)
    raw = jnp.concatenate([t_in[i].astype(F32) for i in range(10)], axis=0)
    turn_i = jnp.bitwise_and(iota((64, 40), 0), 15)
    turn = ones((turn_i < 10) & (iota((64, 40), 1) == turn_i * 4 + jnp.right_shift(iota((64, 40), 0), 4)))
    turned = jnp.dot(turn, (raw * mask).astype(BF16), preferred_element_type=F32).astype(BF16)
    for p in range(4):
        t_own[p] = turned[p * 16:(p + 1) * 16]
    pick_b = ones(iota((16, VT), 0) + 5 * x == iota((16, VT), 1))
    small = jnp.dot(pick_b, i_tiles[...].astype(F32).astype(BF16), preferred_element_type=F32).astype(BF16)
    mask = jnp.dot(small, spread, preferred_element_type=F32)
    load_b.wait()
    for t in range(BLK // TILE):
        wide = jnp.broadcast_to(mask[t:t + 1], (TILE, V)).astype(BF16)
        for j in range(3):
            b_own[j, t * TILE:(t + 1) * TILE] = b_own[j, t * TILE:(t + 1) * TILE] * wide
    pl.semaphore_wait(barrier, 11)

    for d in range(1, 8):
        idx, kk, xx = peer8(d)
        send(t_own.at[2 * lax.rem(xx, 2) + kk], tst.at[me8], t1_ss.at[d], t1_rs.at[d], dev(y, z, kk, xx))
    dest2 = jnp.where(is_owner, xm, xp)
    which2 = jnp.where(is_owner, 0, 2)

    def rows(i):
        return pl.ds(i * SUB, SUB)

    def share(kind, pos, i, src=None):
        slot, blk = (k, None) if kind == 0 else (2, None)
        blk = (x, pos_main(pos) if kind == 0 else pos_second(pos))[pos > 0]
        dst = bbuf.at[slot, blk, rows(i)]
        return rcopy(dst if src is None else src, dst, sh_ss.at[kind, pos, i], sh_rs.at[kind, pos, i], sib)

    def pos_main(pos):
        return (x, xm, xp, xo)[pos]

    def pos_second(pos):
        return (x, xp, xm, xo)[pos]

    which_of = (None, 2, 0, 1)

    for i in range(NS):
        c = share(0, 0, i, b_own.at[main_j, rows(i)])
        c.start()
        pending.append(c)

    @pl.when(is_owner)
    def _():
        for i in range(NS):
            share(1, 0, i, b_own.at[2, rows(i)]).start()

    own_main = pltpu.make_async_copy(b_own.at[main_j], bbuf.at[k, x], own_ls.at[0])
    own_main.start()
    own_second = pltpu.make_async_copy(b_own.at[2], bbuf.at[2, x], own_ls.at[1])

    @pl.when(is_owner)
    def _():
        own_second.start()

    load_occ.wait()
    other = 2 * lax.rem(x, 2) + 1 - k
    orb_row, orb_col = iota((32, 480), 0), iota((32, 480), 1)

    def occ_rows(p):
        aux = jnp.bitwise_and(orb_row, 15)
        orb = jnp.where(orb_row < 16, pairs[1, p], pairs[0, p])
        hot = ones((orb_col == aux * 160 + orb) & (aux < 3))
        return jnp.dot(hot, occ[...].reshape(480, V), preferred_element_type=F32).astype(BF16)

    l_own[...] = occ_rows(other)
    lbuf[0] = occ_rows(pair)
    send(l_own, lbuf.at[1], l_ss, l_rs, sib)

    tst[me8] = t_own[pair]
    ri, ci = iota((PIECE, 128), 0), iota((PIECE, 128), 1)
    within = jnp.bitwise_and(ci, 15)
    pick = ones((within < 10) & (ri == jnp.right_shift(ci, 4) * 10 + within))
    for d in range(1, 8):
        src8 = lax.rem(me8 + 8 - d, 8)
        rcopy(t_own.at[0], tst.at[src8], t1_ss.at[d], t1_rs.at[d], sib).wait_recv()
    for i in range(NS):
        send(b_own.at[1 - main_j, rows(i)], bbuf.at[k, x, rows(i)], bo_ss.at[1, i], b_rs.at[0, 2, i],
             (row, xm))
    for i in range(NS):
        send(b_own.at[2, rows(i)], bbuf.at[2, x, rows(i)], bo_ss.at[2, i], b_rs.at[1, which2, i],
             (row, dest2))
    for i in range(NS):
        send(b_own.at[main_j, rows(i)], bbuf.at[k, x, rows(i)], bo_ss.at[0, i], b_rs.at[0, 0, i],
             (row, xp))

    piece = jnp.dot(pick, tst[...].reshape(128, V), preferred_element_type=F32)
    tbuf[y, z] = piece.astype(BF16)

    col_h = (pl.ds(0, HALF), pl.ds(HALF, HALF))

    def along(half, phase, off):
        if (half == 0) == (phase == 0):
            return ring(y + off), dev(ring(y + off), z, k, x)
        return ring(z + off), dev(y, ring(z + off), k, x)

    def t_at(half, first, second):
        if half == 0:
            return tbuf.at[ring(y + first), ring(z + second), :, col_h[0]]
        return tbuf.at[ring(y + second), ring(z + first), :, col_h[1]]

    offs = (0, -sg, sg, 2)

    def t_one(half, n):
        ref = t_at(half, offs[n], 0)
        return ref, tg_ss.at[half, n], tg_rs.at[half, n]

    def t_two(half, m, n):
        ref = t_at(half, offs[m], offs[n])
        return ref, th_ss.at[half, m, n], th_rs.at[half, m, n]

    def t_spread(half, m):
        ref = t_at(half, offs[m], 0)
        send(ref, ref, th_ss.at[half, m, 0], th_rs.at[half, m, 1], along(half, 1, sg)[1])
        send(ref, ref, th_ss.at[half, m, 1], th_rs.at[half, m, 2], along(half, 1, -sg)[1])

    def t_arrive(ref, ss, rs):
        rcopy(ref, ref, ss, rs, sib).wait_recv()

    def t_first(m):
        for half in range(2):
            if m == 0:
                ref = t_at(half, 0, 0)
                send(ref, ref, tg_ss.at[half, 0], tg_rs.at[half, 1], along(half, 0, sg)[1])
                send(ref, ref, tg_ss.at[half, 1], tg_rs.at[half, 2], along(half, 0, -sg)[1])
            else:
                ref, ss, rs = t_one(half, m)
                t_arrive(ref, ss, rs)
                if m == 1:
                    send(ref, ref, tg_ss.at[half, 2], tg_rs.at[half, 3], along(half, 0, sg)[1])
            if m > 0:
                t_spread(half, m)
        if m == 0:
            for half in range(2):
                t_spread(half, 0)

    def t_second(m):
        for half in range(2):
            ref, ss, rs = t_two(half, m, 1)
            t_arrive(ref, ss, rs)
            send(ref, ref, th_ss.at[half, m, 2], th_rs.at[half, m, 3], along(half, 1, sg)[1])

    def t_finish(m):
        for half in range(2):
            for n in (2, 3):
                t_arrive(*t_two(half, m, n))

    for m in range(4):
        t_first(m)
    for m in range(4):
        t_second(m)

    def land(kind, pos):
        slot = k if kind == 0 else 2
        blk = pos_main(pos) if kind == 0 else pos_second(pos)
        for i in range(NS):
            ref = bbuf.at[slot, blk, rows(i)]
            rcopy(ref, ref, bo_ss.at[0, i], b_rs.at[kind, which_of[pos], i], sib).wait_recv()
            if pos == 1:
                to = xp if kind == 0 else xm
                rcopy(ref, ref, bf_ss.at[kind, i], b_rs.at[kind, 1, i], (row, to)).start()
            share(kind, pos, i).start()

    def from_sib(kind, pos):
        slot = 1 - k if kind == 0 else 2
        blk = pos_main(pos) if kind == 0 else pos_second(pos)
        for i in range(NS):
            ref = bbuf.at[slot, blk, rows(i)]
            rcopy(ref, ref, sh_ss.at[kind, pos, i], sh_rs.at[kind, pos, i], sib).wait_recv()

    def land_second(pos):
        @pl.when(is_owner)
        def _():
            land(1, pos)

    def from_owner(pos):
        @pl.when(jnp.logical_not(is_owner))
        def _():
            from_sib(1, pos)

    slot_b, slot_a = owner2, 1 - owner2

    def get_main(owner_gathers, pos):
        gathers = is_owner if owner_gathers else jnp.logical_not(is_owner)

        @pl.when(gathers)
        def _():
            land(0, pos)

        @pl.when(jnp.logical_not(gathers))
        def _():
            from_sib(0, pos)

    def blk_at(pos):
        off = jnp.where(pos == 1, -s, jnp.where(pos == 2, s, jnp.where(pos == 3, 2, 0)))
        return ring(x + off)

    def first_product(slot, pos):
        val = jnp.dot(bbuf[slot, blk_at(pos)], tbuf[...].reshape(V, V), preferred_element_type=F32)
        xbuf[slot, pl.ds(pl.multiple_of(pos * BLK, 64), BLK), :] = val.astype(BF16)

    def first_products(pos):
        @pl.loop(0, 3)
        def _(sl):
            first_product(sl, pos)

    nt = (((1,), (1,)), ((), ()))

    def second_product(pos, lo, width):
        blk = blk_at(pos)
        cols = pl.ds(lo, width)
        val = jnp.dot(ut[pl.ds(pl.multiple_of(blk * BLK, 64), BLK), :], li2[:, cols], preferred_element_type=F32)
        for sl in range(3):
            val += lax.dot_general(bbuf[sl, blk], xbuf[sl, cols, :], nt, preferred_element_type=F32)
        acc[blk, :, :, cols] = val.reshape(4, PIECE, width)

    def ralong(n, phase, off):
        return along(1 - PARTS[n][0], phase, off)

    def cols_of(n):
        return pl.ds(PARTS[n][1], PARTS[n][2])

    def part(n, t, i):
        if PARTS[n][0] == 0:
            return acc[t, i, :, cols_of(n)]
        return acc[i, t, :, cols_of(n)]

    def put(n, t, i, val):
        if PARTS[n][0] == 0:
            acc[t, i, :, cols_of(n)] = val
        else:
            acc[i, t, :, cols_of(n)] = val

    def p1_at(ref, n, m):
        return ref.at[n, m, :, :, pl.ds(0, PARTS[n][2])]

    def p2_at(ref, n, m):
        return ref.at[n, m, :, pl.ds(0, PARTS[n][2])]

    def p2_send(n, m, to):
        send(p2_at(s2, n, m), p2_at(r2, n, m), p2_ss.at[n, m], p2_rs.at[n, m], to)

    def p2_wait(n, m):
        rcopy(p2_at(s2, n, m), p2_at(r2, n, m), p2_ss.at[n, m], p2_rs.at[n, m], sib).wait_recv()

    def got1(n, m, t):
        return r1[n, m, t, :, pl.ds(0, PARTS[n][2])].astype(F32)

    def got2(n, m):
        return r2[n, m, :, pl.ds(0, PARTS[n][2])].astype(F32)

    def width(n):
        return pl.ds(0, PARTS[n][2])

    def row_at(ref, n, m, t):
        return ref.at[n, m, t, :, width(n)]

    def row_copy(n, m, pos, to):
        t = blk_at(pos)
        return rcopy(row_at(s1, n, m, t), row_at(r1, n, m, t), p1_ss.at[n, m, pos], p1_rs.at[n, m, pos], to)

    def send_rows(n, pos):
        t = blk_at(pos)
        s1[n, 0, t, :, width(n)] = part(n, t, ralong(n, 0, 2)[0]).astype(BF16)
        row_copy(n, 0, pos, ralong(n, 0, sg)[1]).start()
        s1[n, 1, t, :, width(n)] = part(n, t, ralong(n, 0, -sg)[0]).astype(BF16)
        row_copy(n, 1, pos, ralong(n, 0, -sg)[1]).start()

    def middle_rows(n, lo, hi):
        nxt, nxt_dev = ralong(n, 0, sg)

        @pl.loop(lo, hi)
        def _(pos):
            t = blk_at(pos)
            row_copy(n, 0, pos, sib).wait_recv()
            s1[n, 2, t, :, width(n)] = (part(n, t, nxt) + r1[n, 0, t, :, width(n)].astype(F32)).astype(BF16)
            row_copy(n, 2, pos, nxt_dev).start()

    def blk_copy(n, m, to):
        return rcopy(p1_at(s1, n, m), p1_at(r1, n, m), p1_ss.at[n, m, 0], p1_rs.at[n, m, 0], to)

    def send_block(n, pos):
        blk = blk_at(pos)
        for m, off, to in ((0, 2, sg), (1, -sg, -sg)):
            @pl.when(blk == ralong(n, 0, off)[0])
            def _():
                for t in range(4):
                    s1[n, m, t, :, width(n)] = acc[blk, t, :, cols_of(n)].astype(BF16)
                blk_copy(n, m, ralong(n, 0, to)[1]).start()

    def p1_middle(n):
        nxt, nxt_dev = ralong(n, 0, sg)
        blk_copy(n, 0, sib).wait_recv()
        for t in range(4):
            s1[n, 2, t, :, width(n)] = (part(n, t, nxt) + got1(n, 0, t)).astype(BF16)
        blk_copy(n, 2, nxt_dev).start()

    def p1_wait(n, m):
        if PARTS[n][0] == 0:
            @pl.loop(0, 4)
            def _(pos):
                row_copy(n, m, pos, sib).wait_recv()
        else:
            blk_copy(n, m, sib).wait_recv()

    def early_product(lo, hi):
        @pl.loop(lo, hi)
        def _(pos):
            second_product(pos, 0, EARLY)
            send_rows(0, pos)
            send_block(1, pos)

    def late_product(lo, hi):
        @pl.loop(lo, hi)
        def _(pos):
            second_product(pos, EARLY, V - EARLY)
            send_rows(2, pos)
            send_block(3, pos)

    def p1_sent(n):
        for m in range(3):
            if PARTS[n][0] == 0:
                @pl.loop(0, 4)
                def _(pos):
                    row_copy(n, m, pos, sib).wait_send()
            else:
                blk_copy(n, m, sib).wait_send()

    def p1_end(n):
        here = ralong(n, 0, 0)[0]
        p1_wait(n, 1)
        p1_wait(n, 2)

        def total(t):
            return part(n, t, here) + got1(n, 1, t) + got1(n, 2, t)

        far = ralong(n, 1, 2)[0]
        back, back_dev = ralong(n, 1, -sg)
        nxt, nxt_dev = ralong(n, 1, sg)
        s2[n, 0, :, pl.ds(0, PARTS[n][2])] = total(far).astype(BF16)
        p2_send(n, 0, nxt_dev)
        s2[n, 1, :, pl.ds(0, PARTS[n][2])] = total(back).astype(BF16)
        p2_send(n, 1, back_dev)
        put(n, nxt, here, total(nxt))
        mid = ralong(n, 1, 0)[0]
        put(n, mid, here, total(mid))

    def p2_middle(n):
        nxt, nxt_dev = ralong(n, 1, sg)
        here = ralong(n, 0, 0)[0]
        p2_wait(n, 0)
        s2[n, 2, :, pl.ds(0, PARTS[n][2])] = (part(n, nxt, here) + got2(n, 0)).astype(BF16)
        p2_send(n, 2, nxt_dev)

    def p2_end(n):
        mid = ralong(n, 1, 0)[0]
        here = ralong(n, 0, 0)[0]
        p2_wait(n, 1)
        p2_wait(n, 2)
        fin[:, cols_of(n)] = part(n, mid, here) + got2(n, 1) + got2(n, 2)
        xx = blk_at(n)
        for kk in range(2):
            gbuf[n, kk] = fin[kk * 40:(kk + 1) * 40, n * BLK:(n + 1) * BLK]
        if n == 0:
            send(gbuf.at[0, 1 - k], hbuf.at[me8], g_ss.at[0, 0], g_rs.at[me8], sib)
            hbuf[me8] = gbuf[0, k]
        else:
            for kk in range(2):
                send(gbuf.at[n, kk], hbuf.at[me8], g_ss.at[n, kk], g_rs.at[me8], dev(y, z, kk, xx))

    land(0, 1)
    land_second(1)
    for m in range(4):
        t_finish(m)
    own_main.wait()

    @pl.when(is_owner)
    def _():
        own_second.wait()

    from_sib(0, 0)
    from_owner(0)
    first_products(0)

    rcopy(l_own, lbuf.at[1], l_ss, l_rs, sib).wait_recv()
    pick_l = jnp.where(k == x // 2, 0, 1)
    u = jnp.dot(lbuf[pick_l, 0:16], tbuf[...].reshape(V, V), preferred_element_type=F32)
    hi = u.astype(BF16).astype(F32)
    ut[...] = jnp.concatenate([hi, u - hi], axis=0).T.astype(BF16)
    li = lbuf[pick_l, 16:32]
    for n in range(4):
        blk = blk_at(n)
        for kk in range(4):
            @pl.when(blk == kk)
            def _():
                li2[0:16, n * BLK:(n + 1) * BLK] = li[:, kk * BLK:(kk + 1) * BLK]
                li2[16:32, n * BLK:(n + 1) * BLK] = li[:, kk * BLK:(kk + 1) * BLK]

    from_sib(0, 1)

    @pl.loop(0, 2)
    def _(i):
        first_product(jnp.where(i == 0, slot_b, slot_a), 1)

    get_main(True, 2)
    first_product(slot_b, 2)
    from_owner(1)
    first_product(2, 2)
    land_second(2)
    from_owner(2)
    first_product(2, 1)
    get_main(False, 2)
    first_product(slot_a, 2)
    early_product(0, 1)
    land_second(3)
    get_main(True, 3)
    from_owner(3)

    @pl.loop(0, 2)
    def _(i):
        first_product(jnp.where(i == 0, 2, slot_b), 3)

    early_product(1, 3)
    get_main(False, 3)
    first_product(slot_a, 3)
    middle_rows(0, 0, 3)
    early_product(3, 4)
    late_product(0, 2)
    middle_rows(0, 3, 4)
    p1_middle(1)
    late_product(2, 4)
    p1_end(0)
    p1_end(1)
    p2_middle(0)
    p2_middle(1)
    middle_rows(2, 0, 4)
    p1_middle(3)
    p2_end(0)
    p2_end(1)
    p1_end(2)
    p1_end(3)
    p2_middle(2)
    p2_middle(3)
    p2_end(2)
    p2_end(3)

    for d in range(1, 8):
        src8 = lax.rem(me8 + d, 8)
        rcopy(gbuf.at[0, 0], hbuf.at[src8], g_ss.at[0, 0], g_rs.at[src8], sib).wait_recv()
    for p in range(4):
        src = (p % 2) * 4 + p // 2
        out[p] = hbuf[src] + hbuf[src + 2]

    for c in pending:
        c.wait_send()
    for n in range(4):
        p1_sent(n)

    def wait_own(kind, pos_list):
        for pos in pos_list:
            for i in range(NS):
                share(kind, pos, i).wait_send()
        for i in range(NS):
            ref = bbuf.at[k if kind == 0 else 2, xm if kind == 0 else xp, rows(i)]
            rcopy(ref, ref, bf_ss.at[kind, i], b_rs.at[kind, 1, i], (row, xp if kind == 0 else xm)).wait_send()

    wait_own(0, (1, 2, 3))

    @pl.when(is_owner)
    def _():
        wait_own(1, (0, 1, 2, 3))


def exchange(*args):
    vmem = pl.BlockSpec(memory_space=pltpu.VMEM)
    anywhere = pl.BlockSpec(memory_space=pl.ANY)
    smem = pl.BlockSpec(memory_space=pltpu.SMEM)
    dma = pltpu.SemaphoreType.DMA
    return pl.pallas_call(
        kernel,
        out_shape=jax.ShapeDtypeStruct((4, 40, BLK), F32),
        in_specs=[anywhere, vmem, anywhere, smem, vmem, vmem],
        out_specs=vmem,
        scratch_shapes=[
            pltpu.VMEM((3, BLK, V), BF16),
            pltpu.VMEM((4, 16, V), BF16),
            pltpu.VMEM((3, 160, V), BF16),
            pltpu.VMEM((32, V), BF16),
            pltpu.VMEM((3, 4, BLK, V), BF16),
            pltpu.VMEM((8, 16, V), BF16),
            pltpu.VMEM((4, 4, PIECE, V), BF16),
            pltpu.VMEM((2, 32, V), BF16),
            pltpu.VMEM((V, 32), BF16),
            pltpu.VMEM((32, V), BF16),
            pltpu.VMEM((3, V, V), BF16),
            pltpu.VMEM((4, 4, PIECE, V), F32),
            pltpu.VMEM((4, 3, 4, PIECE, WIDE), BF16),
            pltpu.VMEM((4, 3, 4, PIECE, WIDE), BF16),
            pltpu.VMEM((4, 3, PIECE, WIDE), BF16),
            pltpu.VMEM((4, 3, PIECE, WIDE), BF16),
            pltpu.VMEM((PIECE, V), F32),
            pltpu.VMEM((4, 2, 40, BLK), F32),
            pltpu.VMEM((8, 40, BLK), F32),
            dma((2,)),
            dma((8,)), dma((8,)),
            dma((2, 4)), dma((2, 4)),
            dma((2, 4, 4)), dma((2, 4, 4)),
            dma, dma,
            dma((2,)),
            dma((3, NS)), dma((2, NS)), dma((2, 3, NS)),
            dma((2, 4, NS)), dma((2, 4, NS)),
            dma((4, 3, 4)), dma((4, 3, 4)), dma((4, 3)), dma((4, 3)),
            dma((4, 2)), dma((8,)),
        ],
        compiler_params=pltpu.CompilerParams(
            collective_id=0, has_side_effects=True, vmem_limit_bytes=62 * 1024 * 1024
        ),
    )(*args)


def local(
    amplitudes, integrals, occupied_integrals, pair_orbitals, amplitude_tiles, integral_tiles
):
    res = exchange(
        integrals,
        jnp.swapaxes(amplitudes, 0, 1),
        occupied_integrals,
        pair_orbitals.T,
        jnp.swapaxes(amplitude_tiles, 0, 1).reshape(80, 20),
        integral_tiles,
    )
    return jnp.swapaxes(res, 1, 2)


def solution(mesh):
    placed = (
        P(None, ("row", "col"), None),
        P("row", "col", None),
        P("row", None, None),
        P(),
        P(),
        P(),
    )
    return jax.shard_map(
        local, mesh=mesh, in_specs=placed, out_specs=P(None, "col", "row"), check_vma=False
    )
```

```python
import jax
import jax.numpy as jnp
from jax import lax
from jax.experimental import pallas as pl
from jax.experimental.pallas import tpu as pltpu
from jax.sharding import PartitionSpec as P

MESH = pl.DeviceIdType.MESH
TILE = 64
V = 1280
VT = 20
BLK = 320
PIECE = 80
HALF = 640
EARLY = 768
WIDE = 384
PARTS = ((0, 0, WIDE), (1, WIDE, WIDE), (1, EARLY, WIDE), (0, EARLY + WIDE, 128))
OWN, XM, XP, XO = range(4)
LAID = (
    ((0, 0, 320),),
    ((640, 0, 128), (1088, 128, 192)),
    ((320, 0, 320),),
    ((768, 0, 320),),
)
NS = 2
SUB = BLK // NS
F32 = jnp.float32
BF16 = jnp.bfloat16


def kernel(
    b_in, t_in, occ_in, pairs, a_tiles, i_tiles, out,
    b_own, t_own, occ, l_own,
    bbuf, tst, tbuf, lbuf, ut, li2, xbuf, acc,
    s1, r1, s2, r2, fin, gbuf, hbuf,
    in_ls, t1_ss, t1_rs, tg_ss, tg_rs, th_ss, th_rs, l_ss, l_rs, own_ls,
    bo_ss, bf_ss, b_rs, sh_ss, sh_rs, p1_ss, p1_rs, p2_ss, p2_rs, g_ss, g_rs,
):
    x = lax.axis_index("col")
    row = lax.axis_index("row")
    k = lax.rem(row, 2)
    yz = row // 2
    y = yz // 4
    z = lax.rem(yz, 4)
    s = 1 - 2 * lax.rem(x, 2)
    xp = lax.rem(x + s + 4, 4)
    xm = lax.rem(x - s + 4, 4)
    xo = lax.rem(x + 2, 4)
    sg = 1 - 2 * k
    me8 = k * 4 + x
    pair = 2 * lax.rem(x, 2) + k
    sib = (yz * 2 + 1 - k, x)
    owner2 = lax.rem((x + 1) // 2 + 1, 2)
    is_owner = k == owner2
    main_j = x // 2

    def dev(yy, zz, kk, xx):
        return ((yy * 4 + zz) * 2 + kk, xx)

    def ring(v):
        return lax.rem(v + 8, 4)

    def peer8(d):
        idx = lax.rem(me8 + d, 8)
        return idx, idx // 4, lax.rem(idx, 4)

    def rcopy(src, dst, ss, rs, to):
        return pltpu.make_async_remote_copy(
            src_ref=src, dst_ref=dst, send_sem=ss, recv_sem=rs, device_id=to, device_id_type=MESH
        )

    pending = []

    def send(src, dst, ss, rs, to):
        c = rcopy(src, dst, ss, rs, to)
        c.start()
        pending.append(c)
        return c

    load_b = pltpu.make_async_copy(b_in, b_own, in_ls.at[0])
    load_b.start()
    load_occ = pltpu.make_async_copy(occ_in, occ, in_ls.at[1])
    load_occ.start()

    barrier = pltpu.get_barrier_semaphore()
    for d in range(1, 8):
        _, kk, xx = peer8(d)
        pl.semaphore_signal(barrier, inc=1, device_id=dev(y, z, kk, xx), device_id_type=MESH)
    for step in (1, -1):
        pl.semaphore_signal(barrier, inc=1, device_id=dev(ring(y + step), z, k, x), device_id_type=MESH)
        pl.semaphore_signal(barrier, inc=1, device_id=dev(y, ring(z + step), k, x), device_id_type=MESH)

    def iota(shape, dim):
        return lax.broadcasted_iota(jnp.int32, shape, dim)

    def ones(cond):
        return jnp.where(cond, 1.0, 0.0).astype(BF16)

    spread = ones(iota((VT, V), 0) == jnp.right_shift(iota((VT, V), 1), 6))
    tile_row = jnp.right_shift(jnp.right_shift(iota((40, 80), 0), 2) + (row * 4 + x) * 10, 6)
    same_pair = jnp.bitwise_and(iota((40, 80), 0), 3) == jnp.bitwise_and(iota((40, 80), 1), 3)
    pick_t = ones(same_pair & (jnp.right_shift(iota((40, 80), 1), 2) == tile_row))
    small = jnp.dot(pick_t, a_tiles[...].astype(F32).astype(BF16), preferred_element_type=F32).astype(BF16)
    mask = jnp.dot(small, spread, preferred_element_type=F32)
    raw = jnp.concatenate([t_in[i].astype(F32) for i in range(10)], axis=0)
    turn_i = jnp.bitwise_and(iota((64, 40), 0), 15)
    turn = ones((turn_i < 10) & (iota((64, 40), 1) == turn_i * 4 + jnp.right_shift(iota((64, 40), 0), 4)))
    turned = jnp.dot(turn, (raw * mask).astype(BF16), preferred_element_type=F32).astype(BF16)
    for p in range(4):
        t_own[p] = turned[p * 16:(p + 1) * 16]
    pick_b = ones(iota((16, VT), 0) + 5 * x == iota((16, VT), 1))
    small = jnp.dot(pick_b, i_tiles[...].astype(F32).astype(BF16), preferred_element_type=F32).astype(BF16)
    mask = jnp.dot(small, spread, preferred_element_type=F32)
    load_b.wait()
    for t in range(BLK // TILE):
        wide = jnp.broadcast_to(mask[t:t + 1], (TILE, V)).astype(BF16)
        for j in range(3):
            b_own[j, t * TILE:(t + 1) * TILE] = b_own[j, t * TILE:(t + 1) * TILE] * wide
    pl.semaphore_wait(barrier, 11)

    for d in range(1, 8):
        idx, kk, xx = peer8(d)
        send(t_own.at[2 * lax.rem(xx, 2) + kk], tst.at[me8], t1_ss.at[d], t1_rs.at[d], dev(y, z, kk, xx))
    dest2 = jnp.where(is_owner, xm, xp)
    which2 = jnp.where(is_owner, 0, 2)

    def rows(i):
        return pl.ds(i * SUB, SUB)

    for i in range(NS):
        send(b_own.at[1 - main_j, rows(i)], bbuf.at[k, x, rows(i)], bo_ss.at[1, i], b_rs.at[0, 2, i],
             (row, xm))
    for i in range(NS):
        send(b_own.at[2, rows(i)], bbuf.at[2, x, rows(i)], bo_ss.at[2, i], b_rs.at[1, which2, i],
             (row, dest2))
    for i in range(NS):
        send(b_own.at[main_j, rows(i)], bbuf.at[k, x, rows(i)], bo_ss.at[0, i], b_rs.at[0, 0, i],
             (row, xp))

    def share(kind, pos, i, src=None):
        slot, blk = (k, None) if kind == 0 else (2, None)
        blk = (x, pos_main(pos) if kind == 0 else pos_second(pos))[pos > 0]
        dst = bbuf.at[slot, blk, rows(i)]
        return rcopy(dst if src is None else src, dst, sh_ss.at[kind, pos, i], sh_rs.at[kind, pos, i], sib)

    def pos_main(pos):
        return (x, xm, xp, xo)[pos]

    def pos_second(pos):
        return (x, xp, xm, xo)[pos]

    which_of = (None, 2, 0, 1)

    for i in range(NS):
        c = share(0, 0, i, b_own.at[main_j, rows(i)])
        c.start()
        pending.append(c)

    @pl.when(is_owner)
    def _():
        for i in range(NS):
            share(1, 0, i, b_own.at[2, rows(i)]).start()

    own_main = pltpu.make_async_copy(b_own.at[main_j], bbuf.at[k, x], own_ls.at[0])
    own_main.start()
    own_second = pltpu.make_async_copy(b_own.at[2], bbuf.at[2, x], own_ls.at[1])

    @pl.when(is_owner)
    def _():
        own_second.start()

    load_occ.wait()
    other = 2 * lax.rem(x, 2) + 1 - k
    orb_row, orb_col = iota((32, 480), 0), iota((32, 480), 1)

    def occ_rows(p):
        aux = jnp.bitwise_and(orb_row, 15)
        orb = jnp.where(orb_row < 16, pairs[1, p], pairs[0, p])
        hot = ones((orb_col == aux * 160 + orb) & (aux < 3))
        return jnp.dot(hot, occ[...].reshape(480, V), preferred_element_type=F32).astype(BF16)

    l_own[...] = occ_rows(other)
    lbuf[0] = occ_rows(pair)
    send(l_own, lbuf.at[1], l_ss, l_rs, sib)

    tst[me8] = t_own[pair]
    ri, ci = iota((PIECE, 128), 0), iota((PIECE, 128), 1)
    within = jnp.bitwise_and(ci, 15)
    pick = ones((within < 10) & (ri == jnp.right_shift(ci, 4) * 10 + within))
    for d in range(1, 8):
        src8 = lax.rem(me8 + 8 - d, 8)
        rcopy(t_own.at[0], tst.at[src8], t1_ss.at[d], t1_rs.at[d], sib).wait_recv()
    piece = jnp.dot(pick, tst[...].reshape(128, V), preferred_element_type=F32)
    tbuf[y, z] = piece.astype(BF16)

    col_h = (pl.ds(0, HALF), pl.ds(HALF, HALF))

    def along(half, phase, off):
        if (half == 0) == (phase == 0):
            return ring(y + off), dev(ring(y + off), z, k, x)
        return ring(z + off), dev(y, ring(z + off), k, x)

    def t_at(half, first, second):
        if half == 0:
            return tbuf.at[ring(y + first), ring(z + second), :, col_h[0]]
        return tbuf.at[ring(y + second), ring(z + first), :, col_h[1]]

    offs = (0, -sg, sg, 2)

    def t_one(half, n):
        ref = t_at(half, offs[n], 0)
        return ref, tg_ss.at[half, n], tg_rs.at[half, n]

    def t_two(half, m, n):
        ref = t_at(half, offs[m], offs[n])
        return ref, th_ss.at[half, m, n], th_rs.at[half, m, n]

    def t_spread(half, m):
        ref = t_at(half, offs[m], 0)
        send(ref, ref, th_ss.at[half, m, 0], th_rs.at[half, m, 1], along(half, 1, sg)[1])
        send(ref, ref, th_ss.at[half, m, 1], th_rs.at[half, m, 2], along(half, 1, -sg)[1])

    def t_arrive(ref, ss, rs):
        rcopy(ref, ref, ss, rs, sib).wait_recv()

    def t_first(m):
        for half in range(2):
            if m == 0:
                ref = t_at(half, 0, 0)
                send(ref, ref, tg_ss.at[half, 0], tg_rs.at[half, 1], along(half, 0, sg)[1])
                send(ref, ref, tg_ss.at[half, 1], tg_rs.at[half, 2], along(half, 0, -sg)[1])
            else:
                ref, ss, rs = t_one(half, m)
                t_arrive(ref, ss, rs)
                if m == 1:
                    send(ref, ref, tg_ss.at[half, 2], tg_rs.at[half, 3], along(half, 0, sg)[1])
            if m > 0:
                t_spread(half, m)
        if m == 0:
            for half in range(2):
                t_spread(half, 0)

    def t_second(m):
        for half in range(2):
            ref, ss, rs = t_two(half, m, 1)
            t_arrive(ref, ss, rs)
            send(ref, ref, th_ss.at[half, m, 2], th_rs.at[half, m, 3], along(half, 1, sg)[1])

    def t_finish(m):
        for half in range(2):
            for n in (2, 3):
                t_arrive(*t_two(half, m, n))

    for m in range(4):
        t_first(m)
    for m in range(4):
        t_second(m)

    def land(kind, pos):
        slot = k if kind == 0 else 2
        blk = pos_main(pos) if kind == 0 else pos_second(pos)
        for i in range(NS):
            ref = bbuf.at[slot, blk, rows(i)]
            rcopy(ref, ref, bo_ss.at[0, i], b_rs.at[kind, which_of[pos], i], sib).wait_recv()
            if pos == 1:
                to = xp if kind == 0 else xm
                rcopy(ref, ref, bf_ss.at[kind, i], b_rs.at[kind, 1, i], (row, to)).start()
            share(kind, pos, i).start()

    def from_sib(kind, pos):
        slot = 1 - k if kind == 0 else 2
        blk = pos_main(pos) if kind == 0 else pos_second(pos)
        for i in range(NS):
            ref = bbuf.at[slot, blk, rows(i)]
            rcopy(ref, ref, sh_ss.at[kind, pos, i], sh_rs.at[kind, pos, i], sib).wait_recv()

    def land_second(pos):
        @pl.when(is_owner)
        def _():
            land(1, pos)

    def from_owner(pos):
        @pl.when(jnp.logical_not(is_owner))
        def _():
            from_sib(1, pos)

    slot_b, slot_a = owner2, 1 - owner2

    def get_main(owner_gathers, pos):
        gathers = is_owner if owner_gathers else jnp.logical_not(is_owner)

        @pl.when(gathers)
        def _():
            land(0, pos)

        @pl.when(jnp.logical_not(gathers))
        def _():
            from_sib(0, pos)

    def blk_at(pos):
        off = jnp.where(pos == 1, -s, jnp.where(pos == 2, s, jnp.where(pos == 3, 2, 0)))
        return ring(x + off)

    def first_product(slot, pos):
        val = jnp.dot(bbuf[slot, blk_at(pos)], tbuf[...].reshape(V, V), preferred_element_type=F32)
        for col, r, m in LAID[pos]:
            xbuf[slot, col:col + m, :] = val[r:r + m].astype(BF16)

    def first_products(pos):
        @pl.loop(0, 3)
        def _(sl):
            first_product(sl, pos)

    nt = (((1,), (1,)), ((), ()))

    def second_product(blk, lo, width):
        cols = pl.ds(lo, width)
        val = jnp.dot(ut[pl.ds(pl.multiple_of(blk * BLK, 64), BLK), :], li2[:, cols], preferred_element_type=F32)
        for sl in range(3):
            val += lax.dot_general(bbuf[sl, blk], xbuf[sl, cols, :], nt, preferred_element_type=F32)
        acc[blk, :, :, cols] = val.reshape(4, PIECE, width)

    def ralong(n, phase, off):
        return along(1 - PARTS[n][0], phase, off)

    def cols_of(n):
        return pl.ds(PARTS[n][1], PARTS[n][2])

    def part(n, t, i):
        if PARTS[n][0] == 0:
            return acc[t, i, :, cols_of(n)]
        return acc[i, t, :, cols_of(n)]

    def put(n, t, i, val):
        if PARTS[n][0] == 0:
            acc[t, i, :, cols_of(n)] = val
        else:
            acc[i, t, :, cols_of(n)] = val

    def p1_at(ref, n, m):
        return ref.at[n, m, :, :, pl.ds(0, PARTS[n][2])]

    def p2_at(ref, n, m):
        return ref.at[n, m, :, pl.ds(0, PARTS[n][2])]

    def p2_send(n, m, to):
        send(p2_at(s2, n, m), p2_at(r2, n, m), p2_ss.at[n, m], p2_rs.at[n, m], to)

    def p2_wait(n, m):
        rcopy(p2_at(s2, n, m), p2_at(r2, n, m), p2_ss.at[n, m], p2_rs.at[n, m], sib).wait_recv()

    def got1(n, m, t):
        return r1[n, m, t, :, pl.ds(0, PARTS[n][2])].astype(F32)

    def got2(n, m):
        return r2[n, m, :, pl.ds(0, PARTS[n][2])].astype(F32)

    def width(n):
        return pl.ds(0, PARTS[n][2])

    def row_at(ref, n, m, t):
        return ref.at[n, m, t, :, width(n)]

    def row_copy(n, m, t, to):
        return rcopy(row_at(s1, n, m, t), row_at(r1, n, m, t), p1_ss.at[n, m, t], p1_rs.at[n, m, t], to)

    def send_rows(n, t):
        s1[n, 0, t, :, width(n)] = part(n, t, ralong(n, 0, 2)[0]).astype(BF16)
        row_copy(n, 0, t, ralong(n, 0, sg)[1]).start()
        s1[n, 1, t, :, width(n)] = part(n, t, ralong(n, 0, -sg)[0]).astype(BF16)
        row_copy(n, 1, t, ralong(n, 0, -sg)[1]).start()

    def middle_rows(n, lo, hi, order):
        nxt, nxt_dev = ralong(n, 0, sg)

        @pl.loop(lo, hi)
        def _(pos):
            t = order(pos)
            row_copy(n, 0, t, sib).wait_recv()
            s1[n, 2, t, :, width(n)] = (part(n, t, nxt) + r1[n, 0, t, :, width(n)].astype(F32)).astype(BF16)
            row_copy(n, 2, t, nxt_dev).start()

    def blk_copy(n, m, to):
        return rcopy(p1_at(s1, n, m), p1_at(r1, n, m), p1_ss.at[n, m, 0], p1_rs.at[n, m, 0], to)

    def send_block(n, blk):
        for m, off, to in ((0, 2, sg), (1, -sg, -sg)):
            @pl.when(blk == ralong(n, 0, off)[0])
            def _():
                for t in range(4):
                    s1[n, m, t, :, width(n)] = acc[blk, t, :, cols_of(n)].astype(BF16)
                blk_copy(n, m, ralong(n, 0, to)[1]).start()

    def p1_middle(n):
        nxt, nxt_dev = ralong(n, 0, sg)
        blk_copy(n, 0, sib).wait_recv()
        for t in range(4):
            s1[n, 2, t, :, width(n)] = (part(n, t, nxt) + got1(n, 0, t)).astype(BF16)
        blk_copy(n, 2, nxt_dev).start()

    def p1_wait(n, m):
        if PARTS[n][0] == 0:
            @pl.loop(0, 4)
            def _(pos):
                row_copy(n, m, pos, sib).wait_recv()
        else:
            blk_copy(n, m, sib).wait_recv()

    def early_product(lo, hi):
        @pl.loop(lo, hi)
        def _(pos):
            blk = blk_at(pos)
            second_product(blk, 0, EARLY)
            send_rows(0, blk)
            send_block(1, blk)

    def y_order(pos):
        return ring(y + jnp.where(pos == 0, 2, jnp.where(pos == 1, -sg, jnp.where(pos == 2, sg, 0))))

    def late_product(lo, hi):
        @pl.loop(lo, hi)
        def _(pos):
            blk = y_order(pos)
            second_product(blk, EARLY, V - EARLY)
            send_rows(3, blk)
            send_block(2, blk)

    def p1_sent(n):
        for m in range(3):
            if PARTS[n][0] == 0:
                @pl.loop(0, 4)
                def _(pos):
                    row_copy(n, m, pos, sib).wait_send()
            else:
                blk_copy(n, m, sib).wait_send()

    def p1_end(n):
        here = ralong(n, 0, 0)[0]
        p1_wait(n, 1)
        p1_wait(n, 2)

        def total(t):
            return part(n, t, here) + got1(n, 1, t) + got1(n, 2, t)

        far = ralong(n, 1, 2)[0]
        back, back_dev = ralong(n, 1, -sg)
        nxt, nxt_dev = ralong(n, 1, sg)
        s2[n, 0, :, pl.ds(0, PARTS[n][2])] = total(far).astype(BF16)
        p2_send(n, 0, nxt_dev)
        s2[n, 1, :, pl.ds(0, PARTS[n][2])] = total(back).astype(BF16)
        p2_send(n, 1, back_dev)
        put(n, nxt, here, total(nxt))
        mid = ralong(n, 1, 0)[0]
        put(n, mid, here, total(mid))

    def p2_middle(n):
        nxt, nxt_dev = ralong(n, 1, sg)
        here = ralong(n, 0, 0)[0]
        p2_wait(n, 0)
        s2[n, 2, :, pl.ds(0, PARTS[n][2])] = (part(n, nxt, here) + got2(n, 0)).astype(BF16)
        p2_send(n, 2, nxt_dev)

    def p2_end(n):
        mid = ralong(n, 1, 0)[0]
        here = ralong(n, 0, 0)[0]
        p2_wait(n, 1)
        p2_wait(n, 2)
        fin[:, cols_of(n)] = part(n, mid, here) + got2(n, 1) + got2(n, 2)
        place = (OWN, XP, XO, XM)[n]
        xx = blk_at(place)
        for kk in range(2):
            for col, r, m in LAID[place]:
                gbuf[n, kk, :, r:r + m] = fin[kk * 40:(kk + 1) * 40, col:col + m]
        if n == 0:
            send(gbuf.at[0, 1 - k], hbuf.at[me8], g_ss.at[0, 0], g_rs.at[me8], sib)
            hbuf[me8] = gbuf[0, k]
        else:
            for kk in range(2):
                send(gbuf.at[n, kk], hbuf.at[me8], g_ss.at[n, kk], g_rs.at[me8], dev(y, z, kk, xx))

    land(0, 1)
    land_second(1)
    for m in range(4):
        t_finish(m)
    own_main.wait()

    @pl.when(is_owner)
    def _():
        own_second.wait()

    from_sib(0, 0)
    from_owner(0)
    first_products(0)

    rcopy(l_own, lbuf.at[1], l_ss, l_rs, sib).wait_recv()
    pick_l = jnp.where(k == x // 2, 0, 1)
    u = jnp.dot(lbuf[pick_l, 0:16], tbuf[...].reshape(V, V), preferred_element_type=F32)
    hi = u.astype(BF16).astype(F32)
    ut[...] = jnp.concatenate([hi, u - hi], axis=0).T.astype(BF16)
    li = lbuf[pick_l, 16:32]
    for n in range(4):
        blk = blk_at(n)
        for kk in range(4):
            @pl.when(blk == kk)
            def _():
                for col, r, m in LAID[n]:
                    li2[0:16, col:col + m] = li[:, kk * BLK + r:kk * BLK + r + m]
                    li2[16:32, col:col + m] = li[:, kk * BLK + r:kk * BLK + r + m]

    from_sib(0, 1)

    @pl.loop(0, 2)
    def _(i):
        first_product(jnp.where(i == 0, slot_b, slot_a), 1)

    get_main(False, 2)
    first_product(slot_a, 2)
    from_owner(1)
    first_product(2, 2)
    land_second(2)
    from_owner(2)
    first_product(2, 1)
    get_main(True, 2)
    first_product(slot_b, 2)
    land_second(3)
    get_main(False, 3)
    from_owner(3)

    @pl.loop(0, 2)
    def _(i):
        first_product(jnp.where(i == 0, 2, slot_a), 3)

    early_product(0, 2)

    @pl.when(is_owner)
    def _():
        land(0, 3)

    early_product(2, 3)

    @pl.when(jnp.logical_not(is_owner))
    def _():
        from_sib(0, 3)

    first_product(slot_b, 3)
    early_product(3, 4)
    middle_rows(0, 0, 3, blk_at)
    late_product(0, 1)
    p1_middle(1)
    middle_rows(0, 3, 4, blk_at)
    late_product(1, 3)
    p1_middle(2)
    middle_rows(3, 0, 1, y_order)
    late_product(3, 4)
    p1_end(0)
    middle_rows(3, 1, 3, y_order)
    p1_end(1)
    middle_rows(3, 3, 4, y_order)
    p2_middle(0)
    p1_end(2)
    p2_middle(1)
    p1_end(3)
    p2_end(0)
    p2_middle(2)
    p2_end(1)
    p2_middle(3)
    p2_end(2)
    p2_end(3)

    for d in range(1, 8):
        src8 = lax.rem(me8 + d, 8)
        rcopy(gbuf.at[0, 0], hbuf.at[src8], g_ss.at[0, 0], g_rs.at[src8], sib).wait_recv()
    for p in range(4):
        src = (p % 2) * 4 + p // 2
        out[p] = hbuf[src] + hbuf[src + 2]

    for c in pending:
        c.wait_send()
    for n in range(4):
        p1_sent(n)

    def wait_own(kind, pos_list):
        for pos in pos_list:
            for i in range(NS):
                share(kind, pos, i).wait_send()
        for i in range(NS):
            ref = bbuf.at[k if kind == 0 else 2, xm if kind == 0 else xp, rows(i)]
            rcopy(ref, ref, bf_ss.at[kind, i], b_rs.at[kind, 1, i], (row, xp if kind == 0 else xm)).wait_send()

    wait_own(0, (1, 2, 3))

    @pl.when(is_owner)
    def _():
        wait_own(1, (0, 1, 2, 3))


def exchange(*args):
    vmem = pl.BlockSpec(memory_space=pltpu.VMEM)
    anywhere = pl.BlockSpec(memory_space=pl.ANY)
    smem = pl.BlockSpec(memory_space=pltpu.SMEM)
    dma = pltpu.SemaphoreType.DMA
    return pl.pallas_call(
        kernel,
        out_shape=jax.ShapeDtypeStruct((4, 40, BLK), F32),
        in_specs=[anywhere, vmem, anywhere, smem, vmem, vmem],
        out_specs=vmem,
        scratch_shapes=[
            pltpu.VMEM((3, BLK, V), BF16),
            pltpu.VMEM((4, 16, V), BF16),
            pltpu.VMEM((3, 160, V), BF16),
            pltpu.VMEM((32, V), BF16),
            pltpu.VMEM((3, 4, BLK, V), BF16),
            pltpu.VMEM((8, 16, V), BF16),
            pltpu.VMEM((4, 4, PIECE, V), BF16),
            pltpu.VMEM((2, 32, V), BF16),
            pltpu.VMEM((V, 32), BF16),
            pltpu.VMEM((32, V), BF16),
            pltpu.VMEM((3, V, V), BF16),
            pltpu.VMEM((4, 4, PIECE, V), F32),
            pltpu.VMEM((4, 3, 4, PIECE, WIDE), BF16),
            pltpu.VMEM((4, 3, 4, PIECE, WIDE), BF16),
            pltpu.VMEM((4, 3, PIECE, WIDE), BF16),
            pltpu.VMEM((4, 3, PIECE, WIDE), BF16),
            pltpu.VMEM((PIECE, V), F32),
            pltpu.VMEM((4, 2, 40, BLK), F32),
            pltpu.VMEM((8, 40, BLK), F32),
            dma((2,)),
            dma((8,)), dma((8,)),
            dma((2, 4)), dma((2, 4)),
            dma((2, 4, 4)), dma((2, 4, 4)),
            dma, dma,
            dma((2,)),
            dma((3, NS)), dma((2, NS)), dma((2, 3, NS)),
            dma((2, 4, NS)), dma((2, 4, NS)),
            dma((4, 3, 4)), dma((4, 3, 4)), dma((4, 3)), dma((4, 3)),
            dma((4, 2)), dma((8,)),
        ],
        compiler_params=pltpu.CompilerParams(
            collective_id=0, has_side_effects=True, vmem_limit_bytes=62 * 1024 * 1024
        ),
    )(*args)


def local(
    amplitudes, integrals, occupied_integrals, pair_orbitals, amplitude_tiles, integral_tiles
):
    res = exchange(
        integrals,
        jnp.swapaxes(amplitudes, 0, 1),
        occupied_integrals,
        pair_orbitals.T,
        jnp.swapaxes(amplitude_tiles, 0, 1).reshape(80, 20),
        integral_tiles,
    )
    return jnp.swapaxes(res, 1, 2)


def solution(mesh):
    placed = (
        P(None, ("row", "col"), None),
        P("row", "col", None),
        P("row", None, None),
        P(),
        P(),
        P(),
    )
    return jax.shard_map(
        local, mesh=mesh, in_specs=placed, out_specs=P(None, "col", "row"), check_vma=False
    )
```

```python
import jax
import jax.numpy as jnp
from jax import lax
from jax.experimental import pallas as pl
from jax.experimental.pallas import tpu as pltpu
from jax.sharding import PartitionSpec as P

MESH = pl.DeviceIdType.MESH
TILE = 64
V = 1280
VT = 20
BLK = 320
PIECE = 80
HALF = 640
EARLY = 768
WIDE = 384
PARTS = ((0, 0, WIDE), (1, WIDE, WIDE), (1, EARLY, 256), (0, EARLY + 256, 256))
OWN, XM, XP, XO = range(4)
LAID = (
    ((640, 0, 128), (1088, 128, 192)),
    ((0, 0, 320),),
    ((320, 0, 320),),
    ((768, 0, 320),),
)
NS = 2
SUB = BLK // NS
F32 = jnp.float32
BF16 = jnp.bfloat16


def kernel(
    b_in, t_in, occ_in, pairs, a_tiles, i_tiles, out,
    b_own, t_own, occ, l_own,
    bbuf, tst, tbuf, lbuf, ut, li2, xbuf, acc,
    s1, r1, s2, r2, fin, gbuf, hbuf,
    in_ls, t1_ss, t1_rs, tg_ss, tg_rs, th_ss, th_rs, l_ss, l_rs, own_ls,
    bo_ss, bf_ss, b_rs, sh_ss, sh_rs, p1_ss, p1_rs, p2_ss, p2_rs, g_ss, g_rs,
):
    x = lax.axis_index("col")
    row = lax.axis_index("row")
    k = lax.rem(row, 2)
    yz = row // 2
    y = yz // 4
    z = lax.rem(yz, 4)
    s = 1 - 2 * lax.rem(x, 2)
    xp = lax.rem(x + s + 4, 4)
    xm = lax.rem(x - s + 4, 4)
    xo = lax.rem(x + 2, 4)
    sg = 1 - 2 * k
    me8 = k * 4 + x
    pair = 2 * lax.rem(x, 2) + k
    sib = (yz * 2 + 1 - k, x)
    owner2 = lax.rem((x + 1) // 2 + 1, 2)
    is_owner = k == owner2
    main_j = x // 2

    def dev(yy, zz, kk, xx):
        return ((yy * 4 + zz) * 2 + kk, xx)

    def ring(v):
        return lax.rem(v + 8, 4)

    def peer8(d):
        idx = lax.rem(me8 + d, 8)
        return idx, idx // 4, lax.rem(idx, 4)

    def rcopy(src, dst, ss, rs, to):
        return pltpu.make_async_remote_copy(
            src_ref=src, dst_ref=dst, send_sem=ss, recv_sem=rs, device_id=to, device_id_type=MESH
        )

    pending = []

    def send(src, dst, ss, rs, to):
        c = rcopy(src, dst, ss, rs, to)
        c.start()
        pending.append(c)
        return c

    load_b = pltpu.make_async_copy(b_in, b_own, in_ls.at[0])
    load_b.start()
    load_occ = pltpu.make_async_copy(occ_in, occ, in_ls.at[1])
    load_occ.start()

    barrier = pltpu.get_barrier_semaphore()
    for d in range(1, 8):
        _, kk, xx = peer8(d)
        pl.semaphore_signal(barrier, inc=1, device_id=dev(y, z, kk, xx), device_id_type=MESH)
    for step in (1, 2, -1):
        pl.semaphore_signal(barrier, inc=1, device_id=dev(ring(y + step), z, k, x), device_id_type=MESH)
        pl.semaphore_signal(barrier, inc=1, device_id=dev(y, ring(z + step), k, x), device_id_type=MESH)

    def iota(shape, dim):
        return lax.broadcasted_iota(jnp.int32, shape, dim)

    def ones(cond):
        return jnp.where(cond, 1.0, 0.0).astype(BF16)

    spread = ones(iota((VT, V), 0) == jnp.right_shift(iota((VT, V), 1), 6))
    tile_row = jnp.right_shift(jnp.right_shift(iota((40, 80), 0), 2) + (row * 4 + x) * 10, 6)
    same_pair = jnp.bitwise_and(iota((40, 80), 0), 3) == jnp.bitwise_and(iota((40, 80), 1), 3)
    pick_t = ones(same_pair & (jnp.right_shift(iota((40, 80), 1), 2) == tile_row))
    small = jnp.dot(pick_t, a_tiles[...].astype(F32).astype(BF16), preferred_element_type=F32).astype(BF16)
    mask = jnp.dot(small, spread, preferred_element_type=F32)
    raw = jnp.concatenate([t_in[i].astype(F32) for i in range(10)], axis=0)
    turn_i = jnp.bitwise_and(iota((64, 40), 0), 15)
    turn = ones((turn_i < 10) & (iota((64, 40), 1) == turn_i * 4 + jnp.right_shift(iota((64, 40), 0), 4)))
    turned = jnp.dot(turn, (raw * mask).astype(BF16), preferred_element_type=F32).astype(BF16)
    for p in range(4):
        t_own[p] = turned[p * 16:(p + 1) * 16]
    pick_b = ones(iota((16, VT), 0) + 5 * x == iota((16, VT), 1))
    small = jnp.dot(pick_b, i_tiles[...].astype(F32).astype(BF16), preferred_element_type=F32).astype(BF16)
    mask = jnp.dot(small, spread, preferred_element_type=F32)
    load_b.wait()
    for t in range(BLK // TILE):
        wide = jnp.broadcast_to(mask[t:t + 1], (TILE, V)).astype(BF16)
        for j in range(3):
            b_own[j, t * TILE:(t + 1) * TILE] = b_own[j, t * TILE:(t + 1) * TILE] * wide
    pl.semaphore_wait(barrier, 13)

    for d in range(1, 8):
        idx, kk, xx = peer8(d)
        send(t_own.at[2 * lax.rem(xx, 2) + kk], tst.at[me8], t1_ss.at[d], t1_rs.at[d], dev(y, z, kk, xx))
    dest2 = jnp.where(is_owner, xm, xp)
    which2 = jnp.where(is_owner, 0, 2)

    def rows(i):
        return pl.ds(i * SUB, SUB)

    for i in range(NS):
        send(b_own.at[1 - main_j, rows(i)], bbuf.at[k, x, rows(i)], bo_ss.at[1, i], b_rs.at[0, 2, i],
             (row, xm))
    for i in range(NS):
        send(b_own.at[2, rows(i)], bbuf.at[2, x, rows(i)], bo_ss.at[2, i], b_rs.at[1, which2, i],
             (row, dest2))
    for i in range(NS):
        send(b_own.at[main_j, rows(i)], bbuf.at[k, x, rows(i)], bo_ss.at[0, i], b_rs.at[0, 0, i],
             (row, xp))

    def share(kind, pos, i, src=None):
        slot, blk = (k, None) if kind == 0 else (2, None)
        blk = (x, pos_main(pos) if kind == 0 else pos_second(pos))[pos > 0]
        dst = bbuf.at[slot, blk, rows(i)]
        return rcopy(dst if src is None else src, dst, sh_ss.at[kind, pos, i], sh_rs.at[kind, pos, i], sib)

    def pos_main(pos):
        return (x, xm, xp, xo)[pos]

    def pos_second(pos):
        return (x, xp, xm, xo)[pos]

    which_of = (None, 2, 0, 1)

    for i in range(NS):
        c = share(0, 0, i, b_own.at[main_j, rows(i)])
        c.start()
        pending.append(c)

    @pl.when(is_owner)
    def _():
        for i in range(NS):
            share(1, 0, i, b_own.at[2, rows(i)]).start()

    own_main = pltpu.make_async_copy(b_own.at[main_j], bbuf.at[k, x], own_ls.at[0])
    own_main.start()
    own_second = pltpu.make_async_copy(b_own.at[2], bbuf.at[2, x], own_ls.at[1])

    @pl.when(is_owner)
    def _():
        own_second.start()

    load_occ.wait()
    other = 2 * lax.rem(x, 2) + 1 - k
    orb_row, orb_col = iota((32, 480), 0), iota((32, 480), 1)

    def occ_rows(p):
        aux = jnp.bitwise_and(orb_row, 15)
        orb = jnp.where(orb_row < 16, pairs[1, p], pairs[0, p])
        hot = ones((orb_col == aux * 160 + orb) & (aux < 3))
        return jnp.dot(hot, occ[...].reshape(480, V), preferred_element_type=F32).astype(BF16)

    l_own[...] = occ_rows(other)
    lbuf[0] = occ_rows(pair)
    send(l_own, lbuf.at[1], l_ss, l_rs, sib)

    tst[me8] = t_own[pair]
    ri, ci = iota((PIECE, 128), 0), iota((PIECE, 128), 1)
    within = jnp.bitwise_and(ci, 15)
    pick = ones((within < 10) & (ri == jnp.right_shift(ci, 4) * 10 + within))
    for d in range(1, 8):
        src8 = lax.rem(me8 + 8 - d, 8)
        rcopy(t_own.at[0], tst.at[src8], t1_ss.at[d], t1_rs.at[d], sib).wait_recv()
    piece = jnp.dot(pick, tst[...].reshape(128, V), preferred_element_type=F32)
    tbuf[y, z] = piece.astype(BF16)

    col_h = (pl.ds(0, HALF), pl.ds(HALF, HALF))

    def along(half, phase, off):
        if (half == 0) == (phase == 0):
            return ring(y + off), dev(ring(y + off), z, k, x)
        return ring(z + off), dev(y, ring(z + off), k, x)

    def t_at(half, first, second):
        if half == 0:
            return tbuf.at[ring(y + first), ring(z + second), :, col_h[0]]
        return tbuf.at[ring(y + second), ring(z + first), :, col_h[1]]

    offs = (0, -sg, sg, 2)

    def t_one(half, n):
        ref = t_at(half, offs[n], 0)
        return ref, tg_ss.at[half, n], tg_rs.at[half, n]

    def t_two(half, m, n):
        ref = t_at(half, offs[m], offs[n])
        return ref, th_ss.at[half, m, n], th_rs.at[half, m, n]

    def t_spread(half, m):
        ref = t_at(half, offs[m], 0)
        send(ref, ref, th_ss.at[half, m, 0], th_rs.at[half, m, 1], along(half, 1, sg)[1])
        send(ref, ref, th_ss.at[half, m, 1], th_rs.at[half, m, 2], along(half, 1, -sg)[1])

    def t_arrive(ref, ss, rs):
        rcopy(ref, ref, ss, rs, sib).wait_recv()

    def t_first(m):
        for half in range(2):
            if m == 0:
                ref = t_at(half, 0, 0)
                send(ref, ref, tg_ss.at[half, 0], tg_rs.at[half, 1], along(half, 0, sg)[1])
                send(ref, ref, tg_ss.at[half, 1], tg_rs.at[half, 2], along(half, 0, -sg)[1])
            else:
                ref, ss, rs = t_one(half, m)
                t_arrive(ref, ss, rs)
                if m == 1:
                    send(ref, ref, tg_ss.at[half, 2], tg_rs.at[half, 3], along(half, 0, sg)[1])
            if m > 0:
                t_spread(half, m)
        if m == 0:
            for half in range(2):
                t_spread(half, 0)

    def t_second(m):
        for half in range(2):
            ref, ss, rs = t_two(half, m, 1)
            t_arrive(ref, ss, rs)
            send(ref, ref, th_ss.at[half, m, 2], th_rs.at[half, m, 3], along(half, 1, sg)[1])

    def t_finish(m):
        for half in range(2):
            for n in (2, 3):
                t_arrive(*t_two(half, m, n))

    for m in range(4):
        t_first(m)
    for m in range(4):
        t_second(m)

    def land(kind, pos):
        slot = k if kind == 0 else 2
        blk = pos_main(pos) if kind == 0 else pos_second(pos)
        for i in range(NS):
            ref = bbuf.at[slot, blk, rows(i)]
            rcopy(ref, ref, bo_ss.at[0, i], b_rs.at[kind, which_of[pos], i], sib).wait_recv()
            if pos == 1:
                to = xp if kind == 0 else xm
                rcopy(ref, ref, bf_ss.at[kind, i], b_rs.at[kind, 1, i], (row, to)).start()
            share(kind, pos, i).start()

    def from_sib(kind, pos):
        slot = 1 - k if kind == 0 else 2
        blk = pos_main(pos) if kind == 0 else pos_second(pos)
        for i in range(NS):
            ref = bbuf.at[slot, blk, rows(i)]
            rcopy(ref, ref, sh_ss.at[kind, pos, i], sh_rs.at[kind, pos, i], sib).wait_recv()

    def land_second(pos):
        @pl.when(is_owner)
        def _():
            land(1, pos)

    def from_owner(pos):
        @pl.when(jnp.logical_not(is_owner))
        def _():
            from_sib(1, pos)

    slot_b, slot_a = owner2, 1 - owner2

    def get_main(owner_gathers, pos):
        gathers = is_owner if owner_gathers else jnp.logical_not(is_owner)

        @pl.when(gathers)
        def _():
            land(0, pos)

        @pl.when(jnp.logical_not(gathers))
        def _():
            from_sib(0, pos)

    def blk_at(pos):
        off = jnp.where(pos == 1, -s, jnp.where(pos == 2, s, jnp.where(pos == 3, 2, 0)))
        return ring(x + off)

    def pick_pos(pos, values):
        return jnp.where(pos == 0, values[0], jnp.where(pos == 1, values[1], jnp.where(pos == 2, values[2], values[3])))

    def first_product(slot, pos):
        val = jnp.dot(bbuf[slot, blk_at(pos)], tbuf[...].reshape(V, V), preferred_element_type=F32)
        one = pl.multiple_of(pick_pos(pos, (640, 0, 320, 768)), 64)
        two = pl.multiple_of(pick_pos(pos, (1088, 128, 448, 896)), 64)
        xbuf[slot, pl.ds(one, 128), :] = val[0:128].astype(BF16)
        xbuf[slot, pl.ds(two, 192), :] = val[128:320].astype(BF16)

    nt = (((1,), (1,)), ((), ()))

    def second_product(blk, lo, width):
        cols = pl.ds(lo, width)
        val = jnp.dot(ut[pl.ds(pl.multiple_of(blk * BLK, 64), BLK), :], li2[:, cols], preferred_element_type=F32)
        for sl in range(3):
            val += lax.dot_general(bbuf[sl, blk], xbuf[sl, cols, :], nt, preferred_element_type=F32)
        acc[blk, :, :, cols] = val.reshape(4, PIECE, width)

    def ralong(n, phase, off):
        return along(1 - PARTS[n][0], phase, off)

    def cols_of(n):
        return pl.ds(PARTS[n][1], PARTS[n][2])

    def part(n, t, i):
        if PARTS[n][0] == 0:
            return acc[t, i, :, cols_of(n)]
        return acc[i, t, :, cols_of(n)]

    def p1_at(ref, n, m):
        return ref.at[n, m, :, :, pl.ds(0, PARTS[n][2])]

    def p2_at(ref, n, m):
        return ref.at[n, m, :, pl.ds(0, PARTS[n][2])]

    def got1(n, m, t):
        return r1[n, m, t, :, pl.ds(0, PARTS[n][2])].astype(F32)

    def got2(n, m):
        return r2[n, m, :, pl.ds(0, PARTS[n][2])].astype(F32)

    hops = (2, -1, 1)

    def width(n):
        return pl.ds(0, PARTS[n][2])

    def row_copy(n, m, t):
        at = (n, m, t, slice(None), width(n))
        return rcopy(s1.at[at], r1.at[at], p1_ss.at[n, m, t], p1_rs.at[n, m, t], ralong(n, 0, hops[m])[1])

    def send_rows(n, t):
        for m in range(3):
            s1[n, m, t, :, width(n)] = part(n, t, ralong(n, 0, hops[m])[0]).astype(BF16)
            row_copy(n, m, t).start()

    def blk_copy(n, m):
        return rcopy(p1_at(s1, n, m), p1_at(r1, n, m), p1_ss.at[n, m, 0], p1_rs.at[n, m, 0],
                     ralong(n, 0, hops[m])[1])

    def send_block(n, blk):
        for m in range(3):
            @pl.when(blk == ralong(n, 0, hops[m])[0])
            def _():
                for t in range(4):
                    s1[n, m, t, :, width(n)] = acc[blk, t, :, cols_of(n)].astype(BF16)
                blk_copy(n, m).start()

    def p1_each(n, what):
        for m in range(3):
            if PARTS[n][0] == 0:
                @pl.loop(0, 4)
                def _(t):
                    what(row_copy(n, m, t))
            else:
                what(blk_copy(n, m))

    def y_order(pos):
        return ring(y + jnp.where(pos == 0, 2, jnp.where(pos == 1, -1, jnp.where(pos == 2, 1, 0))))

    def p1_end(n):
        here = ralong(n, 0, 0)[0]
        p1_each(n, lambda c: c.wait_recv())

        def total(t):
            return (part(n, t, here) + got1(n, 0, t)) + (got1(n, 1, t) + got1(n, 2, t))

        for m in range(3):
            there, there_dev = ralong(n, 1, hops[m])
            s2[n, m, :, width(n)] = total(there).astype(BF16)
            send(p2_at(s2, n, m), p2_at(r2, n, m), p2_ss.at[n, m], p2_rs.at[n, m], there_dev)
        fin[:, cols_of(n)] = total(ralong(n, 1, 0)[0])

    def p2_end(n):
        for m in range(3):
            rcopy(p2_at(s2, n, m), p2_at(r2, n, m), p2_ss.at[n, m], p2_rs.at[n, m], sib).wait_recv()
        fin[:, cols_of(n)] = (fin[:, cols_of(n)] + got2(n, 0)) + (got2(n, 1) + got2(n, 2))

    def x_send(place):
        xx = blk_at(place)
        for kk in range(2):
            for col, r, m in LAID[place]:
                gbuf[place, kk, :, r:r + m] = fin[kk * 40:(kk + 1) * 40, col:col + m]
        if place == OWN:
            send(gbuf.at[OWN, 1 - k], hbuf.at[me8], g_ss.at[OWN, 0], g_rs.at[me8], sib)
            hbuf[me8] = gbuf[OWN, k]
        else:
            for kk in range(2):
                send(gbuf.at[place, kk], hbuf.at[me8], g_ss.at[place, kk], g_rs.at[me8], dev(y, z, kk, xx))

    def cycle_terms():
        rcopy(l_own, lbuf.at[1], l_ss, l_rs, sib).wait_recv()
        pick_l = jnp.where(k == x // 2, 0, 1)
        u = jnp.dot(lbuf[pick_l, 0:16], tbuf[...].reshape(V, V), preferred_element_type=F32)
        hi = u.astype(BF16).astype(F32)
        ut[...] = jnp.concatenate([hi, u - hi], axis=0).T.astype(BF16)
        li = lbuf[pick_l, 16:32]
        for n in range(4):
            blk = blk_at(n)
            for kk in range(4):
                @pl.when(blk == kk)
                def _():
                    for col, r, m in LAID[n]:
                        li2[0:16, col:col + m] = li[:, kk * BLK + r:kk * BLK + r + m]
                        li2[16:32, col:col + m] = li[:, kk * BLK + r:kk * BLK + r + m]

    def gatherer(owner):
        return pl.when(is_owner if owner else jnp.logical_not(is_owner))

    land(0, 1)
    land_second(1)

    @gatherer(False)
    def _():
        land(0, 2)

    for m in range(4):
        t_finish(m)
    own_main.wait()

    @gatherer(True)
    def _():
        own_second.wait()

    from_sib(0, 0)
    from_owner(0)

    @pl.loop(0, 16)
    def _(step):
        @pl.when(step == 3)
        def _():
            cycle_terms()
            from_sib(0, 1)
            land_second(2)

        @pl.when(step == 5)
        def _():
            @gatherer(True)
            def _():
                from_sib(0, 2)

        @pl.when(step == 6)
        def _():
            from_owner(1)

        @pl.when(step == 7)
        def _():
            from_owner(2)

        @pl.when(step == 8)
        def _():
            get_main(True, 2)

        @pl.when(step == 9)
        def _():
            land_second(3)
            from_owner(3)

        @pl.when(step == 10)
        def _():
            get_main(False, 3)

        @pl.when(step == 13)
        def _():
            @gatherer(True)
            def _():
                land(0, 3)

        @pl.when(step == 14)
        def _():
            @gatherer(False)
            def _():
                from_sib(0, 3)

        late_slot = jnp.where((step == 4) | (step == 5) | (step == 10), slot_a, 2)
        slot = jnp.where(step < 3, step, jnp.where((step == 3) | (step == 8) | (step == 14), slot_b, late_slot))
        late_pos = jnp.where((step == 5) | (step == 6) | (step == 8), 2, 3)
        pos = jnp.where(step < 3, 0, jnp.where((step == 3) | (step == 4) | (step == 7), 1, late_pos))
        summing = ((step >= 11) & (step < 14)) | (step == 15)

        @pl.when(jnp.logical_not(summing))
        def _():
            first_product(slot, pos)

        @pl.when(summing)
        def _():
            blk = blk_at(jnp.where(step == 15, 3, step - 11))
            second_product(blk, 0, EARLY)
            send_rows(0, blk)
            send_block(1, blk)

    @pl.loop(0, 4)
    def _(pos):
        blk = y_order(pos)
        second_product(blk, EARLY, V - EARLY)
        send_rows(3, blk)
        send_block(2, blk)

    p1_end(0)
    p1_end(1)
    p1_end(2)
    p1_end(3)
    p2_end(0)
    x_send(XM)
    p2_end(1)
    x_send(XP)
    p2_end(2)
    p2_end(3)
    x_send(XO)
    x_send(OWN)

    for d in range(1, 8):
        src8 = lax.rem(me8 + d, 8)
        rcopy(gbuf.at[0, 0], hbuf.at[src8], g_ss.at[0, 0], g_rs.at[src8], sib).wait_recv()
    for p in range(4):
        src = (p % 2) * 4 + p // 2
        out[p] = hbuf[src] + hbuf[src + 2]

    for c in pending:
        c.wait_send()
    for n in range(4):
        p1_each(n, lambda c: c.wait_send())

    def wait_own(kind, pos_list):
        for pos in pos_list:
            for i in range(NS):
                share(kind, pos, i).wait_send()
        for i in range(NS):
            ref = bbuf.at[k if kind == 0 else 2, xm if kind == 0 else xp, rows(i)]
            rcopy(ref, ref, bf_ss.at[kind, i], b_rs.at[kind, 1, i], (row, xp if kind == 0 else xm)).wait_send()

    wait_own(0, (1, 2, 3))

    @pl.when(is_owner)
    def _():
        wait_own(1, (0, 1, 2, 3))


def exchange(*args):
    vmem = pl.BlockSpec(memory_space=pltpu.VMEM)
    anywhere = pl.BlockSpec(memory_space=pl.ANY)
    smem = pl.BlockSpec(memory_space=pltpu.SMEM)
    dma = pltpu.SemaphoreType.DMA
    return pl.pallas_call(
        kernel,
        out_shape=jax.ShapeDtypeStruct((4, 40, BLK), F32),
        in_specs=[anywhere, vmem, anywhere, smem, vmem, vmem],
        out_specs=vmem,
        scratch_shapes=[
            pltpu.VMEM((3, BLK, V), BF16),
            pltpu.VMEM((4, 16, V), BF16),
            pltpu.VMEM((3, 160, V), BF16),
            pltpu.VMEM((32, V), BF16),
            pltpu.VMEM((3, 4, BLK, V), BF16),
            pltpu.VMEM((8, 16, V), BF16),
            pltpu.VMEM((4, 4, PIECE, V), BF16),
            pltpu.VMEM((2, 32, V), BF16),
            pltpu.VMEM((V, 32), BF16),
            pltpu.VMEM((32, V), BF16),
            pltpu.VMEM((3, V, V), BF16),
            pltpu.VMEM((4, 4, PIECE, V), F32),
            pltpu.VMEM((4, 3, 4, PIECE, WIDE), BF16),
            pltpu.VMEM((4, 3, 4, PIECE, WIDE), BF16),
            pltpu.VMEM((4, 3, PIECE, WIDE), BF16),
            pltpu.VMEM((4, 3, PIECE, WIDE), BF16),
            pltpu.VMEM((PIECE, V), F32),
            pltpu.VMEM((4, 2, 40, BLK), F32),
            pltpu.VMEM((8, 40, BLK), F32),
            dma((2,)),
            dma((8,)), dma((8,)),
            dma((2, 4)), dma((2, 4)),
            dma((2, 4, 4)), dma((2, 4, 4)),
            dma, dma,
            dma((2,)),
            dma((3, NS)), dma((2, NS)), dma((2, 3, NS)),
            dma((2, 4, NS)), dma((2, 4, NS)),
            dma((4, 3, 4)), dma((4, 3, 4)), dma((4, 3)), dma((4, 3)),
            dma((4, 2)), dma((8,)),
        ],
        compiler_params=pltpu.CompilerParams(
            collective_id=0, has_side_effects=True, vmem_limit_bytes=62 * 1024 * 1024
        ),
    )(*args)


def local(
    amplitudes, integrals, occupied_integrals, pair_orbitals, amplitude_tiles, integral_tiles
):
    res = exchange(
        integrals,
        jnp.swapaxes(amplitudes, 0, 1),
        occupied_integrals,
        pair_orbitals.T,
        jnp.swapaxes(amplitude_tiles, 0, 1).reshape(80, 20),
        integral_tiles,
    )
    return jnp.swapaxes(res, 1, 2)


def solution(mesh):
    placed = (
        P(None, ("row", "col"), None),
        P("row", "col", None),
        P("row", None, None),
        P(),
        P(),
        P(),
    )
    return jax.shard_map(
        local, mesh=mesh, in_specs=placed, out_specs=P(None, "col", "row"), check_vma=False
    )
```

```python
import jax
import jax.numpy as jnp
from jax import lax
from jax.experimental import pallas as pl
from jax.experimental.pallas import tpu as pltpu
from jax.sharding import PartitionSpec as P

MESH = pl.DeviceIdType.MESH
TILE = 64
V = 1280
VT = 20
BLK = 320
PIECE = 80
HALF = 640
EARLY = 768
WIDE = 512
PARTS = ((0, 0, WIDE), (0, WIDE, 256), (1, EARLY, 384), (0, EARLY + 384, 128))
OWN, XM, XP, XO = range(4)
LAID = (
    ((640, 0, 128), (1088, 128, 192)),
    ((0, 0, 320),),
    ((320, 0, 320),),
    ((768, 0, 320),),
)
NS = 2
SUB = BLK // NS
F32 = jnp.float32
BF16 = jnp.bfloat16


def kernel(
    b_in, t_in, occ_in, pairs, a_tiles, i_tiles, out,
    b_own, t_own, occ, l_own,
    bbuf, tst, tbuf, lbuf, ut, li2, xbuf, acc,
    s1, r1, s2, r2, fin, gbuf, hbuf,
    in_ls, t1_ss, t1_rs, tg_ss, tg_rs, th_ss, th_rs, l_ss, l_rs, own_ls,
    bo_ss, bf_ss, b_rs, sh_ss, sh_rs, p1_ss, p1_rs, p2_ss, p2_rs, g_ss, g_rs,
):
    x = lax.axis_index("col")
    row = lax.axis_index("row")
    k = lax.rem(row, 2)
    yz = row // 2
    y = yz // 4
    z = lax.rem(yz, 4)
    s = 1 - 2 * lax.rem(x, 2)
    xp = lax.rem(x + s + 4, 4)
    xm = lax.rem(x - s + 4, 4)
    xo = lax.rem(x + 2, 4)
    sg = 1 - 2 * k
    me8 = k * 4 + x
    pair = 2 * lax.rem(x, 2) + k
    sib = (yz * 2 + 1 - k, x)
    owner2 = lax.rem((x + 1) // 2 + 1, 2)
    is_owner = k == owner2
    main_j = x // 2

    def dev(yy, zz, kk, xx):
        return ((yy * 4 + zz) * 2 + kk, xx)

    def ring(v):
        return lax.rem(v + 8, 4)

    def peer8(d):
        idx = lax.rem(me8 + d, 8)
        return idx, idx // 4, lax.rem(idx, 4)

    def rcopy(src, dst, ss, rs, to):
        return pltpu.make_async_remote_copy(
            src_ref=src, dst_ref=dst, send_sem=ss, recv_sem=rs, device_id=to, device_id_type=MESH
        )

    pending = []

    def send(src, dst, ss, rs, to):
        c = rcopy(src, dst, ss, rs, to)
        c.start()
        pending.append(c)
        return c

    load_b = pltpu.make_async_copy(b_in, b_own, in_ls.at[0])
    load_b.start()
    load_occ = pltpu.make_async_copy(occ_in, occ, in_ls.at[1])
    load_occ.start()

    barrier = pltpu.get_barrier_semaphore()
    for d in range(1, 8):
        _, kk, xx = peer8(d)
        pl.semaphore_signal(barrier, inc=1, device_id=dev(y, z, kk, xx), device_id_type=MESH)
    for step in (1, 2, -1):
        pl.semaphore_signal(barrier, inc=1, device_id=dev(ring(y + step), z, k, x), device_id_type=MESH)
        pl.semaphore_signal(barrier, inc=1, device_id=dev(y, ring(z + step), k, x), device_id_type=MESH)

    def iota(shape, dim):
        return lax.broadcasted_iota(jnp.int32, shape, dim)

    def ones(cond):
        return jnp.where(cond, 1.0, 0.0).astype(BF16)

    spread = ones(iota((VT, V), 0) == jnp.right_shift(iota((VT, V), 1), 6))
    tile_row = jnp.right_shift(jnp.right_shift(iota((40, 80), 0), 2) + (row * 4 + x) * 10, 6)
    same_pair = jnp.bitwise_and(iota((40, 80), 0), 3) == jnp.bitwise_and(iota((40, 80), 1), 3)
    pick_t = ones(same_pair & (jnp.right_shift(iota((40, 80), 1), 2) == tile_row))
    small = jnp.dot(pick_t, a_tiles[...].astype(F32).astype(BF16), preferred_element_type=F32).astype(BF16)
    mask = jnp.dot(small, spread, preferred_element_type=F32)
    raw = jnp.concatenate([t_in[i].astype(F32) for i in range(10)], axis=0)
    turn_i = jnp.bitwise_and(iota((64, 40), 0), 15)
    turn = ones((turn_i < 10) & (iota((64, 40), 1) == turn_i * 4 + jnp.right_shift(iota((64, 40), 0), 4)))
    turned = jnp.dot(turn, (raw * mask).astype(BF16), preferred_element_type=F32).astype(BF16)
    for p in range(4):
        t_own[p] = turned[p * 16:(p + 1) * 16]
    pick_b = ones(iota((16, VT), 0) + 5 * x == iota((16, VT), 1))
    small = jnp.dot(pick_b, i_tiles[...].astype(F32).astype(BF16), preferred_element_type=F32).astype(BF16)
    mask = jnp.dot(small, spread, preferred_element_type=F32)
    load_b.wait()
    for t in range(BLK // TILE):
        wide = jnp.broadcast_to(mask[t:t + 1], (TILE, V)).astype(BF16)
        for j in range(3):
            b_own[j, t * TILE:(t + 1) * TILE] = b_own[j, t * TILE:(t + 1) * TILE] * wide
    pl.semaphore_wait(barrier, 13)

    for d in range(1, 8):
        idx, kk, xx = peer8(d)
        send(t_own.at[2 * lax.rem(xx, 2) + kk], tst.at[me8], t1_ss.at[d], t1_rs.at[d], dev(y, z, kk, xx))
    dest2 = jnp.where(is_owner, xm, xp)
    which2 = jnp.where(is_owner, 0, 2)

    def rows(i):
        return pl.ds(i * SUB, SUB)

    for i in range(NS):
        send(b_own.at[1 - main_j, rows(i)], bbuf.at[k, x, rows(i)], bo_ss.at[1, i], b_rs.at[0, 2, i],
             (row, xm))
    for i in range(NS):
        send(b_own.at[2, rows(i)], bbuf.at[2, x, rows(i)], bo_ss.at[2, i], b_rs.at[1, which2, i],
             (row, dest2))
    for i in range(NS):
        send(b_own.at[main_j, rows(i)], bbuf.at[k, x, rows(i)], bo_ss.at[0, i], b_rs.at[0, 0, i],
             (row, xp))

    def share(kind, pos, i, src=None):
        slot, blk = (k, None) if kind == 0 else (2, None)
        blk = (x, pos_main(pos) if kind == 0 else pos_second(pos))[pos > 0]
        dst = bbuf.at[slot, blk, rows(i)]
        return rcopy(dst if src is None else src, dst, sh_ss.at[kind, pos, i], sh_rs.at[kind, pos, i], sib)

    def pos_main(pos):
        return (x, xm, xp, xo)[pos]

    def pos_second(pos):
        return (x, xp, xm, xo)[pos]

    which_of = (None, 2, 0, 1)

    for i in range(NS):
        c = share(0, 0, i, b_own.at[main_j, rows(i)])
        c.start()
        pending.append(c)

    @pl.when(is_owner)
    def _():
        for i in range(NS):
            share(1, 0, i, b_own.at[2, rows(i)]).start()

    own_main = pltpu.make_async_copy(b_own.at[main_j], bbuf.at[k, x], own_ls.at[0])
    own_main.start()
    own_second = pltpu.make_async_copy(b_own.at[2], bbuf.at[2, x], own_ls.at[1])

    @pl.when(is_owner)
    def _():
        own_second.start()

    load_occ.wait()
    other = 2 * lax.rem(x, 2) + 1 - k
    orb_row, orb_col = iota((32, 480), 0), iota((32, 480), 1)

    def occ_rows(p):
        aux = jnp.bitwise_and(orb_row, 15)
        orb = jnp.where(orb_row < 16, pairs[1, p], pairs[0, p])
        hot = ones((orb_col == aux * 160 + orb) & (aux < 3))
        return jnp.dot(hot, occ[...].reshape(480, V), preferred_element_type=F32).astype(BF16)

    l_own[...] = occ_rows(other)
    lbuf[0] = occ_rows(pair)
    send(l_own, lbuf.at[1], l_ss, l_rs, sib)

    tst[me8] = t_own[pair]
    ri, ci = iota((PIECE, 128), 0), iota((PIECE, 128), 1)
    within = jnp.bitwise_and(ci, 15)
    pick = ones((within < 10) & (ri == jnp.right_shift(ci, 4) * 10 + within))
    for d in range(1, 8):
        src8 = lax.rem(me8 + 8 - d, 8)
        rcopy(t_own.at[0], tst.at[src8], t1_ss.at[d], t1_rs.at[d], sib).wait_recv()
    piece = jnp.dot(pick, tst[...].reshape(128, V), preferred_element_type=F32)
    tbuf[y, z] = piece.astype(BF16)

    col_h = (pl.ds(0, HALF), pl.ds(HALF, HALF))

    def along(half, phase, off):
        if (half == 0) == (phase == 0):
            return ring(y + off), dev(ring(y + off), z, k, x)
        return ring(z + off), dev(y, ring(z + off), k, x)

    def t_at(half, first, second):
        if half == 0:
            return tbuf.at[ring(y + first), ring(z + second), :, col_h[0]]
        return tbuf.at[ring(y + second), ring(z + first), :, col_h[1]]

    offs = (0, -sg, sg, 2)

    def t_one(half, n):
        ref = t_at(half, offs[n], 0)
        return ref, tg_ss.at[half, n], tg_rs.at[half, n]

    def t_two(half, m, n):
        ref = t_at(half, offs[m], offs[n])
        return ref, th_ss.at[half, m, n], th_rs.at[half, m, n]

    def t_spread(half, m):
        ref = t_at(half, offs[m], 0)
        send(ref, ref, th_ss.at[half, m, 0], th_rs.at[half, m, 1], along(half, 1, sg)[1])
        send(ref, ref, th_ss.at[half, m, 1], th_rs.at[half, m, 2], along(half, 1, -sg)[1])

    def t_arrive(ref, ss, rs):
        rcopy(ref, ref, ss, rs, sib).wait_recv()

    def t_first(m):
        for half in range(2):
            if m == 0:
                ref = t_at(half, 0, 0)
                send(ref, ref, tg_ss.at[half, 0], tg_rs.at[half, 1], along(half, 0, sg)[1])
                send(ref, ref, tg_ss.at[half, 1], tg_rs.at[half, 2], along(half, 0, -sg)[1])
            else:
                ref, ss, rs = t_one(half, m)
                t_arrive(ref, ss, rs)
                if m == 1:
                    send(ref, ref, tg_ss.at[half, 2], tg_rs.at[half, 3], along(half, 0, sg)[1])
            if m > 0:
                t_spread(half, m)
        if m == 0:
            for half in range(2):
                t_spread(half, 0)

    def t_second(m):
        for half in range(2):
            ref, ss, rs = t_two(half, m, 1)
            t_arrive(ref, ss, rs)
            send(ref, ref, th_ss.at[half, m, 2], th_rs.at[half, m, 3], along(half, 1, sg)[1])

    def t_finish(m):
        for half in range(2):
            for n in (2, 3):
                t_arrive(*t_two(half, m, n))

    for m in range(4):
        t_first(m)
    for m in range(4):
        t_second(m)

    def land(kind, pos):
        slot = k if kind == 0 else 2
        blk = pos_main(pos) if kind == 0 else pos_second(pos)
        for i in range(NS):
            ref = bbuf.at[slot, blk, rows(i)]
            rcopy(ref, ref, bo_ss.at[0, i], b_rs.at[kind, which_of[pos], i], sib).wait_recv()
            if pos == 1:
                to = xp if kind == 0 else xm
                rcopy(ref, ref, bf_ss.at[kind, i], b_rs.at[kind, 1, i], (row, to)).start()
            share(kind, pos, i).start()

    def from_sib(kind, pos):
        slot = 1 - k if kind == 0 else 2
        blk = pos_main(pos) if kind == 0 else pos_second(pos)
        for i in range(NS):
            ref = bbuf.at[slot, blk, rows(i)]
            rcopy(ref, ref, sh_ss.at[kind, pos, i], sh_rs.at[kind, pos, i], sib).wait_recv()

    def land_second(pos):
        @pl.when(is_owner)
        def _():
            land(1, pos)

    def from_owner(pos):
        @pl.when(jnp.logical_not(is_owner))
        def _():
            from_sib(1, pos)

    slot_b, slot_a = owner2, 1 - owner2

    def blk_at(pos):
        off = jnp.where(pos == 1, -s, jnp.where(pos == 2, s, jnp.where(pos == 3, 2, 0)))
        return ring(x + off)

    def pick_pos(pos, values):
        return jnp.where(pos == 0, values[0], jnp.where(pos == 1, values[1], jnp.where(pos == 2, values[2], values[3])))

    def first_product(slot, pos):
        val = jnp.dot(bbuf[slot, blk_at(pos)], tbuf[...].reshape(V, V), preferred_element_type=F32)
        one = pl.multiple_of(pick_pos(pos, (640, 0, 320, 768)), 64)
        two = pl.multiple_of(pick_pos(pos, (1088, 128, 448, 896)), 64)
        xbuf[slot, pl.ds(one, 128), :] = val[0:128].astype(BF16)
        xbuf[slot, pl.ds(two, 192), :] = val[128:320].astype(BF16)

    nt = (((1,), (1,)), ((), ()))

    def second_product(blk, lo, width):
        cols = pl.ds(lo, width)
        val = jnp.dot(ut[pl.ds(pl.multiple_of(blk * BLK, 64), BLK), :], li2[:, cols], preferred_element_type=F32)
        for sl in range(3):
            val += lax.dot_general(bbuf[sl, blk], xbuf[sl, cols, :], nt, preferred_element_type=F32)
        acc[blk, :, :, cols] = val.reshape(4, PIECE, width)

    def ralong(n, phase, off):
        return along(1 - PARTS[n][0], phase, off)

    def cols_of(n):
        return pl.ds(PARTS[n][1], PARTS[n][2])

    def part(n, t, i):
        if PARTS[n][0] == 0:
            return acc[t, i, :, cols_of(n)]
        return acc[i, t, :, cols_of(n)]

    def p1_at(ref, n, m):
        return ref.at[n, m, :, :, pl.ds(0, PARTS[n][2])]

    def p2_at(ref, n, m):
        return ref.at[n, m, :, pl.ds(0, PARTS[n][2])]

    def got1(n, m, t):
        return r1[n, m, t, :, pl.ds(0, PARTS[n][2])].astype(F32)

    def got2(n, m):
        return r2[n, m, :, pl.ds(0, PARTS[n][2])].astype(F32)

    hops = (2, -1, 1)

    def width(n):
        return pl.ds(0, PARTS[n][2])

    def row_copy(n, m, t):
        at = (n, m, t, slice(None), width(n))
        return rcopy(s1.at[at], r1.at[at], p1_ss.at[n, m, t], p1_rs.at[n, m, t], ralong(n, 0, hops[m])[1])

    def send_rows(n, t):
        for m in range(3):
            s1[n, m, t, :, width(n)] = part(n, t, ralong(n, 0, hops[m])[0]).astype(BF16)
            row_copy(n, m, t).start()

    def blk_copy(n, m):
        return rcopy(p1_at(s1, n, m), p1_at(r1, n, m), p1_ss.at[n, m, 0], p1_rs.at[n, m, 0],
                     ralong(n, 0, hops[m])[1])

    def send_block(n, blk):
        for m in range(3):
            @pl.when(blk == ralong(n, 0, hops[m])[0])
            def _():
                for t in range(4):
                    s1[n, m, t, :, width(n)] = acc[blk, t, :, cols_of(n)].astype(BF16)
                blk_copy(n, m).start()

    def p1_each(n, what):
        for m in range(3):
            if PARTS[n][0] == 0:
                @pl.loop(0, 4)
                def _(t):
                    what(row_copy(n, m, t))
            else:
                what(blk_copy(n, m))

    def y_order(pos):
        return ring(y + jnp.where(pos == 0, 2, jnp.where(pos == 1, -1, jnp.where(pos == 2, 1, 0))))

    def p1_end(n):
        here = ralong(n, 0, 0)[0]
        p1_each(n, lambda c: c.wait_recv())

        def total(t):
            return (part(n, t, here) + got1(n, 0, t)) + (got1(n, 1, t) + got1(n, 2, t))

        for m in range(3):
            there, there_dev = ralong(n, 1, hops[m])
            s2[n, m, :, width(n)] = total(there).astype(BF16)
            send(p2_at(s2, n, m), p2_at(r2, n, m), p2_ss.at[n, m], p2_rs.at[n, m], there_dev)
        fin[:, cols_of(n)] = total(ralong(n, 1, 0)[0])

    def p2_end(n):
        for m in range(3):
            rcopy(p2_at(s2, n, m), p2_at(r2, n, m), p2_ss.at[n, m], p2_rs.at[n, m], sib).wait_recv()
        fin[:, cols_of(n)] = (fin[:, cols_of(n)] + got2(n, 0)) + (got2(n, 1) + got2(n, 2))

    def x_send(place):
        xx = blk_at(place)
        for kk in range(2):
            for col, r, m in LAID[place]:
                gbuf[place, kk, :, r:r + m] = fin[kk * 40:(kk + 1) * 40, col:col + m]
        if place == OWN:
            send(gbuf.at[OWN, 1 - k], hbuf.at[me8], g_ss.at[OWN, 0], g_rs.at[me8], sib)
            hbuf[me8] = gbuf[OWN, k]
        else:
            for kk in range(2):
                send(gbuf.at[place, kk], hbuf.at[me8], g_ss.at[place, kk], g_rs.at[me8], dev(y, z, kk, xx))

    def cycle_terms():
        rcopy(l_own, lbuf.at[1], l_ss, l_rs, sib).wait_recv()
        pick_l = jnp.where(k == x // 2, 0, 1)
        u = jnp.dot(lbuf[pick_l, 0:16], tbuf[...].reshape(V, V), preferred_element_type=F32)
        hi = u.astype(BF16).astype(F32)
        ut[...] = jnp.concatenate([hi, u - hi], axis=0).T.astype(BF16)
        li = lbuf[pick_l, 16:32]
        for n in range(4):
            blk = blk_at(n)
            for kk in range(4):
                @pl.when(blk == kk)
                def _():
                    for col, r, m in LAID[n]:
                        li2[0:16, col:col + m] = li[:, kk * BLK + r:kk * BLK + r + m]
                        li2[16:32, col:col + m] = li[:, kk * BLK + r:kk * BLK + r + m]

    def gatherer(owner):
        return pl.when(is_owner if owner else jnp.logical_not(is_owner))

    land(0, 1)
    land_second(1)

    @gatherer(False)
    def _():
        land(0, 2)

    for m in range(4):
        t_finish(m)
    own_main.wait()

    @gatherer(True)
    def _():
        own_second.wait()

    from_sib(0, 0)
    from_owner(0)

    @pl.loop(0, 16)
    def _(step):
        @pl.when(step == 3)
        def _():
            cycle_terms()
            from_sib(0, 1)
            land_second(2)

        @pl.when(step == 5)
        def _():
            @gatherer(True)
            def _():
                from_sib(0, 2)

        @pl.when(step == 6)
        def _():
            from_owner(1)

        @pl.when(step == 7)
        def _():
            from_owner(2)

            @gatherer(True)
            def _():
                land(0, 2)

        @pl.when(step == 8)
        def _():
            @gatherer(False)
            def _():
                from_sib(0, 2)

        @pl.when(step == 11)
        def _():
            land_second(3)

            @gatherer(False)
            def _():
                land(0, 3)

        @pl.when(step == 12)
        def _():
            from_owner(3)

            @gatherer(True)
            def _():
                land(0, 3)

        @pl.when(step == 13)
        def _():
            @gatherer(True)
            def _():
                from_sib(0, 3)

        @pl.when(step == 14)
        def _():
            @gatherer(False)
            def _():
                from_sib(0, 3)

        late_slot = jnp.where((step == 4) | (step == 5) | (step == 13), slot_a, 2)
        slot = jnp.where(step < 3, step, jnp.where((step == 3) | (step == 8) | (step == 14), slot_b, late_slot))
        late_pos = jnp.where((step == 5) | (step == 6) | (step == 8), 2, 3)
        pos = jnp.where(step < 3, 0, jnp.where((step == 3) | (step == 4) | (step == 7), 1, late_pos))
        summing = ((step >= 9) & (step < 12)) | (step == 15)

        @pl.when(jnp.logical_not(summing))
        def _():
            first_product(slot, pos)

        @pl.when(summing)
        def _():
            blk = blk_at(jnp.where(step == 15, 3, lax.rem(step + y, 3)))
            second_product(blk, 0, EARLY)
            send_rows(0, blk)
            send_rows(1, blk)

    @pl.loop(0, 4)
    def _(pos):
        blk = y_order(pos)
        second_product(blk, EARLY, V - EARLY)
        send_rows(3, blk)
        send_block(2, blk)

    p1_end(0)
    p1_end(1)
    p1_end(2)
    p1_end(3)
    p2_end(0)
    x_send(XM)
    p2_end(1)
    x_send(XP)
    p2_end(2)
    x_send(XO)
    p2_end(3)
    x_send(OWN)

    for d in range(1, 8):
        src8 = lax.rem(me8 + d, 8)
        rcopy(gbuf.at[0, 0], hbuf.at[src8], g_ss.at[0, 0], g_rs.at[src8], sib).wait_recv()
    for p in range(4):
        src = (p % 2) * 4 + p // 2
        out[p] = hbuf[src] + hbuf[src + 2]

    for c in pending:
        c.wait_send()
    for n in range(4):
        p1_each(n, lambda c: c.wait_send())

    def wait_own(kind, pos_list):
        for pos in pos_list:
            for i in range(NS):
                share(kind, pos, i).wait_send()
        for i in range(NS):
            ref = bbuf.at[k if kind == 0 else 2, xm if kind == 0 else xp, rows(i)]
            rcopy(ref, ref, bf_ss.at[kind, i], b_rs.at[kind, 1, i], (row, xp if kind == 0 else xm)).wait_send()

    wait_own(0, (1, 2, 3))

    @pl.when(is_owner)
    def _():
        wait_own(1, (0, 1, 2, 3))


def exchange(*args):
    vmem = pl.BlockSpec(memory_space=pltpu.VMEM)
    anywhere = pl.BlockSpec(memory_space=pl.ANY)
    smem = pl.BlockSpec(memory_space=pltpu.SMEM)
    dma = pltpu.SemaphoreType.DMA
    return pl.pallas_call(
        kernel,
        out_shape=jax.ShapeDtypeStruct((4, 40, BLK), F32),
        in_specs=[anywhere, vmem, anywhere, smem, vmem, vmem],
        out_specs=vmem,
        scratch_shapes=[
            pltpu.VMEM((3, BLK, V), BF16),
            pltpu.VMEM((4, 16, V), BF16),
            pltpu.VMEM((3, 160, V), BF16),
            pltpu.VMEM((32, V), BF16),
            pltpu.VMEM((3, 4, BLK, V), BF16),
            pltpu.VMEM((8, 16, V), BF16),
            pltpu.VMEM((4, 4, PIECE, V), BF16),
            pltpu.VMEM((2, 32, V), BF16),
            pltpu.VMEM((V, 32), BF16),
            pltpu.VMEM((32, V), BF16),
            pltpu.VMEM((3, V, V), BF16),
            pltpu.VMEM((4, 4, PIECE, V), F32),
            pltpu.VMEM((4, 3, 4, PIECE, WIDE), BF16),
            pltpu.VMEM((4, 3, 4, PIECE, WIDE), BF16),
            pltpu.VMEM((4, 3, PIECE, WIDE), BF16),
            pltpu.VMEM((4, 3, PIECE, WIDE), BF16),
            pltpu.VMEM((PIECE, V), F32),
            pltpu.VMEM((4, 2, 40, BLK), F32),
            pltpu.VMEM((8, 40, BLK), F32),
            dma((2,)),
            dma((8,)), dma((8,)),
            dma((2, 4)), dma((2, 4)),
            dma((2, 4, 4)), dma((2, 4, 4)),
            dma, dma,
            dma((2,)),
            dma((3, NS)), dma((2, NS)), dma((2, 3, NS)),
            dma((2, 4, NS)), dma((2, 4, NS)),
            dma((4, 3, 4)), dma((4, 3, 4)), dma((4, 3)), dma((4, 3)),
            dma((4, 2)), dma((8,)),
        ],
        compiler_params=pltpu.CompilerParams(
            collective_id=0, has_side_effects=True, vmem_limit_bytes=62 * 1024 * 1024
        ),
    )(*args)


def local(
    amplitudes, integrals, occupied_integrals, pair_orbitals, amplitude_tiles, integral_tiles
):
    res = exchange(
        integrals,
        jnp.swapaxes(amplitudes, 0, 1),
        occupied_integrals,
        pair_orbitals.T,
        jnp.swapaxes(amplitude_tiles, 0, 1).reshape(80, 20),
        integral_tiles,
    )
    return jnp.swapaxes(res, 1, 2)


def solution(mesh):
    placed = (
        P(None, ("row", "col"), None),
        P("row", "col", None),
        P("row", None, None),
        P(),
        P(),
        P(),
    )
    return jax.shard_map(
        local, mesh=mesh, in_specs=placed, out_specs=P(None, "col", "row"), check_vma=False
    )
```

```python
import jax
import jax.numpy as jnp
from jax import lax
from jax.experimental import pallas as pl
from jax.experimental.pallas import tpu as pltpu
from jax.sharding import PartitionSpec as P

MESH = pl.DeviceIdType.MESH
TILE = 64
V = 1280
VT = 20
BLK = 320
PIECE = 80
HALF = 640
EARLY = 768
WIDE = 512
PARTS = ((0, 0, WIDE), (0, WIDE, 256), (1, EARLY, 256), (0, EARLY + 256, 256))
OWN, XM, XP, XO = range(4)
LAID = (
    ((640, 0, 128), (1088, 128, 192)),
    ((0, 0, 320),),
    ((320, 0, 320),),
    ((768, 0, 320),),
)
NS = 2
SUB = BLK // NS
F32 = jnp.float32
BF16 = jnp.bfloat16


def kernel(
    b_in, t_in, occ_in, pairs, a_tiles, i_tiles, out,
    b_own, t_own, occ, l_own,
    bbuf, tst, tbuf, lbuf, ut, li2, xbuf, acc,
    s1, r1, s2, r2, fin, gbuf, hbuf,
    in_ls, t1_ss, t1_rs, tg_ss, tg_rs, th_ss, th_rs, l_ss, l_rs, own_ls,
    bo_ss, bf_ss, b_rs, sh_ss, sh_rs, p1_ss, p1_rs, p2_ss, p2_rs, g_ss, g_rs,
):
    x = lax.axis_index("col")
    row = lax.axis_index("row")
    k = lax.rem(row, 2)
    yz = row // 2
    y = yz // 4
    z = lax.rem(yz, 4)
    s = 1 - 2 * lax.rem(x, 2)
    xp = lax.rem(x + s + 4, 4)
    xm = lax.rem(x - s + 4, 4)
    xo = lax.rem(x + 2, 4)
    sg = 1 - 2 * k
    me8 = k * 4 + x
    pair = 2 * lax.rem(x, 2) + k
    sib = (yz * 2 + 1 - k, x)
    owner2 = lax.rem((x + 1) // 2 + 1, 2)
    is_owner = k == owner2
    main_j = x // 2

    def dev(yy, zz, kk, xx):
        return ((yy * 4 + zz) * 2 + kk, xx)

    def ring(v):
        return lax.rem(v + 8, 4)

    def peer8(d):
        idx = lax.rem(me8 + d, 8)
        return idx, idx // 4, lax.rem(idx, 4)

    def rcopy(src, dst, ss, rs, to):
        return pltpu.make_async_remote_copy(
            src_ref=src, dst_ref=dst, send_sem=ss, recv_sem=rs, device_id=to, device_id_type=MESH
        )

    pending = []

    def send(src, dst, ss, rs, to):
        c = rcopy(src, dst, ss, rs, to)
        c.start()
        pending.append(c)
        return c

    load_b = pltpu.make_async_copy(b_in, b_own, in_ls.at[0])
    load_b.start()
    load_occ = pltpu.make_async_copy(occ_in, occ, in_ls.at[1])
    load_occ.start()

    barrier = pltpu.get_barrier_semaphore()
    for d in range(1, 8):
        _, kk, xx = peer8(d)
        pl.semaphore_signal(barrier, inc=1, device_id=dev(y, z, kk, xx), device_id_type=MESH)
    for step in (1, 2, -1):
        pl.semaphore_signal(barrier, inc=1, device_id=dev(ring(y + step), z, k, x), device_id_type=MESH)
        pl.semaphore_signal(barrier, inc=1, device_id=dev(y, ring(z + step), k, x), device_id_type=MESH)

    def iota(shape, dim):
        return lax.broadcasted_iota(jnp.int32, shape, dim)

    def ones(cond):
        return jnp.where(cond, 1.0, 0.0).astype(BF16)

    spread = ones(iota((VT, V), 0) == jnp.right_shift(iota((VT, V), 1), 6))
    tile_row = jnp.right_shift(jnp.right_shift(iota((40, 80), 0), 2) + (row * 4 + x) * 10, 6)
    same_pair = jnp.bitwise_and(iota((40, 80), 0), 3) == jnp.bitwise_and(iota((40, 80), 1), 3)
    pick_t = ones(same_pair & (jnp.right_shift(iota((40, 80), 1), 2) == tile_row))
    small = jnp.dot(pick_t, a_tiles[...].astype(F32).astype(BF16), preferred_element_type=F32).astype(BF16)
    mask = jnp.dot(small, spread, preferred_element_type=F32)
    raw = jnp.concatenate([t_in[i].astype(F32) for i in range(10)], axis=0)
    turn_i = jnp.bitwise_and(iota((64, 40), 0), 15)
    turn = ones((turn_i < 10) & (iota((64, 40), 1) == turn_i * 4 + jnp.right_shift(iota((64, 40), 0), 4)))
    turned = jnp.dot(turn, (raw * mask).astype(BF16), preferred_element_type=F32).astype(BF16)
    for p in range(4):
        t_own[p] = turned[p * 16:(p + 1) * 16]
    pick_b = ones(iota((16, VT), 0) + 5 * x == iota((16, VT), 1))
    small = jnp.dot(pick_b, i_tiles[...].astype(F32).astype(BF16), preferred_element_type=F32).astype(BF16)
    mask = jnp.dot(small, spread, preferred_element_type=F32)
    load_b.wait()
    for t in range(BLK // TILE):
        wide = jnp.broadcast_to(mask[t:t + 1], (TILE, V)).astype(BF16)
        for j in range(3):
            b_own[j, t * TILE:(t + 1) * TILE] = b_own[j, t * TILE:(t + 1) * TILE] * wide
    pl.semaphore_wait(barrier, 13)

    for d in range(1, 8):
        idx, kk, xx = peer8(d)
        send(t_own.at[2 * lax.rem(xx, 2) + kk], tst.at[me8], t1_ss.at[d], t1_rs.at[d], dev(y, z, kk, xx))
    dest2 = jnp.where(is_owner, xm, xp)
    which2 = jnp.where(is_owner, 0, 2)

    def rows(i):
        return pl.ds(i * SUB, SUB)

    for i in range(NS):
        send(b_own.at[1 - main_j, rows(i)], bbuf.at[k, x, rows(i)], bo_ss.at[1, i], b_rs.at[0, 2, i],
             (row, xm))
    for i in range(NS):
        send(b_own.at[2, rows(i)], bbuf.at[2, x, rows(i)], bo_ss.at[2, i], b_rs.at[1, which2, i],
             (row, dest2))
    for i in range(NS):
        send(b_own.at[main_j, rows(i)], bbuf.at[k, x, rows(i)], bo_ss.at[0, i], b_rs.at[0, 0, i],
             (row, xp))

    def share(kind, pos, i, src=None):
        slot, blk = (k, None) if kind == 0 else (2, None)
        blk = (x, pos_main(pos) if kind == 0 else pos_second(pos))[pos > 0]
        dst = bbuf.at[slot, blk, rows(i)]
        return rcopy(dst if src is None else src, dst, sh_ss.at[kind, pos, i], sh_rs.at[kind, pos, i], sib)

    def pos_main(pos):
        return (x, xm, xp, xo)[pos]

    def pos_second(pos):
        return (x, xp, xm, xo)[pos]

    which_of = (None, 2, 0, 1)

    for i in range(NS):
        c = share(0, 0, i, b_own.at[main_j, rows(i)])
        c.start()
        pending.append(c)

    @pl.when(is_owner)
    def _():
        for i in range(NS):
            share(1, 0, i, b_own.at[2, rows(i)]).start()

    own_main = pltpu.make_async_copy(b_own.at[main_j], bbuf.at[k, x], own_ls.at[0])
    own_main.start()
    own_second = pltpu.make_async_copy(b_own.at[2], bbuf.at[2, x], own_ls.at[1])

    @pl.when(is_owner)
    def _():
        own_second.start()

    load_occ.wait()
    other = 2 * lax.rem(x, 2) + 1 - k
    orb_row, orb_col = iota((32, 480), 0), iota((32, 480), 1)

    def occ_rows(p):
        aux = jnp.bitwise_and(orb_row, 15)
        orb = jnp.where(orb_row < 16, pairs[1, p], pairs[0, p])
        hot = ones((orb_col == aux * 160 + orb) & (aux < 3))
        return jnp.dot(hot, occ[...].reshape(480, V), preferred_element_type=F32).astype(BF16)

    l_own[...] = occ_rows(other)
    lbuf[0] = occ_rows(pair)
    send(l_own, lbuf.at[1], l_ss, l_rs, sib)

    tst[me8] = t_own[pair]
    ri, ci = iota((PIECE, 128), 0), iota((PIECE, 128), 1)
    within = jnp.bitwise_and(ci, 15)
    pick = ones((within < 10) & (ri == jnp.right_shift(ci, 4) * 10 + within))
    for d in range(1, 8):
        src8 = lax.rem(me8 + 8 - d, 8)
        rcopy(t_own.at[0], tst.at[src8], t1_ss.at[d], t1_rs.at[d], sib).wait_recv()
    piece = jnp.dot(pick, tst[...].reshape(128, V), preferred_element_type=F32)
    tbuf[y, z] = piece.astype(BF16)

    col_h = (pl.ds(0, HALF), pl.ds(HALF, HALF))

    def along(half, phase, off):
        if (half == 0) == (phase == 0):
            return ring(y + off), dev(ring(y + off), z, k, x)
        return ring(z + off), dev(y, ring(z + off), k, x)

    def t_at(half, first, second):
        if half == 0:
            return tbuf.at[ring(y + first), ring(z + second), :, col_h[0]]
        return tbuf.at[ring(y + second), ring(z + first), :, col_h[1]]

    offs = (0, -sg, sg, 2)

    def t_one(half, n):
        ref = t_at(half, offs[n], 0)
        return ref, tg_ss.at[half, n], tg_rs.at[half, n]

    def t_two(half, m, n):
        ref = t_at(half, offs[m], offs[n])
        return ref, th_ss.at[half, m, n], th_rs.at[half, m, n]

    def t_spread(half, m):
        ref = t_at(half, offs[m], 0)
        send(ref, ref, th_ss.at[half, m, 0], th_rs.at[half, m, 1], along(half, 1, sg)[1])
        send(ref, ref, th_ss.at[half, m, 1], th_rs.at[half, m, 2], along(half, 1, -sg)[1])

    def t_arrive(ref, ss, rs):
        rcopy(ref, ref, ss, rs, sib).wait_recv()

    def t_first(m):
        for half in range(2):
            if m == 0:
                ref = t_at(half, 0, 0)
                send(ref, ref, tg_ss.at[half, 0], tg_rs.at[half, 1], along(half, 0, sg)[1])
                send(ref, ref, tg_ss.at[half, 1], tg_rs.at[half, 2], along(half, 0, -sg)[1])
            else:
                ref, ss, rs = t_one(half, m)
                t_arrive(ref, ss, rs)
                if m == 1:
                    send(ref, ref, tg_ss.at[half, 2], tg_rs.at[half, 3], along(half, 0, sg)[1])
            if m > 0:
                t_spread(half, m)
        if m == 0:
            for half in range(2):
                t_spread(half, 0)

    def t_second(m):
        for half in range(2):
            ref, ss, rs = t_two(half, m, 1)
            t_arrive(ref, ss, rs)
            send(ref, ref, th_ss.at[half, m, 2], th_rs.at[half, m, 3], along(half, 1, sg)[1])

    def t_finish(m):
        for half in range(2):
            for n in (2, 3):
                t_arrive(*t_two(half, m, n))

    for m in range(4):
        t_first(m)
    for m in range(4):
        t_second(m)

    def land(kind, pos):
        slot = k if kind == 0 else 2
        blk = pos_main(pos) if kind == 0 else pos_second(pos)
        for i in range(NS):
            ref = bbuf.at[slot, blk, rows(i)]
            rcopy(ref, ref, bo_ss.at[0, i], b_rs.at[kind, which_of[pos], i], sib).wait_recv()
            if pos == 1:
                to = xp if kind == 0 else xm
                rcopy(ref, ref, bf_ss.at[kind, i], b_rs.at[kind, 1, i], (row, to)).start()
            share(kind, pos, i).start()

    def from_sib(kind, pos):
        slot = 1 - k if kind == 0 else 2
        blk = pos_main(pos) if kind == 0 else pos_second(pos)
        for i in range(NS):
            ref = bbuf.at[slot, blk, rows(i)]
            rcopy(ref, ref, sh_ss.at[kind, pos, i], sh_rs.at[kind, pos, i], sib).wait_recv()

    def land_second(pos):
        @pl.when(is_owner)
        def _():
            land(1, pos)

    def from_owner(pos):
        @pl.when(jnp.logical_not(is_owner))
        def _():
            from_sib(1, pos)

    slot_b, slot_a = owner2, 1 - owner2

    def blk_at(pos):
        off = jnp.where(pos == 1, -s, jnp.where(pos == 2, s, jnp.where(pos == 3, 2, 0)))
        return ring(x + off)

    def pick_pos(pos, values):
        return jnp.where(pos == 0, values[0], jnp.where(pos == 1, values[1], jnp.where(pos == 2, values[2], values[3])))

    def first_product(slot, pos):
        val = jnp.dot(bbuf[slot, blk_at(pos)], tbuf[...].reshape(V, V), preferred_element_type=F32)
        one = pl.multiple_of(pick_pos(pos, (640, 0, 320, 768)), 64)
        two = pl.multiple_of(pick_pos(pos, (1088, 128, 448, 896)), 64)
        xbuf[slot, pl.ds(one, 128), :] = val[0:128].astype(BF16)
        xbuf[slot, pl.ds(two, 192), :] = val[128:320].astype(BF16)

    nt = (((1,), (1,)), ((), ()))

    def second_product(blk, lo, width):
        cols = pl.ds(lo, width)
        val = jnp.dot(ut[pl.ds(pl.multiple_of(blk * BLK, 64), BLK), :], li2[:, cols], preferred_element_type=F32)
        for sl in range(3):
            val += lax.dot_general(bbuf[sl, blk], xbuf[sl, cols, :], nt, preferred_element_type=F32)
        acc[blk, :, :, cols] = val.reshape(4, PIECE, width)

    def ralong(n, phase, off):
        return along(1 - PARTS[n][0], phase, off)

    def cols_of(n):
        return pl.ds(PARTS[n][1], PARTS[n][2])

    def part(n, t, i):
        if PARTS[n][0] == 0:
            return acc[t, i, :, cols_of(n)]
        return acc[i, t, :, cols_of(n)]

    def p1_at(ref, n, m):
        return ref.at[n, m, :, :, pl.ds(0, PARTS[n][2])]

    def p2_at(ref, n, m):
        return ref.at[n, m, :, pl.ds(0, PARTS[n][2])]

    def got1(n, m, t):
        return r1[n, m, t, :, pl.ds(0, PARTS[n][2])].astype(F32)

    def got2(n, m):
        return r2[n, m, :, pl.ds(0, PARTS[n][2])].astype(F32)

    hops = (2, -1, 1)

    def width(n):
        return pl.ds(0, PARTS[n][2])

    def early_copy(n, m, t):
        at = (n, m, t, slice(None), width(n))
        return rcopy(s1.at[at], r1.at[at], p1_ss.at[n, m, t], p1_rs.at[n, m, t],
                     ralong(n, 0, (sg, -sg, sg)[m])[1])

    def send_early(n, t):
        for m, off in ((0, 2), (1, -sg)):
            s1[n, m, t, :, width(n)] = part(n, t, ralong(n, 0, off)[0]).astype(BF16)
            early_copy(n, m, t).start()

    def pass_early(t):
        for n in range(2):
            early_copy(n, 0, t).wait_recv()
            s1[n, 2, t, :, width(n)] = (part(n, t, ralong(n, 0, sg)[0]) + got1(n, 0, t)).astype(BF16)
            early_copy(n, 2, t).start()

    def early_blk(step):
        return blk_at(jnp.where(step == 15, 3, lax.rem(step + y, 3)))

    def row_copy(n, m, t):
        at = (n, m, t, slice(None), width(n))
        return rcopy(s1.at[at], r1.at[at], p1_ss.at[n, m, t], p1_rs.at[n, m, t], ralong(n, 0, hops[m])[1])

    def send_rows(n, t):
        for m in range(3):
            s1[n, m, t, :, width(n)] = part(n, t, ralong(n, 0, hops[m])[0]).astype(BF16)
            row_copy(n, m, t).start()

    def blk_copy(n, m):
        return rcopy(p1_at(s1, n, m), p1_at(r1, n, m), p1_ss.at[n, m, 0], p1_rs.at[n, m, 0],
                     ralong(n, 0, hops[m])[1])

    def send_block(n, blk):
        for m in range(3):
            @pl.when(blk == ralong(n, 0, hops[m])[0])
            def _():
                for t in range(4):
                    s1[n, m, t, :, width(n)] = acc[blk, t, :, cols_of(n)].astype(BF16)
                blk_copy(n, m).start()

    def p1_each(n, what, first=0):
        for m in range(first, 3):
            if n < 2:
                @pl.loop(0, 4)
                def _(t):
                    what(early_copy(n, m, t))
            elif PARTS[n][0] == 0:
                @pl.loop(0, 4)
                def _(t):
                    what(row_copy(n, m, t))
            else:
                what(blk_copy(n, m))

    def y_order(pos):
        return ring(y + jnp.where(pos == 0, 2, jnp.where(pos == 1, -1, jnp.where(pos == 2, 1, 0))))

    def p1_end(n):
        here = ralong(n, 0, 0)[0]
        p1_each(n, lambda c: c.wait_recv(), 1 if n < 2 else 0)

        def total(t):
            if n < 2:
                return part(n, t, here) + (got1(n, 1, t) + got1(n, 2, t))
            return (part(n, t, here) + got1(n, 0, t)) + (got1(n, 1, t) + got1(n, 2, t))

        for m in range(3):
            there, there_dev = ralong(n, 1, hops[m])
            s2[n, m, :, width(n)] = total(there).astype(BF16)
            send(p2_at(s2, n, m), p2_at(r2, n, m), p2_ss.at[n, m], p2_rs.at[n, m], there_dev)
        fin[:, cols_of(n)] = total(ralong(n, 1, 0)[0])

    def p2_end(n):
        for m in range(3):
            rcopy(p2_at(s2, n, m), p2_at(r2, n, m), p2_ss.at[n, m], p2_rs.at[n, m], sib).wait_recv()
        fin[:, cols_of(n)] = (fin[:, cols_of(n)] + got2(n, 0)) + (got2(n, 1) + got2(n, 2))

    def x_send(place):
        xx = blk_at(place)
        for kk in range(2):
            for col, r, m in LAID[place]:
                gbuf[place, kk, :, r:r + m] = fin[kk * 40:(kk + 1) * 40, col:col + m]
        if place == OWN:
            send(gbuf.at[OWN, 1 - k], hbuf.at[me8], g_ss.at[OWN, 0], g_rs.at[me8], sib)
            hbuf[me8] = gbuf[OWN, k]
        else:
            for kk in range(2):
                send(gbuf.at[place, kk], hbuf.at[me8], g_ss.at[place, kk], g_rs.at[me8], dev(y, z, kk, xx))

    def cycle_terms():
        rcopy(l_own, lbuf.at[1], l_ss, l_rs, sib).wait_recv()
        pick_l = jnp.where(k == x // 2, 0, 1)
        u = jnp.dot(lbuf[pick_l, 0:16], tbuf[...].reshape(V, V), preferred_element_type=F32)
        hi = u.astype(BF16).astype(F32)
        ut[...] = jnp.concatenate([hi, u - hi], axis=0).T.astype(BF16)
        li = lbuf[pick_l, 16:32]
        for n in range(4):
            blk = blk_at(n)
            for kk in range(4):
                @pl.when(blk == kk)
                def _():
                    for col, r, m in LAID[n]:
                        li2[0:16, col:col + m] = li[:, kk * BLK + r:kk * BLK + r + m]
                        li2[16:32, col:col + m] = li[:, kk * BLK + r:kk * BLK + r + m]

    def gatherer(owner):
        return pl.when(is_owner if owner else jnp.logical_not(is_owner))

    land(0, 1)
    land_second(1)

    @gatherer(False)
    def _():
        land(0, 2)

    for m in range(4):
        t_finish(m)
    own_main.wait()

    @gatherer(True)
    def _():
        own_second.wait()

    from_sib(0, 0)
    from_owner(0)

    @pl.loop(0, 16)
    def _(step):
        @pl.when(step == 3)
        def _():
            cycle_terms()
            from_sib(0, 1)
            land_second(2)

        @pl.when(step == 5)
        def _():
            @gatherer(True)
            def _():
                from_sib(0, 2)

        @pl.when(step == 6)
        def _():
            from_owner(1)

        @pl.when(step == 7)
        def _():
            from_owner(2)

            @gatherer(True)
            def _():
                land(0, 2)

        @pl.when(step == 8)
        def _():
            @gatherer(False)
            def _():
                from_sib(0, 2)

        @pl.when(step == 11)
        def _():
            land_second(3)

            @gatherer(False)
            def _():
                land(0, 3)

        @pl.when((step >= 13) & (step < 16))
        def _():
            pass_early(early_blk(step - 4))

        @pl.when(step == 12)
        def _():
            from_owner(3)

            @gatherer(True)
            def _():
                land(0, 3)

        @pl.when(step == 13)
        def _():
            @gatherer(True)
            def _():
                from_sib(0, 3)

        @pl.when(step == 14)
        def _():
            @gatherer(False)
            def _():
                from_sib(0, 3)

        late_slot = jnp.where((step == 4) | (step == 5) | (step == 13), slot_a, 2)
        slot = jnp.where(step < 3, step, jnp.where((step == 3) | (step == 8) | (step == 14), slot_b, late_slot))
        late_pos = jnp.where((step == 5) | (step == 6) | (step == 8), 2, 3)
        pos = jnp.where(step < 3, 0, jnp.where((step == 3) | (step == 4) | (step == 7), 1, late_pos))
        summing = ((step >= 9) & (step < 12)) | (step == 15)

        @pl.when(jnp.logical_not(summing))
        def _():
            first_product(slot, pos)

        @pl.when(summing)
        def _():
            blk = early_blk(step)
            second_product(blk, 0, EARLY)
            send_early(0, blk)
            send_early(1, blk)

    @pl.loop(0, 4)
    def _(pos):
        blk = y_order(pos)
        second_product(blk, EARLY, V - EARLY)
        send_rows(3, blk)
        send_block(2, blk)

        @pl.when(pos == 2)
        def _():
            pass_early(xo)


    p1_end(0)
    p1_end(1)
    p1_end(2)
    p1_end(3)
    p2_end(0)
    x_send(XM)
    p2_end(1)
    x_send(XP)
    p2_end(2)
    p2_end(3)
    x_send(XO)
    x_send(OWN)

    for d in range(1, 8):
        src8 = lax.rem(me8 + d, 8)
        rcopy(gbuf.at[0, 0], hbuf.at[src8], g_ss.at[0, 0], g_rs.at[src8], sib).wait_recv()
    for p in range(4):
        src = (p % 2) * 4 + p // 2
        out[p] = hbuf[src] + hbuf[src + 2]

    for c in pending:
        c.wait_send()
    for n in range(4):
        p1_each(n, lambda c: c.wait_send())

    def wait_own(kind, pos_list):
        for pos in pos_list:
            for i in range(NS):
                share(kind, pos, i).wait_send()
        for i in range(NS):
            ref = bbuf.at[k if kind == 0 else 2, xm if kind == 0 else xp, rows(i)]
            rcopy(ref, ref, bf_ss.at[kind, i], b_rs.at[kind, 1, i], (row, xp if kind == 0 else xm)).wait_send()

    wait_own(0, (1, 2, 3))

    @pl.when(is_owner)
    def _():
        wait_own(1, (0, 1, 2, 3))


def exchange(*args):
    vmem = pl.BlockSpec(memory_space=pltpu.VMEM)
    anywhere = pl.BlockSpec(memory_space=pl.ANY)
    smem = pl.BlockSpec(memory_space=pltpu.SMEM)
    dma = pltpu.SemaphoreType.DMA
    return pl.pallas_call(
        kernel,
        out_shape=jax.ShapeDtypeStruct((4, 40, BLK), F32),
        in_specs=[anywhere, vmem, anywhere, smem, vmem, vmem],
        out_specs=vmem,
        scratch_shapes=[
            pltpu.VMEM((3, BLK, V), BF16),
            pltpu.VMEM((4, 16, V), BF16),
            pltpu.VMEM((3, 160, V), BF16),
            pltpu.VMEM((32, V), BF16),
            pltpu.VMEM((3, 4, BLK, V), BF16),
            pltpu.VMEM((8, 16, V), BF16),
            pltpu.VMEM((4, 4, PIECE, V), BF16),
            pltpu.VMEM((2, 32, V), BF16),
            pltpu.VMEM((V, 32), BF16),
            pltpu.VMEM((32, V), BF16),
            pltpu.VMEM((3, V, V), BF16),
            pltpu.VMEM((4, 4, PIECE, V), F32),
            pltpu.VMEM((4, 3, 4, PIECE, WIDE), BF16),
            pltpu.VMEM((4, 3, 4, PIECE, WIDE), BF16),
            pltpu.VMEM((4, 3, PIECE, WIDE), BF16),
            pltpu.VMEM((4, 3, PIECE, WIDE), BF16),
            pltpu.VMEM((PIECE, V), F32),
            pltpu.VMEM((4, 2, 40, BLK), F32),
            pltpu.VMEM((8, 40, BLK), F32),
            dma((2,)),
            dma((8,)), dma((8,)),
            dma((2, 4)), dma((2, 4)),
            dma((2, 4, 4)), dma((2, 4, 4)),
            dma, dma,
            dma((2,)),
            dma((3, NS)), dma((2, NS)), dma((2, 3, NS)),
            dma((2, 4, NS)), dma((2, 4, NS)),
            dma((4, 3, 4)), dma((4, 3, 4)), dma((4, 3)), dma((4, 3)),
            dma((4, 2)), dma((8,)),
        ],
        compiler_params=pltpu.CompilerParams(
            collective_id=0, has_side_effects=True, vmem_limit_bytes=62 * 1024 * 1024
        ),
    )(*args)


def local(
    amplitudes, integrals, occupied_integrals, pair_orbitals, amplitude_tiles, integral_tiles
):
    res = exchange(
        integrals,
        jnp.swapaxes(amplitudes, 0, 1),
        occupied_integrals,
        pair_orbitals.T,
        jnp.swapaxes(amplitude_tiles, 0, 1).reshape(80, 20),
        integral_tiles,
    )
    return jnp.swapaxes(res, 1, 2)


def solution(mesh):
    placed = (
        P(None, ("row", "col"), None),
        P("row", "col", None),
        P("row", None, None),
        P(),
        P(),
        P(),
    )
    return jax.shard_map(
        local, mesh=mesh, in_specs=placed, out_specs=P(None, "col", "row"), check_vma=False
    )
```

```python
import jax
import jax.numpy as jnp
from jax import lax
from jax.experimental import pallas as pl
from jax.experimental.pallas import tpu as pltpu
from jax.sharding import PartitionSpec as P

MESH = pl.DeviceIdType.MESH
TILE = 64
V = 1280
VT = 20
BLK = 320
PIECE = 80
HALF = 640
EARLY = 768
WIDE = 512
PARTS = ((0, 0, WIDE), (0, WIDE, 256), (1, EARLY, 256), (0, EARLY + 256, 256))
OWN, XM, XP, XO = range(4)
LAID = (
    ((640, 0, 128), (1088, 128, 192)),
    ((0, 0, 320),),
    ((320, 0, 320),),
    ((768, 0, 320),),
)
NS = 2
SUB = BLK // NS
F32 = jnp.float32
BF16 = jnp.bfloat16


def kernel(
    b_in, t_in, occ_in, pairs, a_tiles, i_tiles, out,
    b_own, t_own, occ, l_own,
    bbuf, tst, tbuf, lbuf, ut, li2, xbuf, acc,
    s1, r1, s2, r2, fin, gbuf, hbuf,
    in_ls, t1_ss, t1_rs, tg_ss, tg_rs, th_ss, th_rs, l_ss, l_rs, own_ls,
    bo_ss, bf_ss, b_rs, sh_ss, sh_rs, p1_ss, p1_rs, p2_ss, p2_rs, g_ss, g_rs,
):
    x = lax.axis_index("col")
    row = lax.axis_index("row")
    k = lax.rem(row, 2)
    yz = row // 2
    y = yz // 4
    z = lax.rem(yz, 4)
    s = 1 - 2 * lax.rem(x, 2)
    xp = lax.rem(x + s + 4, 4)
    xm = lax.rem(x - s + 4, 4)
    xo = lax.rem(x + 2, 4)
    sg = 1 - 2 * k
    me8 = k * 4 + x
    pair = 2 * lax.rem(x, 2) + k
    sib = (yz * 2 + 1 - k, x)
    owner2 = lax.rem((x + 1) // 2 + 1, 2)
    is_owner = k == owner2
    main_j = x // 2

    def dev(yy, zz, kk, xx):
        return ((yy * 4 + zz) * 2 + kk, xx)

    def ring(v):
        return lax.rem(v + 8, 4)

    def peer8(d):
        idx = lax.rem(me8 + d, 8)
        return idx, idx // 4, lax.rem(idx, 4)

    def rcopy(src, dst, ss, rs, to):
        return pltpu.make_async_remote_copy(
            src_ref=src, dst_ref=dst, send_sem=ss, recv_sem=rs, device_id=to, device_id_type=MESH
        )

    pending = []

    def send(src, dst, ss, rs, to):
        c = rcopy(src, dst, ss, rs, to)
        c.start()
        pending.append(c)
        return c

    load_b = pltpu.make_async_copy(b_in, b_own, in_ls.at[0])
    load_b.start()
    load_occ = pltpu.make_async_copy(occ_in, occ, in_ls.at[1])
    load_occ.start()

    barrier = pltpu.get_barrier_semaphore()
    for d in range(1, 8):
        _, kk, xx = peer8(d)
        pl.semaphore_signal(barrier, inc=1, device_id=dev(y, z, kk, xx), device_id_type=MESH)
    for step in (1, 2, -1):
        pl.semaphore_signal(barrier, inc=1, device_id=dev(ring(y + step), z, k, x), device_id_type=MESH)
        pl.semaphore_signal(barrier, inc=1, device_id=dev(y, ring(z + step), k, x), device_id_type=MESH)

    def iota(shape, dim):
        return lax.broadcasted_iota(jnp.int32, shape, dim)

    def ones(cond):
        return jnp.where(cond, 1.0, 0.0).astype(BF16)

    spread = ones(iota((VT, V), 0) == jnp.right_shift(iota((VT, V), 1), 6))
    tile_row = jnp.right_shift(jnp.right_shift(iota((40, 80), 0), 2) + (row * 4 + x) * 10, 6)
    same_pair = jnp.bitwise_and(iota((40, 80), 0), 3) == jnp.bitwise_and(iota((40, 80), 1), 3)
    pick_t = ones(same_pair & (jnp.right_shift(iota((40, 80), 1), 2) == tile_row))
    small = jnp.dot(pick_t, a_tiles[...].astype(F32).astype(BF16), preferred_element_type=F32).astype(BF16)
    mask = jnp.dot(small, spread, preferred_element_type=F32)
    raw = jnp.concatenate([t_in[i].astype(F32) for i in range(10)], axis=0)
    turn_i = jnp.bitwise_and(iota((64, 40), 0), 15)
    turn = ones((turn_i < 10) & (iota((64, 40), 1) == turn_i * 4 + jnp.right_shift(iota((64, 40), 0), 4)))
    turned = jnp.dot(turn, (raw * mask).astype(BF16), preferred_element_type=F32).astype(BF16)
    for p in range(4):
        t_own[p] = turned[p * 16:(p + 1) * 16]
    pick_b = ones(iota((16, VT), 0) + 5 * x == iota((16, VT), 1))
    small = jnp.dot(pick_b, i_tiles[...].astype(F32).astype(BF16), preferred_element_type=F32).astype(BF16)
    mask = jnp.dot(small, spread, preferred_element_type=F32)
    load_b.wait()
    for t in range(BLK // TILE):
        wide = jnp.broadcast_to(mask[t:t + 1], (TILE, V)).astype(BF16)
        for j in range(3):
            b_own[j, t * TILE:(t + 1) * TILE] = b_own[j, t * TILE:(t + 1) * TILE] * wide
    pl.semaphore_wait(barrier, 13)

    for d in range(1, 8):
        idx, kk, xx = peer8(d)
        send(t_own.at[2 * lax.rem(xx, 2) + kk], tst.at[me8], t1_ss.at[d], t1_rs.at[d], dev(y, z, kk, xx))
    dest2 = jnp.where(is_owner, xm, xp)
    which2 = jnp.where(is_owner, 0, 2)

    def rows(i):
        return pl.ds(i * SUB, SUB)

    for i in range(NS):
        send(b_own.at[1 - main_j, rows(i)], bbuf.at[k, x, rows(i)], bo_ss.at[1, i], b_rs.at[0, 2, i],
             (row, xm))
    for i in range(NS):
        send(b_own.at[2, rows(i)], bbuf.at[2, x, rows(i)], bo_ss.at[2, i], b_rs.at[1, which2, i],
             (row, dest2))
    for i in range(NS):
        send(b_own.at[main_j, rows(i)], bbuf.at[k, x, rows(i)], bo_ss.at[0, i], b_rs.at[0, 0, i],
             (row, xp))

    def share(kind, pos, i, src=None):
        slot, blk = (k, None) if kind == 0 else (2, None)
        blk = (x, pos_main(pos) if kind == 0 else pos_second(pos))[pos > 0]
        dst = bbuf.at[slot, blk, rows(i)]
        return rcopy(dst if src is None else src, dst, sh_ss.at[kind, pos, i], sh_rs.at[kind, pos, i], sib)

    def pos_main(pos):
        return (x, xm, xp, xo)[pos]

    def pos_second(pos):
        return (x, xp, xm, xo)[pos]

    which_of = (None, 2, 0, 1)

    for i in range(NS):
        c = share(0, 0, i, b_own.at[main_j, rows(i)])
        c.start()
        pending.append(c)

    @pl.when(is_owner)
    def _():
        for i in range(NS):
            share(1, 0, i, b_own.at[2, rows(i)]).start()

    own_main = pltpu.make_async_copy(b_own.at[main_j], bbuf.at[k, x], own_ls.at[0])
    own_main.start()
    own_second = pltpu.make_async_copy(b_own.at[2], bbuf.at[2, x], own_ls.at[1])

    @pl.when(is_owner)
    def _():
        own_second.start()

    load_occ.wait()
    other = 2 * lax.rem(x, 2) + 1 - k
    orb_row, orb_col = iota((32, 480), 0), iota((32, 480), 1)

    def occ_rows(p):
        aux = jnp.bitwise_and(orb_row, 15)
        orb = jnp.where(orb_row < 16, pairs[1, p], pairs[0, p])
        hot = ones((orb_col == aux * 160 + orb) & (aux < 3))
        return jnp.dot(hot, occ[...].reshape(480, V), preferred_element_type=F32).astype(BF16)

    l_own[...] = occ_rows(other)
    lbuf[0] = occ_rows(pair)
    send(l_own, lbuf.at[1], l_ss, l_rs, sib)

    tst[me8] = t_own[pair]
    ri, ci = iota((PIECE, 128), 0), iota((PIECE, 128), 1)
    within = jnp.bitwise_and(ci, 15)
    pick = ones((within < 10) & (ri == jnp.right_shift(ci, 4) * 10 + within))
    for d in range(1, 8):
        src8 = lax.rem(me8 + 8 - d, 8)
        rcopy(t_own.at[0], tst.at[src8], t1_ss.at[d], t1_rs.at[d], sib).wait_recv()
    piece = jnp.dot(pick, tst[...].reshape(128, V), preferred_element_type=F32)
    tbuf[y, z] = piece.astype(BF16)

    col_h = (pl.ds(0, HALF), pl.ds(HALF, HALF))

    def along(half, phase, off):
        if (half == 0) == (phase == 0):
            return ring(y + off), dev(ring(y + off), z, k, x)
        return ring(z + off), dev(y, ring(z + off), k, x)

    def t_at(half, first, second):
        if half == 0:
            return tbuf.at[ring(y + first), ring(z + second), :, col_h[0]]
        return tbuf.at[ring(y + second), ring(z + first), :, col_h[1]]

    offs = (0, -sg, sg, 2)

    def t_one(half, n):
        ref = t_at(half, offs[n], 0)
        return ref, tg_ss.at[half, n], tg_rs.at[half, n]

    def t_two(half, m, n):
        ref = t_at(half, offs[m], offs[n])
        return ref, th_ss.at[half, m, n], th_rs.at[half, m, n]

    def t_spread(half, m):
        ref = t_at(half, offs[m], 0)
        send(ref, ref, th_ss.at[half, m, 0], th_rs.at[half, m, 1], along(half, 1, sg)[1])
        send(ref, ref, th_ss.at[half, m, 1], th_rs.at[half, m, 2], along(half, 1, -sg)[1])

    def t_arrive(ref, ss, rs):
        rcopy(ref, ref, ss, rs, sib).wait_recv()

    def t_first(m):
        for half in range(2):
            if m == 0:
                ref = t_at(half, 0, 0)
                send(ref, ref, tg_ss.at[half, 0], tg_rs.at[half, 1], along(half, 0, sg)[1])
                send(ref, ref, tg_ss.at[half, 1], tg_rs.at[half, 2], along(half, 0, -sg)[1])
            else:
                ref, ss, rs = t_one(half, m)
                t_arrive(ref, ss, rs)
                if m == 1:
                    send(ref, ref, tg_ss.at[half, 2], tg_rs.at[half, 3], along(half, 0, sg)[1])
            if m > 0:
                t_spread(half, m)
        if m == 0:
            for half in range(2):
                t_spread(half, 0)

    def t_second(m):
        for half in range(2):
            ref, ss, rs = t_two(half, m, 1)
            t_arrive(ref, ss, rs)
            send(ref, ref, th_ss.at[half, m, 2], th_rs.at[half, m, 3], along(half, 1, sg)[1])

    def t_finish(m):
        for half in range(2):
            for n in (2, 3):
                t_arrive(*t_two(half, m, n))

    for m in range(4):
        t_first(m)
    for m in range(4):
        t_second(m)

    def land(kind, pos):
        slot = k if kind == 0 else 2
        blk = pos_main(pos) if kind == 0 else pos_second(pos)
        for i in range(NS):
            ref = bbuf.at[slot, blk, rows(i)]
            rcopy(ref, ref, bo_ss.at[0, i], b_rs.at[kind, which_of[pos], i], sib).wait_recv()
            if pos == 1:
                to = xp if kind == 0 else xm
                rcopy(ref, ref, bf_ss.at[kind, i], b_rs.at[kind, 1, i], (row, to)).start()
            share(kind, pos, i).start()

    def from_sib(kind, pos):
        slot = 1 - k if kind == 0 else 2
        blk = pos_main(pos) if kind == 0 else pos_second(pos)
        for i in range(NS):
            ref = bbuf.at[slot, blk, rows(i)]
            rcopy(ref, ref, sh_ss.at[kind, pos, i], sh_rs.at[kind, pos, i], sib).wait_recv()

    def land_second(pos):
        @pl.when(is_owner)
        def _():
            land(1, pos)

    def from_owner(pos):
        @pl.when(jnp.logical_not(is_owner))
        def _():
            from_sib(1, pos)

    slot_b, slot_a = owner2, 1 - owner2

    def blk_at(pos):
        off = jnp.where(pos == 1, -s, jnp.where(pos == 2, s, jnp.where(pos == 3, 2, 0)))
        return ring(x + off)

    def pick_pos(pos, values):
        return jnp.where(pos == 0, values[0], jnp.where(pos == 1, values[1], jnp.where(pos == 2, values[2], values[3])))

    def first_product(slot, pos):
        val = jnp.dot(bbuf[slot, blk_at(pos)], tbuf[...].reshape(V, V), preferred_element_type=F32)
        one = pl.multiple_of(pick_pos(pos, (640, 0, 320, 768)), 64)
        two = pl.multiple_of(pick_pos(pos, (1088, 128, 448, 896)), 64)
        xbuf[slot, pl.ds(one, 128), :] = val[0:128].astype(BF16)
        xbuf[slot, pl.ds(two, 192), :] = val[128:320].astype(BF16)

    nt = (((1,), (1,)), ((), ()))

    def second_product(blk, lo, width):
        cols = pl.ds(lo, width)
        val = jnp.dot(ut[pl.ds(pl.multiple_of(blk * BLK, 64), BLK), :], li2[:, cols], preferred_element_type=F32)
        for sl in range(3):
            val += lax.dot_general(bbuf[sl, blk], xbuf[sl, cols, :], nt, preferred_element_type=F32)
        acc[blk, :, :, cols] = val.reshape(4, PIECE, width)

    def ralong(n, phase, off):
        return along(1 - PARTS[n][0], phase, off)

    def cols_of(n):
        return pl.ds(PARTS[n][1], PARTS[n][2])

    def part(n, t, i):
        if PARTS[n][0] == 0:
            return acc[t, i, :, cols_of(n)]
        return acc[i, t, :, cols_of(n)]

    def p1_at(ref, n, m):
        return ref.at[n, m, :, :, pl.ds(0, PARTS[n][2])]

    def p2_at(ref, n, m):
        return ref.at[n, m, :, pl.ds(0, PARTS[n][2])]

    def got1(n, m, t):
        return r1[n, m, t, :, pl.ds(0, PARTS[n][2])].astype(F32)

    def got2(n, m):
        return r2[n, m, :, pl.ds(0, PARTS[n][2])].astype(F32)

    hops = (2, -1, 1)

    def width(n):
        return pl.ds(0, PARTS[n][2])

    def early_copy(n, m, t):
        at = (n, m, t, slice(None), width(n))
        return rcopy(s1.at[at], r1.at[at], p1_ss.at[n, m, t], p1_rs.at[n, m, t],
                     ralong(n, 0, (sg, -sg, sg)[m])[1])

    def send_early(n, t):
        for m, off in ((0, 2), (1, -sg)):
            s1[n, m, t, :, width(n)] = part(n, t, ralong(n, 0, off)[0]).astype(BF16)
            early_copy(n, m, t).start()

    def pass_early(t):
        for n in range(2):
            early_copy(n, 0, t).wait_recv()
            s1[n, 2, t, :, width(n)] = (part(n, t, ralong(n, 0, sg)[0]) + got1(n, 0, t)).astype(BF16)
            early_copy(n, 2, t).start()

    def early_blk(step):
        return blk_at(jnp.where(step == 15, 3, lax.rem(step + y, 3)))

    def row_copy(n, m, t):
        at = (n, m, t, slice(None), width(n))
        return rcopy(s1.at[at], r1.at[at], p1_ss.at[n, m, t], p1_rs.at[n, m, t], ralong(n, 0, hops[m])[1])

    def send_rows(n, t):
        for m in range(3):
            s1[n, m, t, :, width(n)] = part(n, t, ralong(n, 0, hops[m])[0]).astype(BF16)
            row_copy(n, m, t).start()

    def blk_copy(n, m):
        return rcopy(p1_at(s1, n, m), p1_at(r1, n, m), p1_ss.at[n, m, 0], p1_rs.at[n, m, 0],
                     ralong(n, 0, hops[m])[1])

    def send_block(n, blk):
        for m in range(3):
            @pl.when(blk == ralong(n, 0, hops[m])[0])
            def _():
                for t in range(4):
                    s1[n, m, t, :, width(n)] = acc[blk, t, :, cols_of(n)].astype(BF16)
                blk_copy(n, m).start()

    def p1_each(n, what, first=0):
        for m in range(first, 3):
            if n < 2:
                @pl.loop(0, 4)
                def _(t):
                    what(early_copy(n, m, t))
            elif PARTS[n][0] == 0:
                @pl.loop(0, 4)
                def _(t):
                    what(row_copy(n, m, t))
            else:
                what(blk_copy(n, m))

    def y_order(pos):
        return ring(y + jnp.where(pos == 0, 2, jnp.where(pos == 1, -1, jnp.where(pos == 2, 1, 0))))

    def p1_end(n):
        here = ralong(n, 0, 0)[0]
        p1_each(n, lambda c: c.wait_recv(), 1 if n < 2 else 0)

        def total(t):
            if n < 2:
                return part(n, t, here) + (got1(n, 1, t) + got1(n, 2, t))
            return (part(n, t, here) + got1(n, 0, t)) + (got1(n, 1, t) + got1(n, 2, t))

        for m in range(3):
            there, there_dev = ralong(n, 1, hops[m])
            s2[n, m, :, width(n)] = total(there).astype(BF16)
            send(p2_at(s2, n, m), p2_at(r2, n, m), p2_ss.at[n, m], p2_rs.at[n, m], there_dev)
        fin[:, cols_of(n)] = total(ralong(n, 1, 0)[0])

    def p2_end(n):
        for m in range(3):
            rcopy(p2_at(s2, n, m), p2_at(r2, n, m), p2_ss.at[n, m], p2_rs.at[n, m], sib).wait_recv()
        fin[:, cols_of(n)] = (fin[:, cols_of(n)] + got2(n, 0)) + (got2(n, 1) + got2(n, 2))

    def x_send(place):
        xx = blk_at(place)
        for kk in range(2):
            for col, r, m in LAID[place]:
                gbuf[place, kk, :, r:r + m] = fin[kk * 40:(kk + 1) * 40, col:col + m]
        if place == OWN:
            send(gbuf.at[OWN, 1 - k], hbuf.at[me8], g_ss.at[OWN, 0], g_rs.at[me8], sib)
            hbuf[me8] = gbuf[OWN, k]
        else:
            for kk in range(2):
                send(gbuf.at[place, kk], hbuf.at[me8], g_ss.at[place, kk], g_rs.at[me8], dev(y, z, kk, xx))

    def cycle_terms():
        rcopy(l_own, lbuf.at[1], l_ss, l_rs, sib).wait_recv()
        pick_l = jnp.where(k == x // 2, 0, 1)
        u = jnp.dot(lbuf[pick_l, 0:16], tbuf[...].reshape(V, V), preferred_element_type=F32)
        hi = u.astype(BF16).astype(F32)
        ut[...] = jnp.concatenate([hi, u - hi], axis=0).T.astype(BF16)
        li = lbuf[pick_l, 16:32]
        for n in range(4):
            blk = blk_at(n)
            for kk in range(4):
                @pl.when(blk == kk)
                def _():
                    for col, r, m in LAID[n]:
                        li2[0:16, col:col + m] = li[:, kk * BLK + r:kk * BLK + r + m]
                        li2[16:32, col:col + m] = li[:, kk * BLK + r:kk * BLK + r + m]

    def gatherer(owner):
        return pl.when(is_owner if owner else jnp.logical_not(is_owner))

    land(0, 1)
    land_second(1)

    @gatherer(False)
    def _():
        land(0, 2)

    for m in range(4):
        t_finish(m)
    own_main.wait()

    @gatherer(True)
    def _():
        own_second.wait()

    from_sib(0, 0)
    from_owner(0)

    @pl.loop(0, 16)
    def _(step):
        @pl.when(step == 3)
        def _():
            cycle_terms()
            from_sib(0, 1)
            land_second(2)

        @pl.when(step == 5)
        def _():
            @gatherer(True)
            def _():
                from_sib(0, 2)

        @pl.when(step == 6)
        def _():
            from_owner(1)

        @pl.when(step == 7)
        def _():
            from_owner(2)

            @gatherer(True)
            def _():
                land(0, 2)

        @pl.when(step == 8)
        def _():
            @gatherer(False)
            def _():
                from_sib(0, 2)

        @pl.when(step == 11)
        def _():
            land_second(3)

            @gatherer(False)
            def _():
                land(0, 3)

        @pl.when((step >= 13) & (step < 16))
        def _():
            pass_early(early_blk(step - 4))

        @pl.when(step == 12)
        def _():
            from_owner(3)

            @gatherer(True)
            def _():
                land(0, 3)

        @pl.when(step == 13)
        def _():
            @gatherer(True)
            def _():
                from_sib(0, 3)

        @pl.when(step == 14)
        def _():
            @gatherer(False)
            def _():
                from_sib(0, 3)

        late_slot = jnp.where((step == 4) | (step == 5) | (step == 13), slot_a, 2)
        slot = jnp.where(step < 3, step, jnp.where((step == 3) | (step == 8) | (step == 14), slot_b, late_slot))
        late_pos = jnp.where((step == 5) | (step == 6) | (step == 8), 2, 3)
        pos = jnp.where(step < 3, 0, jnp.where((step == 3) | (step == 4) | (step == 7), 1, late_pos))
        summing = ((step >= 9) & (step < 12)) | (step == 15)

        @pl.when(jnp.logical_not(summing))
        def _():
            first_product(slot, pos)

        @pl.when(summing)
        def _():
            blk = early_blk(step)
            second_product(blk, 0, EARLY)
            send_early(0, blk)
            send_early(1, blk)

    @pl.loop(0, 4)
    def _(pos):
        blk = y_order(pos)
        second_product(blk, EARLY, V - EARLY)
        send_rows(3, blk)
        send_block(2, blk)

        @pl.when(pos == 1)
        def _():
            pass_early(xo)


    p1_end(2)
    p1_end(3)
    p1_end(0)
    p1_end(1)
    p2_end(2)
    p2_end(3)
    x_send(XO)
    p2_end(0)
    x_send(XM)
    p2_end(1)
    x_send(XP)
    x_send(OWN)

    for d in range(1, 8):
        src8 = lax.rem(me8 + d, 8)
        rcopy(gbuf.at[0, 0], hbuf.at[src8], g_ss.at[0, 0], g_rs.at[src8], sib).wait_recv()
    for p in range(4):
        src = (p % 2) * 4 + p // 2
        out[p] = hbuf[src] + hbuf[src + 2]

    for c in pending:
        c.wait_send()
    for n in range(4):
        p1_each(n, lambda c: c.wait_send())

    def wait_own(kind, pos_list):
        for pos in pos_list:
            for i in range(NS):
                share(kind, pos, i).wait_send()
        for i in range(NS):
            ref = bbuf.at[k if kind == 0 else 2, xm if kind == 0 else xp, rows(i)]
            rcopy(ref, ref, bf_ss.at[kind, i], b_rs.at[kind, 1, i], (row, xp if kind == 0 else xm)).wait_send()

    wait_own(0, (1, 2, 3))

    @pl.when(is_owner)
    def _():
        wait_own(1, (0, 1, 2, 3))


def exchange(*args):
    vmem = pl.BlockSpec(memory_space=pltpu.VMEM)
    anywhere = pl.BlockSpec(memory_space=pl.ANY)
    smem = pl.BlockSpec(memory_space=pltpu.SMEM)
    dma = pltpu.SemaphoreType.DMA
    return pl.pallas_call(
        kernel,
        out_shape=jax.ShapeDtypeStruct((4, 40, BLK), F32),
        in_specs=[anywhere, vmem, anywhere, smem, vmem, vmem],
        out_specs=vmem,
        scratch_shapes=[
            pltpu.VMEM((3, BLK, V), BF16),
            pltpu.VMEM((4, 16, V), BF16),
            pltpu.VMEM((3, 160, V), BF16),
            pltpu.VMEM((32, V), BF16),
            pltpu.VMEM((3, 4, BLK, V), BF16),
            pltpu.VMEM((8, 16, V), BF16),
            pltpu.VMEM((4, 4, PIECE, V), BF16),
            pltpu.VMEM((2, 32, V), BF16),
            pltpu.VMEM((V, 32), BF16),
            pltpu.VMEM((32, V), BF16),
            pltpu.VMEM((3, V, V), BF16),
            pltpu.VMEM((4, 4, PIECE, V), F32),
            pltpu.VMEM((4, 3, 4, PIECE, WIDE), BF16),
            pltpu.VMEM((4, 3, 4, PIECE, WIDE), BF16),
            pltpu.VMEM((4, 3, PIECE, WIDE), BF16),
            pltpu.VMEM((4, 3, PIECE, WIDE), BF16),
            pltpu.VMEM((PIECE, V), F32),
            pltpu.VMEM((4, 2, 40, BLK), F32),
            pltpu.VMEM((8, 40, BLK), F32),
            dma((2,)),
            dma((8,)), dma((8,)),
            dma((2, 4)), dma((2, 4)),
            dma((2, 4, 4)), dma((2, 4, 4)),
            dma, dma,
            dma((2,)),
            dma((3, NS)), dma((2, NS)), dma((2, 3, NS)),
            dma((2, 4, NS)), dma((2, 4, NS)),
            dma((4, 3, 4)), dma((4, 3, 4)), dma((4, 3)), dma((4, 3)),
            dma((4, 2)), dma((8,)),
        ],
        compiler_params=pltpu.CompilerParams(
            collective_id=0, has_side_effects=True, vmem_limit_bytes=62 * 1024 * 1024
        ),
    )(*args)


def local(
    amplitudes, integrals, occupied_integrals, pair_orbitals, amplitude_tiles, integral_tiles
):
    res = exchange(
        integrals,
        jnp.swapaxes(amplitudes, 0, 1),
        occupied_integrals,
        pair_orbitals.T,
        jnp.swapaxes(amplitude_tiles, 0, 1).reshape(80, 20),
        integral_tiles,
    )
    return jnp.swapaxes(res, 1, 2)


def solution(mesh):
    placed = (
        P(None, ("row", "col"), None),
        P("row", "col", None),
        P("row", None, None),
        P(),
        P(),
        P(),
    )
    return jax.shard_map(
        local, mesh=mesh, in_specs=placed, out_specs=P(None, "col", "row"), check_vma=False
    )
```
